32 devices in a mesh: dp: 2 (over x), seq: 16 (over z, y, core).
Axes of the slice: x: 2, y: 2, z: 4, core: 2. Of those that a mesh axis runs over, the one named last changes fastest.
Arguments:
- layer_input: bfloat16 [2, 4, 2048, 512], P(None, 'dp', 'seq'), may hold values from -6 to 6
- qkv_weight: bfloat16 [512, 1536], P(('dp', 'seq')), may hold values from -0.25 to 0.25
- qv_bias: bfloat16 [1024], P(('dp', 'seq')), may hold values from -4 to 4
- out_weight: bfloat16 [512, 512], P(('dp', 'seq')), may hold values from -1 to 1
- out_bias: bfloat16 [512], P(('dp', 'seq')), may hold values from -4 to 4
- first_gain: bfloat16 [512], P(('dp', 'seq')), may hold values from 0.5 to 1.5
- first_shift: bfloat16 [512], P(('dp', 'seq')), may hold values from -4 to 4
- second_gain: bfloat16 [512], P(('dp', 'seq')), may hold values from 0.5 to 1.5
- second_shift: bfloat16 [512], P(('dp', 'seq')), may hold values from -4 to 4
- up_weight: bfloat16 [512, 2048], P(('dp', 'seq')), may hold values from -0.25 to 0.25
- up_bias: bfloat16 [2048], P(('dp', 'seq')), may hold values from -4 to 4
- down_weight: bfloat16 [2048, 512], P(('dp', 'seq')), may hold values from -0.125 to 0.125
- down_bias: bfloat16 [512], P(('dp', 'seq')), may hold values from -4 to 4
- cotangent: bfloat16 [2, 4, 2048, 512], P(None, 'dp', 'seq'), may hold values from -6 to 6
Outputs:
- layer_output: bfloat16 [2, 4, 2048, 512], P(None, 'dp', 'seq')
- input_grad: float32 [2, 4, 2048, 512], P(None, 'dp', 'seq')
- qkv_weight_grad: float32 [512, 1536], P(('dp', 'seq'))
- qv_bias_grad: float32 [1024], P(('dp', 'seq'))
- out_weight_grad: float32 [512, 512], P(('dp', 'seq'))
- out_bias_grad: float32 [512], P(('dp', 'seq'))
- first_gain_grad: float32 [512], P(('dp', 'seq'))
- first_shift_grad: float32 [512], P(('dp', 'seq'))
- second_gain_grad: float32 [512], P(('dp', 'seq'))
- second_shift_grad: float32 [512], P(('dp', 'seq'))
- up_weight_grad: float32 [512, 2048], P(('dp', 'seq'))
- up_bias_grad: float32 [2048], P(('dp', 'seq'))
- down_weight_grad: float32 [2048, 512], P(('dp', 'seq'))
- down_bias_grad: float32 [512], P(('dp', 'seq'))
The draws below stay inside these ranges and needn't reach their ends.
All inputs are finite; a program needn't handle non-finite values.
Results may differ from the reference program's by a relative error of at most 0.013.
Values may be sent and summed in bfloat16 or wider, within the bound.
No kernel may reach another device: no remote copies, remote signals or barrier semaphores. Data moves between devices by JAX's collectives and lax.ppermute only.
A program may use at most 192 MiB of HBM per device.

```python
import jax
import jax.numpy as jnp
from jax import lax

D = 512
HEADS = 8
FF = 2048
MB = 2
PIECE = 128
LEN = 2048
SEQS = 4


def block_levels(rng, shape, cuts, low, largest):
    def one(position, blocks):
        draws = jax.random.uniform(jax.random.fold_in(jax.random.fold_in(rng, 6), position), (blocks,), jnp.float32, low / len(cuts), largest / len(cuts))
        return jnp.repeat(jnp.exp(draws), shape[position] // blocks).reshape((-1,) + (1,) * (len(shape) - position - 1))

    factor_of = one(*cuts[0])
    for cut in cuts[1:]:
        factor_of = factor_of * one(*cut)
    return factor_of


def scatter_about(key, extent, spread, limit, cuts=(), dtype=jnp.bfloat16):
    drawn = jax.random.normal(key, extent, jnp.float32) * spread
    if len(cuts) > 0:
        drawn = block_levels(key, extent, cuts, -0.22, 0.18) * drawn
    return jnp.clip(drawn, min=-limit, max=limit).astype(dtype)


def setup_inputs(seed: int = 0) -> dict:
    splits = jax.random.split(jax.random.key(seed), 15)
    layer_input = scatter_about(splits[0], (MB, SEQS, LEN, D), 1.0, 6.0, ((1, 2), (2, 16)))
    qkv_weight = scatter_about(splits[1], (D, 3 * D), D ** -0.5, 0.25, ((0, 32),))
    qv_bias = scatter_about(splits[2], (2 * D,), 0.3, 4.0, ((0, 32),))
    out_weight = scatter_about(splits[3], (D, D), (D // 16) ** -0.5, 1.0, ((0, 32),))
    out_bias = scatter_about(splits[4], (D,), 0.3, 4.0, ((0, 32),))
    first_gain = jnp.clip(1.0 + 0.1 * jax.random.normal(splits[5], (D,), jnp.float32), 0.5, 1.5).astype(jnp.bfloat16)
    first_shift = scatter_about(splits[6], (D,), 0.3, 4.0, ((0, 32),))
    second_gain = jnp.clip(1.0 + 0.1 * jax.random.normal(splits[7], (D,), jnp.float32), 0.5, 1.5).astype(jnp.bfloat16)
    second_shift = scatter_about(splits[8], (D,), 0.3, 4.0, ((0, 32),))
    up_weight = scatter_about(splits[9], (D, FF), D ** -0.5, 0.25, ((0, 32),))
    up_bias = scatter_about(splits[10], (FF,), 0.3, 4.0, ((0, 32),))
    down_weight = scatter_about(splits[11], (FF, D), FF ** -0.5, 0.125, ((0, 32),))
    down_bias = scatter_about(splits[12], (D,), 0.3, 4.0, ((0, 32),))
    cotangent = scatter_about(splits[13], (MB, SEQS, LEN, D), 1.0, 6.0, ((1, 2), (2, 16)))
    return dict(layer_input=layer_input, qkv_weight=qkv_weight, qv_bias=qv_bias, out_weight=out_weight, out_bias=out_bias, first_gain=first_gain, first_shift=first_shift, second_gain=second_gain, second_shift=second_shift, up_weight=up_weight, up_bias=up_bias, down_weight=down_weight, down_bias=down_bias, cotangent=cotangent)


precise = lax.Precision.HIGHEST

@jax.custom_vjp
def low(v):
    return lax.optimization_barrier(v.astype(jnp.bfloat16)).astype(jnp.float32)

@jax.custom_vjp
def low_back(v):
    return v

def low_keep(v):
    return (low(v), None)

def low_pass(kept, grad):
    return (grad,)

def back_keep(v):
    return (v, None)

def back_low(kept, grad):
    return (low(grad),)
low.defvjp(low_keep, low_pass)
low_back.defvjp(back_keep, back_low)

def coarsen(values):
    return (values[0::2] + values[1::2]) * 0.5

def swapped(values):
    count = values.shape[0]
    paired = values.reshape(count // 32, 2, 16, values.shape[1], values.shape[2])
    return paired[:, ::-1].reshape(count // 16, 16, values.shape[1], values.shape[2])

def attend(queries, keys, values, factor):
    scale = queries.shape[-1] ** (-0.5)
    scores = jnp.einsum('bqhd,bkhd->bqhk', queries, keys, precision=precise) * scale
    weights = factor * jnp.exp(scores)
    return (jnp.einsum('bqhk,bkhd->bqhd', weights, values, precision=precise), lax.optimization_barrier(jnp.sum(weights, axis=-1)))

def hierarchy(queries, keys, values):
    length, heads, width = queries.shape
    local_top = (PIECE // 16).bit_length() - 1
    top = (length // 32).bit_length() - 1
    numer = jnp.zeros((length, heads, width), jnp.float32)
    denom = jnp.zeros((length, heads), jnp.float32)
    for level in range(top + 1):
        if level == local_top:
            keys = low(keys)
            values = low(values)
        count = queries.shape[0]
        blocks = count // 16
        query_blocks = queries.reshape(blocks, 16, heads, width)
        key_blocks = swapped(keys)
        value_blocks = swapped(values)
        if level == 0:
            key_blocks = jnp.concatenate([keys.reshape(blocks, 16, heads, width), key_blocks], axis=1)
            value_blocks = jnp.concatenate([values.reshape(blocks, 16, heads, width), value_blocks], axis=1)
        part_num, part_den = attend(query_blocks, key_blocks, value_blocks, 2.0 ** level)
        factor = 2 ** level
        numer = numer + jnp.repeat(part_num.reshape(count, heads, width), factor, axis=0)
        denom = denom + jnp.repeat(part_den.reshape(count, heads), factor, axis=0)
        if level < top:
            queries, keys, values = (coarsen(queries), coarsen(keys), coarsen(values))
    return numer / denom[:, :, None]

def normed(values, gain, shift):
    centred = values - lax.optimization_barrier(jnp.mean(values, axis=-1, keepdims=True))
    scale = lax.rsqrt(lax.optimization_barrier(jnp.mean(centred * centred, axis=-1, keepdims=True)) + 1e-05)
    return centred * scale * gain + shift

def layer(params, tokens):
    qkv_weight, qv_bias, out_weight, out_bias, first_gain, first_shift, second_gain, second_shift, up_weight, up_bias, down_weight, down_bias = params
    length, width = tokens.shape
    head_size = width // HEADS
    normed_one = low(normed(tokens, first_gain, first_shift))
    bias_full = jnp.concatenate([qv_bias[:width], jnp.zeros((width,), jnp.float32), qv_bias[width:]])
    mixed = low(low_back(jnp.dot(normed_one, qkv_weight, precision=precise) + bias_full))
    queries = mixed[:, :width].reshape(length, HEADS, head_size)
    keys = mixed[:, width:2 * width].reshape(length, HEADS, head_size)
    values = mixed[:, 2 * width:].reshape(length, HEADS, head_size)
    attended = hierarchy(queries, keys, values).reshape(length, width)
    branch = low_back(jnp.dot(low(attended), out_weight, precision=precise) + out_bias)
    middle = tokens + branch
    normed_two = low(normed(middle, second_gain, second_shift))
    pre = low_back(jnp.dot(normed_two, up_weight, precision=precise) + up_bias)
    hidden = low(jax.nn.gelu(pre, approximate=False))
    return middle + low_back(jnp.dot(hidden, down_weight, precision=precise) + down_bias)

def reference(layer_input, qkv_weight, qv_bias, out_weight, out_bias, first_gain, first_shift, second_gain, second_shift, up_weight, up_bias, down_weight, down_bias, cotangent):
    params = tuple((item.astype(jnp.float32) for item in (qkv_weight, qv_bias, out_weight, out_bias, first_gain, first_shift, second_gain, second_shift, up_weight, up_bias, down_weight, down_bias)))
    inputs = layer_input.astype(jnp.float32).reshape(MB * SEQS, LEN, D)
    cotans = cotangent.astype(jnp.float32).reshape(MB * SEQS, LEN, D)

    def per_sequence(totals, item):
        tokens, grad_out = item
        result, pullback = jax.vjp(layer, params, tokens)
        grad_params, grad_tokens = pullback(grad_out)
        totals = jax.tree.map(lambda left, right: left + right, totals, grad_params)
        return (totals, (result.astype(jnp.bfloat16), grad_tokens))
    start = jax.tree.map(jnp.zeros_like, params)
    totals, (outputs, grads_in) = lax.scan(per_sequence, start, (inputs, cotans))
    shape = (MB, SEQS, LEN, D)
    return (outputs.reshape(shape), grads_in.reshape(shape), totals[0], totals[1], totals[2], totals[3], totals[4], totals[5], totals[6], totals[7], totals[8], totals[9], totals[10], totals[11])
```

```python
from functools import partial

import jax
import jax.numpy as jnp
import numpy as np
from jax import lax
from jax.experimental import pallas as pl
from jax.experimental.pallas import tpu as pltpu
from jax.sharding import PartitionSpec as P

HEADS = 8
AXES = ("dp", "seq")
F32 = jnp.float32
BF16 = jnp.bfloat16
GROUPS = 32
EPS = 1e-05
VMEM_LIMIT = 60 * 1024 * 1024


def dot(left, right):
    return jnp.dot(left, right, preferred_element_type=F32)


def dot_right(left, right):
    return lax.dot_general(left, right, (((1,), (1,)), ((), ())), preferred_element_type=F32)


def dot_left(left, right):
    return lax.dot_general(left, right, (((0,), (0,)), ((), ())), preferred_element_type=F32)


def unit_of(values):
    centred = values - jnp.mean(values, axis=-1, keepdims=True)
    scale = lax.rsqrt(jnp.mean(centred * centred, axis=-1, keepdims=True) + EPS)
    return centred * scale, scale


def norm_back(grad, unit, scale, gain):
    scaled = grad * gain
    inner = (
        scaled
        - jnp.mean(scaled, axis=-1, keepdims=True)
        - unit * jnp.mean(scaled * unit, axis=-1, keepdims=True)
    )
    return inner * scale


def column_sum(values):
    return jnp.sum(values, axis=0, keepdims=True)


def expand_small(small, width, chunk):
    eye = lax.broadcasted_iota(jnp.int32, (128, width), 0) == (
        lax.broadcasted_iota(jnp.int32, (128, width), 1) % chunk
    )
    spread = dot(small, eye.astype(F32).astype(BF16))
    runs = GROUPS * chunk // width
    per_run = GROUPS // runs
    group = lax.broadcasted_iota(jnp.int32, (GROUPS * 8, width), 0) // 8
    column = lax.broadcasted_iota(jnp.int32, (GROUPS * 8, width), 1) // chunk
    kept = jnp.where(group % per_run == column, spread, 0.0).reshape(GROUPS, 8, width)
    return [jnp.sum(kept[run * per_run : (run + 1) * per_run], axis=0) for run in range(runs)]


def shrink_vectors(vectors, chunk, first_row):
    width = vectors.shape[1]
    runs = GROUPS * chunk // width
    per_run = GROUPS // runs
    tiled = jnp.broadcast_to(vectors[None], (GROUPS, 8, width)).reshape(GROUPS * 8, width)
    row = lax.broadcasted_iota(jnp.int32, (GROUPS * 8, width), 0)
    column = lax.broadcasted_iota(jnp.int32, (GROUPS * 8, width), 1) // chunk
    group = row // 8
    keep = group % per_run == column
    if runs > 1:
        keep = keep & (row % 8 - first_row == group // per_run)
    else:
        keep = keep & (row % 8 < first_row)
    eye = lax.broadcasted_iota(jnp.int32, (width, 128), 0) % chunk == lax.broadcasted_iota(
        jnp.int32, (width, 128), 1
    )
    return dot(jnp.where(keep, tiled, 0.0).astype(BF16), eye.astype(F32).astype(BF16))


def load_slots(first_ref, second_ref, groups_ref, target_ref, sems):
    half = first_ref.shape[0]
    copies = []
    for slot in range(half):
        copies.append(
            pltpu.make_async_copy(
                first_ref.at[slot], target_ref.at[groups_ref[0, slot]], sems.at[slot]
            )
        )
        copies.append(
            pltpu.make_async_copy(
                second_ref.at[slot],
                target_ref.at[groups_ref[0, half + slot]],
                sems.at[half + slot],
            )
        )
    for copy in copies:
        copy.start()
    return copies


def store_slots(source_ref, first_ref, second_ref, groups_ref, sems):
    half = first_ref.shape[0]
    copies = []
    for slot in range(half):
        copies.append(
            pltpu.make_async_copy(
                source_ref.at[groups_ref[0, half + slot]],
                second_ref.at[slot],
                sems.at[half + slot],
            )
        )
        copies.append(
            pltpu.make_async_copy(
                source_ref.at[groups_ref[0, slot]], first_ref.at[slot], sems.at[slot]
            )
        )
    for copy in copies:
        copy.start()
    for copy in copies:
        copy.wait()


def pair_average(rows):
    out = np.zeros((rows // 2, rows), np.float32)
    for i in range(rows // 2):
        out[i, 2 * i] = out[i, 2 * i + 1] = 0.5
    return out


def average(rows, factor):
    out = np.zeros((rows // factor, rows), np.float32)
    for i in range(rows // factor):
        out[i, i * factor : (i + 1) * factor] = 1.0 / factor
    return out


def attention_constants(piece, far_levels, local_top):
    top = local_top + far_levels - 1
    averaged = []
    for level in range(1, top + 1):
        averaged.append(np.repeat(average(piece, 2**level), 2**level, axis=0))
    coarse = np.concatenate([average(piece, 2**level) for level in range(1, local_top)], axis=0)
    tokens = np.arange(piece)
    masks = []
    sizes = []
    for level in range(local_top):
        keys = np.arange(piece >> level)
        block = (tokens >> level)[:, None] // 16
        if level == 0:
            mask = (block // 2) == (keys[None, :] // 32)
        else:
            mask = (block ^ 1) == (keys[None, :] // 16)
        masks += [mask, mask]
        sizes.append(piece >> level)
    for _ in range(far_levels):
        masks += [np.ones((piece, 16), bool)] * 2
        sizes.append(16)
    ones = []
    for level, size in enumerate(sizes):
        head_a = np.zeros((size, 128), np.float32)
        head_a[:, :64] = 2.0**level
        head_b = np.zeros((size, 128), np.float32)
        head_b[:, 64:] = 2.0**level
        ones += [head_a, head_b]
    return dict(
        averaged=np.concatenate(averaged, axis=0),
        averaged_wide=np.concatenate(averaged, axis=1),
        coarse=coarse,
        coarse_t=coarse.T.copy(),
        mask=np.concatenate(masks, axis=1).astype(np.float32),
        ones=np.concatenate(ones, axis=0),
        sizes=tuple(sizes),
    )


def far_constants(seqs):
    out = np.zeros((seqs * 16, seqs * (8 + 16 + 8 + 8)), np.float32)
    starts = (0, seqs * 8, seqs * 24, seqs * 32)
    for seq in range(seqs):
        for slot in range(4):
            for i in range(4):
                row = seq * 16 + slot * 4 + i
                if slot == 1:
                    at = starts[1] + seq * 16 + 4 * i
                    out[row, at : at + 4] = 0.25
                else:
                    at = starts[slot] + seq * 8 + 2 * i
                    out[row, at : at + 2] = 0.5
    return out


def mix_kernel(
    x_ref, first_ref, second_ref, groups_ref, coarse_ref, pair_ref,
    q_ref, k_ref, v_ref, base_ref, next_ref, vec_ref,
    weight_ref, sems,
):
    width = x_ref.shape[1]
    copies = load_slots(first_ref, second_ref, groups_ref, weight_ref, sems)
    unit, _ = unit_of(x_ref[...].astype(F32))
    for copy in copies:
        copy.wait()
    small = weight_ref[:, 48:56, 0:128].astype(F32).reshape(GROUPS * 8, 128).astype(BF16)
    plain = expand_small(small, width, width // GROUPS)[0]
    biases = expand_small(small, width, 2 * width // GROUPS)
    vec_ref[...] = plain
    normed = (unit * plain[0:1] + plain[1:2]).astype(BF16)
    for part, ref in enumerate((k_ref, v_ref, q_ref)):
        at = (16, 32, 0)[part]
        weight = weight_ref[:, at : at + 16, :].reshape(width, width)
        mixed = dot(normed, weight)
        if part == 1:
            mixed = mixed + biases[1][2:3]
        if part == 2:
            mixed = mixed + biases[0][2:3]
        mixed = mixed.astype(BF16)
        ref[...] = mixed
        if part < 2:
            base = dot(coarse_ref[...], mixed).astype(BF16)
            base_ref[:, part * width : (part + 1) * width] = base
            next_ref[:, part * width : (part + 1) * width] = dot(pair_ref[...], base).astype(BF16)


def far_kernel(own_ref, one_ref, two_ref, three_ref, gather_ref, pair_ref, five_ref, six_ref):
    rows = jnp.concatenate(
        [ref[...].astype(F32) for ref in (own_ref, one_ref, two_ref, three_ref)], axis=0
    ).astype(BF16)
    five = dot(gather_ref[...], rows).astype(BF16)
    five_ref[...] = five
    six_ref[...] = dot(pair_ref[...], five).astype(BF16)


def far_back_kernel(
    five_ref, six_a_ref, six_b_ref, one_ref, two_ref, three_ref, spread_ref, pair_ref,
    own_out, one_out, two_out, three_out,
):
    six = (six_a_ref[...].astype(F32) + six_b_ref[...].astype(F32)).astype(BF16)
    five = (five_ref[...].astype(F32) + dot(pair_ref[...], six)).astype(BF16)
    rows = dot(spread_ref[...], five)
    own = own_out.shape[0]
    one = own + one_ref.shape[0]
    two = one + two_ref.shape[0]
    own_out[...] = rows[:own]
    one_out[...] = (rows[own:one] + one_ref[...].astype(F32)).astype(BF16)
    two_out[...] = (rows[one:two] + two_ref[...].astype(F32)).astype(BF16)
    three_out[...] = (rows[two:] + three_ref[...].astype(F32)).astype(BF16)


def layer_kernel(*refs, far_rows, sizes, local_top, piece):
    fars = len(far_rows)
    (x_ref, cot_ref, q_ref, k_ref, v_ref) = refs[:5]
    far_refs = refs[5 : 5 + fars]
    (
        first_ref, second_ref, groups_ref, averaged_ref, wide_ref, coarse_ref, coarse_t_ref,
        mask_ref, ones_ref,
    ) = refs[5 + fars : 14 + fars]
    outs = refs[14 + fars :]
    (
        out_ref, hidden_ref, gpre_ref, normed_ref, att_ref, branch_ref, dmid_ref, vec_ref,
        dq_ref, dk_ref, dv_ref,
    ) = outs[:11]
    dfar_refs = outs[11 : 11 + fars]
    (
        weight_ref, qe_ref, kall_ref, vall_ref, p_ref, o_ref, rden_ref, datt_ref, dkall_ref,
        dvall_ref, t_ref, dqacc_ref, sems,
    ) = outs[11 + fars :]
    tokens, width = x_ref.shape
    seqs = tokens // piece
    pairs = width // 128
    levels = len(sizes)
    top = levels - 1
    starts = np.concatenate([[0], np.cumsum(sizes)]).tolist()
    local = starts[local_top]
    scale = 0.125

    copies = load_slots(first_ref, second_ref, groups_ref, weight_ref, sems)

    def lane_a(rows):
        return lax.broadcasted_iota(jnp.int32, (rows, 128), 1) < 64

    def stacked(block):
        in_a = lane_a(block.shape[0])
        zero = jnp.zeros_like(block)
        head_a = jnp.where(in_a, block, zero)
        head_b = jnp.where(in_a, zero, block)
        parts = []
        for level in range(levels):
            parts.append(head_a[starts[level] : starts[level + 1]])
            parts.append(head_b[starts[level] : starts[level + 1]])
        return parts

    def blocked(parts):
        rows = []
        for level in range(2, levels):
            block = jnp.concatenate(parts[2 * level : 2 * level + 2], axis=0)
            zero = jnp.zeros_like(block)
            rows.append(
                jnp.concatenate(
                    [block if other == level else zero for other in range(2, levels)], axis=1
                )
            )
        return jnp.concatenate(rows, axis=0)

    def queries_of(seq, pair):
        lanes = slice(pair * 128, pair * 128 + 128)
        plain = q_ref[pl.ds(pl.multiple_of(seq * piece, piece), piece), lanes]
        plain = (plain.astype(F32) * scale).astype(BF16)
        one = qe_ref[seq, 0:piece, lanes]
        rest = jnp.concatenate(
            [
                qe_ref[seq, (level - 1) * piece : level * piece, lanes]
                for level in range(2, levels)
            ],
            axis=1,
        )
        return plain, one, rest

    def attention_forward(seq, carry):
        rows = pl.ds(pl.multiple_of(seq * piece, piece), piece)
        queries = (q_ref[rows, :].astype(F32) * scale).astype(BF16)
        qe_ref[seq] = dot(averaged_ref[...], queries).astype(BF16)
        keys = k_ref[rows, :]
        values = v_ref[rows, :]
        coarse_keys = dot(coarse_ref[...], keys).astype(BF16)
        coarse_values = dot(coarse_ref[...], values)
        scaled = [values]
        at = 0
        for level in range(1, local_top):
            part = coarse_values[at : at + sizes[level]] * 2.0**level
            scaled.append(part.astype(BF16))
            at += sizes[level]
        far = jnp.concatenate(
            [
                ref[pl.ds(pl.multiple_of(seq * n, n), n), :].astype(F32)
                for ref, n in zip(far_refs, far_rows)
            ],
            axis=0,
        )
        far_values = [
            far[16 * extra : 16 * extra + 16, width:] * 2.0 ** (local_top + extra)
            for extra in range(levels - local_top)
        ]
        kall_ref[seq] = jnp.concatenate([keys, coarse_keys, far[:, :width].astype(BF16)], axis=0)
        vall_ref[seq] = jnp.concatenate(
            scaled + [jnp.concatenate(far_values, axis=0).astype(BF16)], axis=0
        )
        for pair in range(pairs):
            lanes = slice(pair * 128, pair * 128 + 128)
            plain, one, rest = queries_of(seq, pair)
            key_parts = stacked(kall_ref[seq, :, lanes])
            scores = jnp.concatenate(
                [
                    dot_right(plain, jnp.concatenate(key_parts[0:2], axis=0)),
                    dot_right(one, jnp.concatenate(key_parts[2:4], axis=0)),
                    dot_right(rest, blocked(key_parts)),
                ],
                axis=1,
            )
            weights = jnp.where(mask_ref[...] > 0.0, jnp.exp(scores), 0.0).astype(BF16)
            p_ref[seq, pair] = weights
            both = jnp.concatenate(
                [jnp.concatenate(stacked(vall_ref[seq, :, lanes]), axis=0), ones_ref[...]], axis=1
            )
            sums = dot(weights, both)
            rden = 1.0 / sums[:, 128:]
            attended = sums[:, :128] * rden
            o_ref[rows, lanes] = attended
            rden_ref[rows, lanes] = rden
            att_ref[rows, lanes] = attended.astype(BF16)
        return carry

    lax.fori_loop(0, seqs, attention_forward, 0)

    for copy in copies:
        copy.wait()
    small = weight_ref[:, 144:152, 0:128].astype(F32).reshape(GROUPS * 8, 128).astype(BF16)
    plain_vectors = expand_small(small, width, width // GROUPS)[0]
    up_biases = expand_small(small, width, 4 * width // GROUPS)
    out_bias = plain_vectors[0:1]
    gain = plain_vectors[1:2]
    shift = plain_vectors[2:3]
    down_bias = plain_vectors[3:4]
    out_weight = weight_ref[:, 0:16, :].reshape(width, width)
    vec_ref[...] = jnp.zeros_like(vec_ref)
    tile = 256

    def feed(i, carry):
        rows = pl.ds(pl.multiple_of(i * tile, tile), tile)
        middle = x_ref[rows, :].astype(F32) + dot(att_ref[rows, :], out_weight) + out_bias
        unit, inverse = unit_of(middle)
        normed = (unit * gain + shift).astype(BF16)
        normed_ref[rows, :] = normed
        g_out = cot_ref[rows, :]
        result = middle + down_bias
        d_two = jnp.zeros((tile, width), F32)
        for block in range(4):
            lanes = slice(block * width, block * width + width)
            up = weight_ref[:, 16 + 16 * block : 32 + 16 * block, :].reshape(width, width)
            down = weight_ref[8 * block : 8 * block + 8, 80:144, :].reshape(width, width)
            pre = dot(normed, up) + up_biases[block][4:5]
            cdf = 0.5 + 0.5 * lax.erf(pre * 0.7071067811865476)
            hidden = (pre * cdf).astype(BF16)
            hidden_ref[rows, lanes] = hidden
            result = result + dot(hidden, down)
            slope = cdf + pre * (0.3989422804014327 * jnp.exp(-0.5 * pre * pre))
            g_pre = (dot_right(g_out, down) * slope).astype(BF16)
            gpre_ref[rows, lanes] = g_pre
            vec_ref[4 + block : 5 + block, :] += column_sum(g_pre.astype(F32))
            d_two = d_two + dot_right(g_pre, up)
        out_ref[rows, :] = result.astype(BF16)
        cot = g_out.astype(F32)
        d_middle = cot + norm_back(d_two, unit, inverse, gain)
        dmid_ref[rows, :] = d_middle
        branch = d_middle.astype(BF16)
        branch_ref[rows, :] = branch
        datt_ref[rows, :] = dot_right(branch, out_weight)
        vec_ref[0:1, :] += column_sum(d_two * unit)
        vec_ref[1:2, :] += column_sum(d_two)
        vec_ref[2:3, :] += column_sum(branch.astype(F32))
        vec_ref[3:4, :] += column_sum(cot)
        return carry

    lax.fori_loop(0, tokens // tile, feed, 0)

    def attention_backward(seq, carry):
        rows = pl.ds(pl.multiple_of(seq * piece, piece), piece)
        for pair in range(pairs):
            lanes = slice(pair * 128, pair * 128 + 128)
            plain, one, rest = queries_of(seq, pair)
            key_parts = stacked(kall_ref[seq, :, lanes])
            blocks = blocked(key_parts)
            both = jnp.concatenate(
                [jnp.concatenate(stacked(vall_ref[seq, :, lanes]), axis=0), ones_ref[...]], axis=1
            )
            d_num = datt_ref[rows, lanes] * rden_ref[rows, lanes]
            d_den = -d_num * o_ref[rows, lanes]
            d_num = d_num.astype(BF16)
            weights = p_ref[seq, pair]
            d_weights = dot_right(jnp.concatenate([d_num, d_den.astype(BF16)], axis=1), both)
            d_scores = (weights.astype(F32) * d_weights).astype(BF16)
            near = 2 * sizes[0]
            mid = near + 2 * sizes[1]
            d_key_near = dot_left(d_scores[:, :near], plain)
            d_key_mid = dot_left(d_scores[:, near:mid], one)
            d_key_rest = dot_left(d_scores[:, mid:], rest)
            d_value = dot_left(weights, d_num)
            dqacc_ref[:, lanes] = dot(d_scores[:, :near], jnp.concatenate(key_parts[0:2], axis=0))
            t_ref[0:piece, lanes] = dot(
                d_scores[:, near:mid], jnp.concatenate(key_parts[2:4], axis=0)
            ).astype(BF16)
            d_rest = dot(d_scores[:, mid:], blocks).astype(BF16)
            at = 0
            for level in range(levels):
                size = sizes[level]
                low, high = starts[level], starts[level + 1]
                in_a = lane_a(size)
                if level == 0:
                    source = d_key_near
                elif level == 1:
                    source = d_key_mid
                else:
                    first = at - mid
                    source = d_key_rest[
                        first : first + 2 * size, (level - 2) * 128 : (level - 1) * 128
                    ]
                    t_ref[(level - 1) * piece : level * piece, lanes] = d_rest[
                        :, (level - 2) * 128 : (level - 1) * 128
                    ]
                dkall_ref[low:high, lanes] = jnp.where(in_a, source[:size], source[size:])
                values = d_value[at : at + 2 * size]
                dvall_ref[low:high, lanes] = (
                    jnp.where(in_a, values[:size], values[size:]) * 2.0**level
                )
                at += 2 * size
        dq_ref[rows, :] = ((dqacc_ref[...] + dot(wide_ref[...], t_ref[...])) * scale).astype(BF16)
        dk_ref[rows, :] = dkall_ref[0:piece, :] + dot(
            coarse_t_ref[...], dkall_ref[piece:local, :].astype(BF16)
        )
        dv_ref[rows, :] = dvall_ref[0:piece, :] + dot(
            coarse_t_ref[...], dvall_ref[piece:local, :].astype(BF16)
        )
        at = local
        for ref, n in zip(dfar_refs, far_rows):
            target = pl.ds(pl.multiple_of(seq * n, n), n)
            ref[target, 0:width] = dkall_ref[at : at + n, :].astype(BF16)
            ref[target, width : 2 * width] = dvall_ref[at : at + n, :].astype(BF16)
            at += n
        return carry

    lax.fori_loop(0, seqs, attention_backward, 0)


def feed_grad_kernel(
    hidden_ref, gpre_ref, normed_ref, att_ref, branch_ref, cot_ref, vec_ref, groups_ref,
    first_ref, second_ref,
    grad_ref, sems,
):
    width = cot_ref.shape[1]
    vectors = vec_ref[...]
    small = shrink_vectors(vectors, width // GROUPS, 4) + shrink_vectors(
        vectors, 4 * width // GROUPS, 4
    )
    grad_ref[:, 144:152, :] = jnp.zeros((GROUPS, 8, width), BF16)
    grad_ref[:, 144:152, 0:128] = small.reshape(GROUPS, 8, 128).astype(BF16)
    grad = dot_left(att_ref[...], branch_ref[...])
    grad_ref[:, 0:16, :] = grad.astype(BF16).reshape(GROUPS, 16, width)
    for block in range(4):
        lanes = slice(block * width, block * width + width)
        grad = dot_left(hidden_ref[:, lanes], cot_ref[...])
        grad_ref[8 * block : 8 * block + 8, 80:144, :] = grad.astype(BF16).reshape(8, 64, width)
        grad = dot_left(normed_ref[...], gpre_ref[:, lanes])
        grad_ref[:, 16 + 16 * block : 32 + 16 * block, :] = grad.astype(BF16).reshape(
            GROUPS, 16, width
        )
    store_slots(grad_ref, first_ref, second_ref, groups_ref, sems)


def input_kernel(
    x_ref, dmid_ref, dq_ref, dk_ref, dv_ref, own_ref, one_ref, two_ref, three_ref, vec_ref,
    pair_ref, spread_ref, first_in, second_in, groups_ref,
    din_ref, first_ref, second_ref,
    weight_ref, grad_ref, in_sems, out_sems,
):
    width = x_ref.shape[1]
    copies = load_slots(first_in, second_in, groups_ref, weight_ref, in_sems)
    gain = vec_ref[0:1, :]
    shift = vec_ref[1:2, :]
    unit, inverse = unit_of(x_ref[...].astype(F32))
    normed = (unit * gain + shift).astype(BF16)
    lower = own_ref[...] + two_ref[...].astype(F32) + three_ref[...].astype(F32)
    base = one_ref[...].astype(F32) + dot(pair_ref[...], lower.astype(BF16))
    far = dot(spread_ref[...], base.astype(BF16))
    grads = (
        dq_ref[...],
        (dk_ref[...] + far[:, :width]).astype(BF16),
        (dv_ref[...] + far[:, width:]).astype(BF16),
    )
    for copy in copies:
        copy.wait()
    d_one = jnp.zeros(x_ref.shape, F32)
    for part in range(3):
        weight = weight_ref[:, 16 * part : 16 * part + 16, :].reshape(width, width)
        d_one = d_one + dot_right(grads[part], weight)
        grad = dot_left(normed, grads[part])
        grad_ref[:, 16 * part : 16 * part + 16, :] = grad.astype(BF16).reshape(GROUPS, 16, width)
    din_ref[...] = dmid_ref[...] + norm_back(d_one, unit, inverse, gain)
    vectors = jnp.concatenate(
        [
            column_sum(d_one * unit),
            column_sum(d_one),
            column_sum(grads[0].astype(F32)),
            column_sum(grads[2].astype(F32)),
            jnp.zeros((4, width), F32),
        ],
        axis=0,
    )
    small = shrink_vectors(vectors, width // GROUPS, 2) + shrink_vectors(
        vectors, 2 * width // GROUPS, 2
    )
    grad_ref[:, 48:56, :] = jnp.zeros((GROUPS, 8, width), BF16)
    grad_ref[:, 48:56, 0:128] = small.reshape(GROUPS, 8, 128).astype(BF16)
    store_slots(grad_ref, first_ref, second_ref, groups_ref, out_sems)


def vmem():
    return pl.BlockSpec(memory_space=pltpu.VMEM)


def anywhere():
    return pl.BlockSpec(memory_space=pl.ANY)


def scalars():
    return pl.BlockSpec(memory_space=pltpu.SMEM)


def shape(dims, dtype):
    return jax.ShapeDtypeStruct(dims, dtype)


def params():
    return pltpu.CompilerParams(vmem_limit_bytes=VMEM_LIMIT)


def cost(flops, traffic, exps=0):
    return pl.CostEstimate(flops=flops, bytes_accessed=traffic, transcendentals=exps)


def const(values):
    return jnp.asarray(values, BF16)


def bit_orders():
    return ((8, 4, 16, 2), (8, 4, 2, 16))


def slot_offset(slot, order):
    return sum(bit for k, bit in enumerate(order) if slot >> k & 1)


def group_table():
    orders = bit_orders()
    table = np.zeros((32, 32), np.int32)
    for device in range(32):
        core = device & 1
        for slot in range(16):
            table[device, slot] = device ^ slot_offset(slot, orders[core])
            table[device, 16 + slot] = device ^ 1 ^ slot_offset(slot, orders[1 - core])
    return table


def exchange(value, bits):
    if isinstance(bits, int):
        bits = (bits, bits)
    count = lax.axis_size(AXES)
    return lax.ppermute(value, AXES, [(i, i ^ bits[i & 1]) for i in range(count)])


def gather_slots(pack):
    buffer = pack[None]
    orders = bit_orders()
    for k in range(4):
        other = exchange(buffer, (orders[0][k], orders[1][k]))
        buffer = jnp.concatenate([buffer, other], axis=0)
    return buffer, exchange(buffer, 1)


def scatter_slots(kept, sent):
    orders = bit_orders()
    other = exchange(sent, 1)
    for k in (3, 2, 1, 0):
        half = 2**k
        high = (kept[half:].astype(F32) + other[half:].astype(F32)).astype(BF16)
        received = exchange(high, (orders[0][k], orders[1][k]))
        kept = (kept[:half].astype(F32) + other[:half].astype(F32)).astype(BF16)
        other = received
    return kept[0].astype(F32) + other[0].astype(F32)


def padded(vector, lanes):
    return jnp.pad(vector, (0, lanes - vector.shape[0]))


def coarsen(values):
    return (values[:, 0::2] + values[:, 1::2]) * 0.5


def whole_far(base, seqs, far_levels, position):
    rows = base.reshape(seqs, 16, base.shape[1])
    full = lax.all_gather(rows, "seq", axis=1, tiled=True).astype(F32)
    parts = []
    for extra in range(far_levels):
        partner = (position // 2**extra) ^ 1
        parts.append(lax.dynamic_slice_in_dim(full, partner * 16, 16, axis=1))
        if extra + 1 < far_levels:
            full = coarsen(full)
    return jnp.concatenate(parts, axis=1).astype(BF16).reshape(seqs * 16 * far_levels, -1)


def whole_far_back(grad, seqs, far_levels, position):
    stack = grad.reshape(seqs, far_levels, 16, -1).astype(F32)
    ids = jnp.arange(far_levels).reshape(1, far_levels, 1, 1)
    count = lax.axis_size("seq")
    for bit in range(far_levels):
        pairs = [(i, i ^ 1 << bit) for i in range(count)]
        other = lax.ppermute(stack.astype(BF16), "seq", pairs).astype(F32)
        stack = jnp.where(ids > bit, stack + other, jnp.where(ids == bit, other, stack))
    own = jnp.zeros((seqs, 16, stack.shape[-1]), F32)
    for extra in range(far_levels):
        rows = 16 >> extra
        offset = position % 2**extra * rows
        part = lax.dynamic_slice_in_dim(stack[:, extra], offset, rows, axis=1)
        own = own + jnp.repeat(part, 2**extra, axis=1) * 0.5**extra
    return own.reshape(seqs * 16, -1).astype(BF16)


def body(
    layer_input, qkv_weight, qv_bias, out_weight, out_bias, first_gain, first_shift, second_gain,
    second_shift, up_weight, up_bias, down_weight, down_bias, cotangent,
):
    batches, per_batch, piece, width = layer_input.shape
    seqs = batches * per_batch
    tokens = seqs * piece
    hidden = up_weight.shape[1]
    blocks = hidden // width
    devices = lax.axis_size(AXES)
    pieces = lax.axis_size("seq")
    position = lax.axis_index("seq")
    far_levels = pieces.bit_length() - 1
    local_top = (piece // 16).bit_length() - 1
    fast = devices == GROUPS and pieces == 16
    x = layer_input.reshape(tokens, width)
    cot = cotangent.reshape(tokens, width)
    consts = attention_constants(piece, far_levels, local_top)
    sizes = consts["sizes"]
    keys = sum(sizes)

    if fast:
        me = lax.axis_index(AXES)
        groups = lax.dynamic_slice_in_dim(jnp.asarray(group_table()), me, 1, axis=0)
        zero = jnp.zeros((width,), BF16)
        small_a = jnp.stack(
            [padded(v, width) for v in (first_gain, first_shift, qv_bias)] + [zero] * 5
        )
        small_b = jnp.stack(
            [padded(v, width) for v in (out_bias, second_gain, second_shift, down_bias, up_bias)]
            + [zero] * 3
        )
        pack_a = jnp.concatenate(
            [qkv_weight[:, i * width : (i + 1) * width] for i in range(3)] + [small_a]
        )
        pack_b = jnp.concatenate(
            [out_weight]
            + [up_weight[:, i * width : (i + 1) * width] for i in range(blocks)]
            + [down_weight, small_b]
        )
        first_a, second_a = gather_slots(pack_a)
        first_b, second_b = gather_slots(pack_b)
    else:
        groups = jnp.arange(GROUPS, dtype=jnp.int32)[None]

        def whole(value):
            return lax.all_gather(value, AXES, axis=0, tiled=True)

        def chunks(value):
            rows = whole(value).reshape(GROUPS, -1)
            return jnp.pad(rows, ((0, 0), (0, width - rows.shape[1])))[:, None]

        def columns(value, count):
            value = value.reshape(GROUPS, -1, count, width).transpose(0, 2, 1, 3)
            return value.reshape(GROUPS, -1, width)

        gathered_a = jnp.concatenate(
            [columns(whole(qkv_weight), 3)]
            + [chunks(v) for v in (first_gain, first_shift, qv_bias)]
            + [jnp.zeros((GROUPS, 5, width), BF16)],
            axis=1,
        )
        gathered_b = jnp.concatenate(
            [
                columns(whole(out_weight), 1),
                columns(whole(up_weight), blocks),
                columns(whole(down_weight), 1),
            ]
            + [chunks(v) for v in (out_bias, second_gain, second_shift, down_bias, up_bias)]
            + [jnp.zeros((GROUPS, 3, width), BF16)],
            axis=1,
        )
        first_a, second_a = gathered_a[:16], gathered_a[16:]
        first_b, second_b = gathered_b[:16], gathered_b[16:]

    rows_a = first_a.shape[1]
    rows_b = first_b.shape[1]
    flat = (tokens, width)
    base_rows = seqs * 16
    coarse_all = np.kron(np.eye(seqs, dtype=np.float32), average(piece, piece // 16))
    pair = np.kron(np.eye(seqs, dtype=np.float32), pair_average(16))

    queries, key, value, base, below, vec_one = pl.pallas_call(
        mix_kernel,
        out_shape=(
            shape(flat, BF16),
            shape(flat, BF16),
            shape(flat, BF16),
            shape((base_rows, 2 * width), BF16),
            shape((base_rows // 2, 2 * width), BF16),
            shape((8, width), F32),
        ),
        in_specs=[vmem(), anywhere(), anywhere(), scalars(), vmem(), vmem()],
        out_specs=(vmem(),) * 6,
        scratch_shapes=[
            pltpu.VMEM((GROUPS, rows_a, width), BF16),
            pltpu.SemaphoreType.DMA((GROUPS,)),
        ],
        compiler_params=params(),
        cost_estimate=cost(2 * tokens * width * width * 3, 6 << 20),
        name="mix",
    )(x, first_a, second_a, groups, const(coarse_all), const(pair))

    if fast:
        gather_far = far_constants(seqs)
        one = exchange(base, 1)
        two = exchange(below, 2)
        three = exchange(below, 3)
        five, six = pl.pallas_call(
            far_kernel,
            out_shape=(
                shape((base_rows, 2 * width), BF16),
                shape((base_rows // 2, 2 * width), BF16),
            ),
            in_specs=[vmem()] * 6,
            out_specs=(vmem(),) * 2,
            compiler_params=params(),
            cost_estimate=cost(1 << 24, 1 << 19),
            name="far",
        )(below, one, two, three, const(gather_far), const(pair))
        far = (
            one,
            two,
            three,
            exchange(five, 4),
            exchange(six, 8),
            exchange(six, 12),
        )
        far_rows = (16, 8, 8, 16, 8, 8)
    else:
        far = (whole_far(base, seqs, far_levels, position),)
        far_rows = (16 * far_levels,)

    top = len(sizes) - 1
    outs = pl.pallas_call(
        partial(layer_kernel, far_rows=far_rows, sizes=sizes, local_top=local_top, piece=piece),
        out_shape=(
            shape(flat, BF16),
            shape((tokens, hidden), BF16),
            shape((tokens, hidden), BF16),
            shape(flat, BF16),
            shape(flat, BF16),
            shape(flat, BF16),
            shape(flat, F32),
            shape((8, width), F32),
            shape(flat, BF16),
            shape(flat, F32),
            shape(flat, F32),
        )
        + tuple(shape(item.shape, BF16) for item in far),
        in_specs=[vmem()] * (5 + len(far)) + [anywhere(), anywhere(), scalars()] + [vmem()] * 6,
        out_specs=(vmem(),) * (11 + len(far)),
        scratch_shapes=[
            pltpu.VMEM((GROUPS, rows_b, width), BF16),
            pltpu.VMEM((seqs, top * piece, width), BF16),
            pltpu.VMEM((seqs, keys, width), BF16),
            pltpu.VMEM((seqs, keys, width), BF16),
            pltpu.VMEM((seqs, width // 128, piece, 2 * keys), BF16),
            pltpu.VMEM(flat, F32),
            pltpu.VMEM(flat, F32),
            pltpu.VMEM(flat, F32),
            pltpu.VMEM((keys, width), F32),
            pltpu.VMEM((keys, width), F32),
            pltpu.VMEM((top * piece, width), BF16),
            pltpu.VMEM((piece, width), F32),
            pltpu.SemaphoreType.DMA((GROUPS,)),
        ],
        compiler_params=params(),
        cost_estimate=cost(2 * tokens * width * (2 * width + 4 * hidden), 20 << 20),
        name="layer",
    )(
        x, cot, queries, key, value, *far, first_b, second_b, groups,
        const(consts["averaged"]), const(consts["averaged_wide"]), const(consts["coarse"]),
        const(consts["coarse_t"]), jnp.asarray(consts["mask"]), const(consts["ones"]),
    )
    (
        result, hidden_act, g_pre, normed_two, attended, branch, d_middle, vec_two, d_query, d_key,
        d_value,
    ) = outs[:11]
    d_far = outs[11:]

    half_b = (GROUPS // 2, rows_b, width)
    kept_b, sent_b = pl.pallas_call(
        feed_grad_kernel,
        out_shape=(shape(half_b, BF16),) * 2,
        in_specs=[vmem()] * 7 + [scalars()],
        out_specs=(anywhere(),) * 2,
        scratch_shapes=[
            pltpu.VMEM((GROUPS, rows_b, width), BF16),
            pltpu.SemaphoreType.DMA((GROUPS,)),
        ],
        compiler_params=params(),
        cost_estimate=cost(2 * tokens * width * (width + 2 * hidden), 12 << 20),
        name="feed_grad",
    )(hidden_act, g_pre, normed_two, attended, branch, cot, vec_two, groups)

    if fast:
        back_five = exchange(d_far[3], 4)
        back_six_a = exchange(d_far[4], 8)
        back_six_b = exchange(d_far[5], 12)
        own, out_one, out_two, out_three = pl.pallas_call(
            far_back_kernel,
            out_shape=(
                shape((base_rows // 2, 2 * width), F32),
                shape((base_rows, 2 * width), BF16),
                shape((base_rows // 2, 2 * width), BF16),
                shape((base_rows // 2, 2 * width), BF16),
            ),
            in_specs=[vmem()] * 8,
            out_specs=(vmem(),) * 4,
            compiler_params=params(),
            cost_estimate=cost(1 << 24, 1 << 19),
            name="far_back",
        )(
            back_five, back_six_a, back_six_b, d_far[0], d_far[1], d_far[2],
            const(gather_far.T), const(pair.T),
        )
        back_one = exchange(out_one, 1)
        back_two = exchange(out_two, 2)
        back_three = exchange(out_three, 3)
    else:
        back_one = whole_far_back(d_far[0], seqs, far_levels, position)
        own = jnp.zeros((base_rows // 2, 2 * width), F32)
        back_two = back_three = jnp.zeros((base_rows // 2, 2 * width), BF16)

    half_a = (GROUPS // 2, rows_a, width)
    d_input, kept_a, sent_a = pl.pallas_call(
        input_kernel,
        out_shape=(shape(flat, F32), shape(half_a, BF16), shape(half_a, BF16)),
        in_specs=[vmem()] * 12 + [anywhere(), anywhere(), scalars()],
        out_specs=(vmem(), anywhere(), anywhere()),
        scratch_shapes=[
            pltpu.VMEM((GROUPS, rows_a, width), BF16),
            pltpu.VMEM((GROUPS, rows_a, width), BF16),
            pltpu.SemaphoreType.DMA((GROUPS,)),
            pltpu.SemaphoreType.DMA((GROUPS,)),
        ],
        compiler_params=params(),
        cost_estimate=cost(2 * tokens * width * width * 6, 10 << 20),
        name="input_grad",
    )(
        x, d_middle, d_query, d_key, d_value, own, back_one, back_two, back_three, vec_one,
        const(pair.T), const(coarse_all.T), first_a, second_a, groups,
    )

    if fast:
        grad_b = scatter_slots(kept_b, sent_b)
        grad_a = scatter_slots(kept_a, sent_a)
        down_end = 16 + 16 * blocks + hidden // GROUPS
        grad_qkv = jnp.concatenate([grad_a[16 * i : 16 * i + 16] for i in range(3)], axis=1)
        small = grad_a[48:]
        grad_gain_one = small[0, :16]
        grad_shift_one = small[1, :16]
        grad_qv = small[2, :32] + small[3, :32]
        grad_out_weight = grad_b[0:16]
        grad_up = jnp.concatenate(
            [grad_b[16 + 16 * i : 32 + 16 * i] for i in range(blocks)], axis=1
        )
        grad_down = grad_b[16 + 16 * blocks : down_end]
        small = grad_b[down_end:]
        grad_gain_two = small[0, :16]
        grad_shift_two = small[1, :16]
        grad_out_bias = small[2, :16]
        grad_down_bias = small[3, :16]
        grad_up_bias = jnp.sum(small[4:8, :64], axis=0)
    else:

        def reduced(item):
            return lax.psum_scatter(item.astype(F32), AXES, scatter_dimension=0, tiled=True)

        def uncolumns(item, count):
            item = item.reshape(GROUPS, count, -1, width).transpose(0, 2, 1, 3)
            return reduced(item.reshape(-1, count * width))

        def unchunks(item, size):
            return reduced(item[:, : size // GROUPS].reshape(-1))

        all_a = jnp.concatenate([kept_a, sent_a])
        all_b = jnp.concatenate([kept_b, sent_b])
        down_end = 16 + 16 * blocks + hidden // GROUPS
        grad_qkv = uncolumns(all_a[:, :48], 3)
        grad_gain_one = unchunks(all_a[:, 48], width)
        grad_shift_one = unchunks(all_a[:, 49], width)
        grad_qv = unchunks(all_a[:, 50] + all_a[:, 51], 2 * width)
        grad_out_weight = uncolumns(all_b[:, :16], 1)
        grad_up = uncolumns(all_b[:, 16 : 16 + 16 * blocks], blocks)
        grad_down = uncolumns(all_b[:, 16 + 16 * blocks : down_end], 1)
        small = all_b[:, down_end:]
        grad_gain_two = unchunks(small[:, 0], width)
        grad_shift_two = unchunks(small[:, 1], width)
        grad_out_bias = unchunks(small[:, 2], width)
        grad_down_bias = unchunks(small[:, 3], width)
        grad_up_bias = unchunks(jnp.sum(small[:, 4:8], axis=1), hidden)

    return (
        result.reshape(layer_input.shape),
        d_input.reshape(layer_input.shape),
        grad_qkv,
        grad_qv,
        grad_out_weight,
        grad_out_bias,
        grad_gain_one,
        grad_shift_one,
        grad_gain_two,
        grad_shift_two,
        grad_up,
        grad_up_bias,
        grad_down,
        grad_down_bias,
    )


def solution(mesh):
    tokens = P(None, "dp", "seq", None)
    matrix = P(AXES, None)
    vector = P(AXES)
    in_specs = (
        tokens, matrix, vector, matrix, vector, vector, vector, vector, vector, matrix, vector,
        matrix, vector, tokens,
    )
    out_specs = (
        tokens, tokens, matrix, vector, matrix, vector, vector, vector, vector, vector, matrix,
        vector, matrix, vector,
    )
    return jax.shard_map(body, mesh=mesh, in_specs=in_specs, out_specs=out_specs, check_vma=False)
```

```python
from functools import partial

import jax
import jax.numpy as jnp
import numpy as np
from jax import lax
from jax.experimental import pallas as pl
from jax.experimental.pallas import tpu as pltpu
from jax.sharding import PartitionSpec as P

HEADS = 8
AXES = ("dp", "seq")
F32 = jnp.float32
BF16 = jnp.bfloat16
GROUPS = 32
SMALL = 16
EPS = 1e-05
VMEM_LIMIT = 60 * 1024 * 1024


def dot(left, right):
    return jnp.dot(left, right, preferred_element_type=F32)


def dot_right(left, right):
    return lax.dot_general(left, right, (((1,), (1,)), ((), ())), preferred_element_type=F32)


def dot_left(left, right):
    return lax.dot_general(left, right, (((0,), (0,)), ((), ())), preferred_element_type=F32)


def unit_of(values):
    centred = values - jnp.mean(values, axis=-1, keepdims=True)
    scale = lax.rsqrt(jnp.mean(centred * centred, axis=-1, keepdims=True) + EPS)
    return centred * scale, scale


def norm_back(grad, unit, scale, gain):
    scaled = grad * gain
    inner = (
        scaled
        - jnp.mean(scaled, axis=-1, keepdims=True)
        - unit * jnp.mean(scaled * unit, axis=-1, keepdims=True)
    )
    return inner * scale


def column_sum(values):
    return jnp.sum(values, axis=0, keepdims=True)


def expand_small(small, width, chunk):
    eye = lax.broadcasted_iota(jnp.int32, (128, width), 0) == (
        lax.broadcasted_iota(jnp.int32, (128, width), 1) % chunk
    )
    spread = dot(small, eye.astype(F32).astype(BF16))
    runs = GROUPS * chunk // width
    per_run = GROUPS // runs
    group = lax.broadcasted_iota(jnp.int32, (GROUPS * SMALL, width), 0) // SMALL
    column = lax.broadcasted_iota(jnp.int32, (GROUPS * SMALL, width), 1) // chunk
    kept = jnp.where(group % per_run == column, spread, 0.0).reshape(GROUPS, SMALL, width)
    return [jnp.sum(kept[run * per_run : (run + 1) * per_run], axis=0) for run in range(runs)]


def shrink_vectors(vectors, parts):
    width = vectors.shape[1]
    tiled = jnp.broadcast_to(vectors[None], (GROUPS, SMALL, width)).reshape(-1, width)
    row = lax.broadcasted_iota(jnp.int32, (GROUPS * SMALL, width), 0)
    lane = lax.broadcasted_iota(jnp.int32, (GROUPS * SMALL, width), 1)
    group = row // SMALL
    row = row % SMALL
    total = None
    for chunk, first, end in parts:
        runs = GROUPS * chunk // width
        per_run = GROUPS // runs
        keep = (group % per_run == lane // chunk) & (row >= first) & (row < end)
        if runs > 1:
            keep = keep & (row - first == group // per_run)
        eye = lax.broadcasted_iota(jnp.int32, (width, 128), 0) % chunk == lax.broadcasted_iota(
            jnp.int32, (width, 128), 1
        )
        part = dot(jnp.where(keep, tiled, 0.0).astype(BF16), eye.astype(F32).astype(BF16))
        total = part if total is None else total + part
    return total


def load_slots(first_ref, second_ref, groups_ref, target_ref, sems, at):
    half = first_ref.shape[0]
    lanes = pl.ds(at, target_ref.shape[2])
    copies = []
    for slot in range(half):
        copies.append(
            pltpu.make_async_copy(
                first_ref.at[slot, :, lanes], target_ref.at[groups_ref[0, slot]], sems.at[slot]
            )
        )
        copies.append(
            pltpu.make_async_copy(
                second_ref.at[slot, :, lanes],
                target_ref.at[groups_ref[0, half + slot]],
                sems.at[half + slot],
            )
        )
    for copy in copies:
        copy.start()
    return copies


def store_slots(source_ref, first_ref, second_ref, groups_ref, sems):
    half = first_ref.shape[0]
    copies = []
    for slot in range(half):
        copies.append(
            pltpu.make_async_copy(
                source_ref.at[groups_ref[0, half + slot]],
                second_ref.at[slot],
                sems.at[half + slot],
            )
        )
        copies.append(
            pltpu.make_async_copy(
                source_ref.at[groups_ref[0, slot]], first_ref.at[slot], sems.at[slot]
            )
        )
    for copy in copies:
        copy.start()
    for copy in copies:
        copy.wait()


def pair_average(rows):
    out = np.zeros((rows // 2, rows), np.float32)
    for i in range(rows // 2):
        out[i, 2 * i] = out[i, 2 * i + 1] = 0.5
    return out


def average(rows, factor):
    out = np.zeros((rows // factor, rows), np.float32)
    for i in range(rows // factor):
        out[i, i * factor : (i + 1) * factor] = 1.0 / factor
    return out


def attention_constants(piece, far_levels, local_top):
    top = local_top + far_levels - 1
    averaged = []
    for level in range(1, top + 1):
        averaged.append(np.repeat(average(piece, 2**level), 2**level, axis=0))
    coarse = np.concatenate([average(piece, 2**level) for level in range(1, local_top)], axis=0)
    tokens = np.arange(piece)
    masks = []
    sizes = []
    for level in range(local_top):
        keys = np.arange(piece >> level)
        block = (tokens >> level)[:, None] // 16
        if level == 0:
            mask = (block // 2) == (keys[None, :] // 32)
        else:
            mask = (block ^ 1) == (keys[None, :] // 16)
        masks += [mask, mask]
        sizes.append(piece >> level)
    for _ in range(far_levels):
        masks += [np.ones((piece, 16), bool)] * 2
        sizes.append(16)
    ones = []
    for level, size in enumerate(sizes):
        head_a = np.zeros((size, 128), np.float32)
        head_a[:, :64] = 2.0**level
        head_b = np.zeros((size, 128), np.float32)
        head_b[:, 64:] = 2.0**level
        ones += [head_a, head_b]
    return dict(
        averaged=np.concatenate(averaged, axis=0),
        averaged_wide=np.concatenate(averaged, axis=1),
        coarse=coarse,
        coarse_t=coarse.T.copy(),
        mask=np.concatenate(masks, axis=1).astype(np.float32),
        ones=np.concatenate(ones, axis=0),
        sizes=tuple(sizes),
    )


def far_constants(seqs):
    out = np.zeros((seqs * 16, seqs * (8 + 16 + 8 + 8)), np.float32)
    starts = (0, seqs * 8, seqs * 24, seqs * 32)
    for seq in range(seqs):
        for slot in range(4):
            for i in range(4):
                row = seq * 16 + slot * 4 + i
                if slot == 1:
                    at = starts[1] + seq * 16 + 4 * i
                    out[row, at : at + 4] = 0.25
                else:
                    at = starts[slot] + seq * 8 + 2 * i
                    out[row, at : at + 2] = 0.5
    return out


def lane_a(rows):
    return lax.broadcasted_iota(jnp.int32, (rows, 128), 1) < 64


def stacked(block, sizes):
    in_a = lane_a(block.shape[0])
    zero = jnp.zeros_like(block)
    head_a = jnp.where(in_a, block, zero)
    head_b = jnp.where(in_a, zero, block)
    parts = []
    at = 0
    for size in sizes:
        parts.append(head_a[at : at + size])
        parts.append(head_b[at : at + size])
        at += size
    return parts


def blocked(parts):
    levels = len(parts) // 2
    rows = []
    for level in range(2, levels):
        block = jnp.concatenate(parts[2 * level : 2 * level + 2], axis=0)
        zero = jnp.zeros_like(block)
        rows.append(
            jnp.concatenate(
                [block if other == level else zero for other in range(2, levels)], axis=1
            )
        )
    return jnp.concatenate(rows, axis=0)


def queries_of(plain_ref, averaged_ref, pair, levels):
    piece = plain_ref.shape[0]
    lanes = slice(pair * 128, pair * 128 + 128)
    rest = jnp.concatenate(
        [averaged_ref[(level - 1) * piece : level * piece, lanes] for level in range(2, levels)],
        axis=1,
    )
    return plain_ref[:, lanes], averaged_ref[0:piece, lanes], rest


def far_rows_of(refs):
    return jnp.concatenate([ref[...].astype(F32) for ref in refs], axis=0)


def pick_far(source_ref, seq, far_rows, seqs):
    parts = []
    at = 0
    for n in far_rows:
        parts.append(source_ref[pl.ds(pl.multiple_of(at + seq * n, n), n), :])
        at += seqs * n
    return jnp.concatenate(parts, axis=0)


def norm_kernel(x_ref, coarse_ref, pair_ref, base_ref, next_ref):
    unit, _ = unit_of(x_ref[...].astype(F32))
    base = dot(coarse_ref[...], unit.astype(BF16)).astype(BF16)
    base_ref[...] = base
    next_ref[...] = dot(pair_ref[...], base).astype(BF16)


def far_kernel(own_ref, one_ref, two_ref, three_ref, gather_ref, pair_ref, five_ref, six_ref):
    rows = far_rows_of((own_ref, one_ref, two_ref, three_ref)).astype(BF16)
    five = dot(gather_ref[...], rows).astype(BF16)
    five_ref[...] = five
    six_ref[...] = dot(pair_ref[...], five).astype(BF16)


def far_back_kernel(
    five_ref, six_a_ref, six_b_ref, one_ref, two_ref, three_ref, spread_ref, pair_ref,
    own_out, one_out, two_out, three_out,
):
    six = (six_a_ref[...].astype(F32) + six_b_ref[...].astype(F32)).astype(BF16)
    five = (five_ref[...].astype(F32) + dot(pair_ref[...], six)).astype(BF16)
    rows = dot(spread_ref[...], five)
    own = own_out.shape[0]
    one = own + one_ref.shape[0]
    two = one + two_ref.shape[0]
    own_out[...] = rows[:own]
    one_out[...] = (rows[own:one] + one_ref[...].astype(F32)).astype(BF16)
    two_out[...] = (rows[one:two] + two_ref[...].astype(F32)).astype(BF16)
    three_out[...] = (rows[two:] + three_ref[...].astype(F32)).astype(BF16)


def mix_kernel(*refs, far_rows, sizes, local_top):
    fars = len(far_rows)
    x_ref, first_ref, second_ref, groups_ref = refs[:4]
    far_refs = refs[4 : 4 + fars]
    averaged_ref, coarse_ref, mask_ref, ones_ref = refs[4 + fars : 8 + fars]
    vec_ref, q_out, kall_ref, vall_ref, p_ref, att_ref, rden_ref = refs[8 + fars : 15 + fars]
    weight_ref, q_ref, k_ref, v_ref, kf_ref, vf_ref, qe_ref, sems = refs[15 + fars :]
    width = x_ref.shape[1]
    piece = q_out.shape[0]
    seqs = x_ref.shape[0] // piece
    levels = len(sizes)
    seq = pl.program_id(0)

    @pl.when(seq == 0)
    def _():
        copies = load_slots(first_ref, second_ref, groups_ref, weight_ref, sems, 0)
        unit, _ = unit_of(x_ref[...].astype(F32))
        far = far_rows_of(far_refs)
        for copy in copies:
            copy.wait()
        small = weight_ref[:, :, 3 * width :].reshape(GROUPS * SMALL, 128)
        plain = expand_small(small, width, width // GROUPS)[0]
        biases = expand_small(small, width, 2 * width // GROUPS)
        ups = expand_small(small, width, 4 * width // GROUPS)
        vec_ref[...] = jnp.concatenate(
            [plain[0:6], biases[0][6:7], biases[1][6:7]]
            + [up[7:8] for up in ups]
            + [jnp.zeros((4, width), F32)],
            axis=0,
        )
        gain, shift = plain[0:1], plain[1:2]
        query_bias, value_bias = biases[0][6:7], biases[1][6:7]
        normed = (unit * gain + shift).astype(BF16)
        far = (far * gain + shift).astype(BF16)
        weight = weight_ref[:, :, 0:width].reshape(width, width)
        q_ref[...] = ((dot(normed, weight) + query_bias).astype(BF16).astype(F32) * 0.125).astype(
            BF16
        )
        weight = weight_ref[:, :, width : 2 * width].reshape(width, width)
        k_ref[...] = dot(normed, weight).astype(BF16)
        kf_ref[...] = dot(far, weight)
        weight = weight_ref[:, :, 2 * width : 3 * width].reshape(width, width)
        v_ref[...] = (dot(normed, weight) + value_bias).astype(BF16)
        vf_ref[...] = dot(far, weight) + value_bias

    rows = pl.ds(pl.multiple_of(seq * piece, piece), piece)
    queries = q_ref[rows, :]
    q_out[...] = queries
    qe_ref[...] = dot(averaged_ref[...], queries).astype(BF16)
    keys = k_ref[rows, :]
    values = v_ref[rows, :]
    coarse_keys = dot(coarse_ref[...], keys).astype(BF16)
    coarse_values = dot(coarse_ref[...], values)
    scaled = [values]
    at = 0
    for level in range(1, local_top):
        scaled.append((coarse_values[at : at + sizes[level]] * 2.0**level).astype(BF16))
        at += sizes[level]
    far_values = pick_far(vf_ref, seq, far_rows, seqs)
    for level in range(local_top, levels):
        at = 16 * (level - local_top)
        scaled.append((far_values[at : at + 16] * 2.0**level).astype(BF16))
    kall_ref[0] = jnp.concatenate(
        [keys, coarse_keys, pick_far(kf_ref, seq, far_rows, seqs).astype(BF16)], axis=0
    )
    vall_ref[0] = jnp.concatenate(scaled, axis=0)
    for pair in range(width // 128):
        lanes = slice(pair * 128, pair * 128 + 128)
        plain, one, rest = queries_of(q_out, qe_ref, pair, levels)
        key_parts = stacked(kall_ref[0, :, lanes], sizes)
        scores = jnp.concatenate(
            [
                dot_right(plain, jnp.concatenate(key_parts[0:2], axis=0)),
                dot_right(one, jnp.concatenate(key_parts[2:4], axis=0)),
                dot_right(rest, blocked(key_parts)),
            ],
            axis=1,
        )
        weights = jnp.where(mask_ref[...] > 0.0, jnp.exp(scores), 0.0).astype(BF16)
        p_ref[0, pair] = weights
        both = jnp.concatenate(
            [jnp.concatenate(stacked(vall_ref[0, :, lanes], sizes), axis=0), ones_ref[...]], axis=1
        )
        sums = dot(weights, both)
        rden = 1.0 / sums[:, 128:]
        rden_ref[:, lanes] = rden
        att_ref[:, lanes] = (sums[:, :128] * rden).astype(BF16)


def feed_kernel(
    x_ref, cot_ref, att_ref, vec_ref, first_in, second_in, down_ref, groups_ref,
    out_ref, dmid_ref, datt_ref, sum_ref, first_ref, second_ref,
    weight_ref, hidden_ref, gpre_ref, normed_ref, branch_ref, grad_ref, in_sems, out_sems,
):
    tokens, width = x_ref.shape
    copies = load_slots(first_in, second_in, groups_ref, weight_ref, in_sems, 0)
    blocks = hidden_ref.shape[1] // width
    out_bias = vec_ref[2:3, :]
    gain = vec_ref[3:4, :]
    shift = vec_ref[4:5, :]
    down_bias = vec_ref[5:6, :]
    sum_ref[...] = jnp.zeros_like(sum_ref)
    tile = 256
    for copy in copies:
        copy.wait()
    out_weight = weight_ref[:, :, 0:width].reshape(width, width)

    def feed(i, carry):
        rows = pl.ds(pl.multiple_of(i * tile, tile), tile)
        middle = x_ref[rows, :].astype(F32) + dot(att_ref[rows, :], out_weight) + out_bias
        unit, inverse = unit_of(middle)
        normed = (unit * gain + shift).astype(BF16)
        normed_ref[rows, :] = normed
        g_out = cot_ref[rows, :]
        result = middle + down_bias
        d_two = jnp.zeros((tile, width), F32)
        for block in range(blocks):
            lanes = slice(block * width, block * width + width)
            up = weight_ref[:, :, width * (block + 1) : width * (block + 2)].reshape(width, width)
            down = down_ref[lanes, :]
            pre = dot(normed, up) + vec_ref[8 + block : 9 + block, :]
            cdf = 0.5 + 0.5 * lax.erf(pre * 0.7071067811865476)
            hidden = (pre * cdf).astype(BF16)
            hidden_ref[rows, lanes] = hidden
            result = result + dot(hidden, down)
            slope = cdf + pre * (0.3989422804014327 * jnp.exp(-0.5 * pre * pre))
            g_pre = (dot_right(g_out, down) * slope).astype(BF16)
            gpre_ref[rows, lanes] = g_pre
            sum_ref[8 + block : 9 + block, :] += column_sum(g_pre.astype(F32))
            d_two = d_two + dot_right(g_pre, up)
        out_ref[rows, :] = result.astype(BF16)
        cot = g_out.astype(F32)
        d_middle = cot + norm_back(d_two, unit, inverse, gain)
        dmid_ref[rows, :] = d_middle
        branch = d_middle.astype(BF16)
        branch_ref[rows, :] = branch
        datt_ref[rows, :] = dot_right(branch, out_weight)
        sum_ref[2:3, :] += column_sum(branch.astype(F32))
        sum_ref[3:4, :] += column_sum(d_two * unit)
        sum_ref[4:5, :] += column_sum(d_two)
        sum_ref[5:6, :] += column_sum(cot)
        return carry

    lax.fori_loop(0, tokens // tile, feed, 0)
    per_group = down_ref.shape[0] // GROUPS
    first_row = 16 + 16 * blocks
    grad = dot_left(att_ref[...], branch_ref[...])
    grad_ref[:, 0:16, :] = grad.astype(BF16).reshape(GROUPS, 16, width)
    for block in range(blocks):
        lanes = slice(block * width, block * width + width)
        groups = width // per_group
        grad = dot_left(hidden_ref[:, lanes], cot_ref[...])
        grad_ref[groups * block : groups * (block + 1), first_row : first_row + per_group, :] = (
            grad.astype(BF16).reshape(groups, per_group, width)
        )
        grad = dot_left(normed_ref[...], gpre_ref[:, lanes])
        grad_ref[:, 16 + 16 * block : 32 + 16 * block, :] = grad.astype(BF16).reshape(
            GROUPS, 16, width
        )
    store_slots(grad_ref, first_ref, second_ref, groups_ref, out_sems)


def attention_back_kernel(*refs, far_rows, sizes, local_top):
    fars = len(far_rows)
    q_ref, kall_ref, vall_ref, p_ref, att_ref, rden_ref, datt_ref = refs[:7]
    x_ref, vec_ref, sum_ref, first_in, second_in, groups_ref = refs[7:13]
    averaged_ref, wide_ref, coarse_t_ref, ones_ref = refs[13:17]
    far_refs = refs[17 : 17 + fars]
    scaled_ref, first_ref, second_ref = refs[17 + fars : 20 + fars]
    dfar_refs = refs[20 + fars : 20 + 2 * fars]
    (
        weight_ref, grad_ref, dq_ref, dk_ref, dv_ref, dkf_ref, dvf_ref, qe_ref, dkall_ref,
        dvall_ref, t_ref, dqacc_ref, in_sems, out_sems,
    ) = refs[20 + 2 * fars :]
    width = x_ref.shape[1]
    piece = q_ref.shape[0]
    seqs = x_ref.shape[0] // piece
    levels = len(sizes)
    starts = np.concatenate([[0], np.cumsum(sizes)]).tolist()
    local = starts[local_top]
    seq = pl.program_id(0)

    def weights_in():
        return load_slots(first_in, second_in, groups_ref, weight_ref, in_sems, 0)

    qe_ref[...] = dot(averaged_ref[...], q_ref[...]).astype(BF16)
    near = 2 * sizes[0]
    mid = near + 2 * sizes[1]
    for pair in range(width // 128):
        lanes = slice(pair * 128, pair * 128 + 128)
        plain, one, rest = queries_of(q_ref, qe_ref, pair, levels)
        key_parts = stacked(kall_ref[0, :, lanes], sizes)
        both = jnp.concatenate(
            [jnp.concatenate(stacked(vall_ref[0, :, lanes], sizes), axis=0), ones_ref[...]], axis=1
        )
        d_num = datt_ref[:, lanes] * rden_ref[:, lanes]
        d_den = -d_num * att_ref[:, lanes].astype(F32)
        d_num = d_num.astype(BF16)
        weights = p_ref[0, pair]
        d_weights = dot_right(jnp.concatenate([d_num, d_den.astype(BF16)], axis=1), both)
        d_scores = (weights.astype(F32) * d_weights).astype(BF16)
        d_key_near = dot_left(d_scores[:, :near], plain)
        d_key_mid = dot_left(d_scores[:, near:mid], one)
        d_key_rest = dot_left(d_scores[:, mid:], rest)
        d_value = dot_left(weights, d_num)
        dqacc_ref[:, lanes] = dot(d_scores[:, :near], jnp.concatenate(key_parts[0:2], axis=0))
        t_ref[0:piece, lanes] = dot(
            d_scores[:, near:mid], jnp.concatenate(key_parts[2:4], axis=0)
        ).astype(BF16)
        d_rest = dot(d_scores[:, mid:], blocked(key_parts)).astype(BF16)
        at = 0
        for level in range(levels):
            size = sizes[level]
            low, high = starts[level], starts[level + 1]
            in_a = lane_a(size)
            if level == 0:
                source = d_key_near
            elif level == 1:
                source = d_key_mid
            else:
                block = slice((level - 2) * 128, (level - 1) * 128)
                source = d_key_rest[at - mid : at - mid + 2 * size, block]
                t_ref[(level - 1) * piece : level * piece, lanes] = d_rest[:, block]
            dkall_ref[low:high, lanes] = jnp.where(in_a, source[:size], source[size:])
            values = d_value[at : at + 2 * size]
            dvall_ref[low:high, lanes] = jnp.where(in_a, values[:size], values[size:]) * 2.0**level
            at += 2 * size
    rows = pl.ds(pl.multiple_of(seq * piece, piece), piece)
    dq_ref[rows, :] = ((dqacc_ref[...] + dot(wide_ref[...], t_ref[...])) * 0.125).astype(BF16)
    for target, source in ((dk_ref, dkall_ref), (dv_ref, dvall_ref)):
        spread = dot(coarse_t_ref[...], source[piece:local, :].astype(BF16))
        target[rows, :] = (source[0:piece, :] + spread).astype(BF16)
    at = 0
    low = local
    for n in far_rows:
        target = pl.ds(pl.multiple_of(at + seq * n, n), n)
        dkf_ref[target, :] = dkall_ref[low : low + n, :]
        dvf_ref[target, :] = dvall_ref[low : low + n, :]
        at += seqs * n
        low += n

    @pl.when(seq == seqs - 1)
    def _():
        copies = weights_in()
        gain = vec_ref[0:1, :]
        shift = vec_ref[1:2, :]
        unit, _ = unit_of(x_ref[...].astype(F32))
        normed = (unit * gain + shift).astype(BF16)
        far = far_rows_of(far_refs)
        far_normed = (far * gain + shift).astype(BF16)
        both = jnp.concatenate([normed, far_normed], axis=0)
        far_grads = (None, dkf_ref[...].astype(BF16), dvf_ref[...].astype(BF16))
        grads = (dq_ref[...], dk_ref[...], dv_ref[...])
        for copy in copies:
            copy.wait()
        d_one = jnp.zeros(x_ref.shape, F32)
        d_far = jnp.zeros(far.shape, F32)
        for part in range(3):
            lanes = slice(part * width, part * width + width)
            weight = weight_ref[:, :, lanes].reshape(width, width)
            d_one = d_one + dot_right(grads[part], weight)
            if part == 0:
                grad = dot_left(normed, grads[part])
            else:
                d_far = d_far + dot_right(far_grads[part], weight)
                grad = dot_left(both, jnp.concatenate([grads[part], far_grads[part]], axis=0))
            grad_ref[:, :, lanes] = grad.astype(BF16).reshape(GROUPS, 16, width)
        scaled_ref[...] = d_one * gain
        at = 0
        for ref in dfar_refs:
            ref[...] = (d_far[at : at + ref.shape[0]] * gain).astype(BF16)
            at += ref.shape[0]
        vectors = jnp.concatenate(
            [
                column_sum(d_one * unit) + column_sum(d_far * far),
                column_sum(d_one) + column_sum(d_far),
                sum_ref[2:6, :],
                column_sum(grads[0].astype(F32)),
                column_sum(grads[2].astype(F32)) + column_sum(dvf_ref[...]),
                sum_ref[8:16, :],
            ],
            axis=0,
        )
        chunk = width // GROUPS
        small = shrink_vectors(vectors, ((chunk, 0, 6), (2 * chunk, 6, 8), (4 * chunk, 8, 12)))
        grad_ref[:, :, 3 * width :] = small.reshape(GROUPS, SMALL, 128).astype(BF16)
        store_slots(grad_ref, first_ref, second_ref, groups_ref, out_sems)


def input_kernel(
    x_ref, dmid_ref, scaled_ref, own_ref, one_ref, two_ref, three_ref, pair_ref, spread_ref,
    din_ref,
):
    unit, inverse = unit_of(x_ref[...].astype(F32))
    lower = own_ref[...] + two_ref[...].astype(F32) + three_ref[...].astype(F32)
    base = one_ref[...].astype(F32) + dot(pair_ref[...], lower.astype(BF16))
    scaled = scaled_ref[...] + dot(spread_ref[...], base.astype(BF16))
    inner = (
        scaled
        - jnp.mean(scaled, axis=-1, keepdims=True)
        - unit * jnp.mean(scaled * unit, axis=-1, keepdims=True)
    )
    din_ref[...] = dmid_ref[...] + inner * inverse


def last_mix_kernel(kept_ref, other_ref, matrix_ref, *vector_refs):
    total = kept_ref[0].astype(F32) + other_ref[0].astype(F32)
    lanes = matrix_ref.shape[1]
    matrix_ref[...] = total[:, :lanes]
    small = total[:, lanes:]
    for i in range(6):
        vector_refs[i][...] = small[i : i + 1, : vector_refs[i].shape[1]]
    vector_refs[6][...] = column_sum(small[6:8])[:, : vector_refs[6].shape[1]]
    vector_refs[7][...] = column_sum(small[8:12])[:, : vector_refs[7].shape[1]]


def last_feed_kernel(kept_ref, other_ref, out_ref, up_ref, down_ref):
    total = kept_ref[0].astype(F32) + other_ref[0].astype(F32)
    width = out_ref.shape[1]
    blocks = up_ref.shape[1] // width
    out_ref[...] = total[0:16]
    for block in range(blocks):
        up_ref[:, block * width : (block + 1) * width] = total[16 + 16 * block : 32 + 16 * block]
    down_ref[...] = total[16 + 16 * blocks :]


def vmem():
    return pl.BlockSpec(memory_space=pltpu.VMEM)


def anywhere():
    return pl.BlockSpec(memory_space=pl.ANY)


def scalars():
    return pl.BlockSpec(memory_space=pltpu.SMEM)


def fixed(*dims):
    return pl.BlockSpec(dims, lambda i: (0,) * len(dims))


def moving(*dims):
    return pl.BlockSpec(dims, lambda i: (i,) + (0,) * (len(dims) - 1))


def shape(dims, dtype):
    return jax.ShapeDtypeStruct(dims, dtype)


def params():
    return pltpu.CompilerParams(vmem_limit_bytes=VMEM_LIMIT)


def cost(flops, traffic, exps=0):
    return pl.CostEstimate(flops=flops, bytes_accessed=traffic, transcendentals=exps)


def const(values):
    return jnp.asarray(values, BF16)


def bit_orders():
    return ((8, 4, 16, 2), (2, 8, 4, 16))


def slot_offset(slot, order):
    return sum(bit for k, bit in enumerate(order) if slot >> k & 1)


def group_table():
    orders = bit_orders()
    table = np.zeros((32, 32), np.int32)
    for device in range(32):
        core = device & 1
        for slot in range(16):
            table[device, slot] = device ^ slot_offset(slot, orders[core])
            table[device, 16 + slot] = device ^ 1 ^ slot_offset(slot, orders[1 - core])
    return table


def exchange(value, bits):
    if isinstance(bits, int):
        bits = (bits, bits)
    count = lax.axis_size(AXES)
    return lax.ppermute(value, AXES, [(i, i ^ bits[i & 1]) for i in range(count)])


def after(value, *others):
    return lax.optimization_barrier((value,) + others)[0]


def gather_step(buffer, k):
    orders = bit_orders()
    return jnp.concatenate([buffer, exchange(buffer, (orders[0][k], orders[1][k]))], axis=0)


def added(left, right):
    return (left.astype(F32) + right.astype(F32)).astype(BF16)


def scatter_step(kept, other, k, give=False):
    orders = bit_orders()
    half = 2**k
    high = added(kept[half:], other[half:])
    received = exchange(high, (orders[0][k], orders[1][k]))
    low = added(kept[:half], other[:half])
    return (low, received, high) if give else (low, received)


def coarsen(values):
    return (values[:, 0::2] + values[:, 1::2]) * 0.5


def whole_far(base, seqs, far_levels, position):
    rows = base.reshape(seqs, 16, base.shape[1])
    full = lax.all_gather(rows, "seq", axis=1, tiled=True).astype(F32)
    parts = []
    for extra in range(far_levels):
        partner = (position // 2**extra) ^ 1
        parts.append(lax.dynamic_slice_in_dim(full, partner * 16, 16, axis=1))
        if extra + 1 < far_levels:
            full = coarsen(full)
    return jnp.concatenate(parts, axis=1).astype(BF16).reshape(seqs * 16 * far_levels, -1)


def whole_far_back(grad, seqs, far_levels, position):
    stack = grad.reshape(seqs, far_levels, 16, -1).astype(F32)
    ids = jnp.arange(far_levels).reshape(1, far_levels, 1, 1)
    count = lax.axis_size("seq")
    for bit in range(far_levels):
        pairs = [(i, i ^ 1 << bit) for i in range(count)]
        other = lax.ppermute(stack.astype(BF16), "seq", pairs).astype(F32)
        stack = jnp.where(ids > bit, stack + other, jnp.where(ids == bit, other, stack))
    own = jnp.zeros((seqs, 16, stack.shape[-1]), F32)
    for extra in range(far_levels):
        rows = 16 >> extra
        offset = position % 2**extra * rows
        part = lax.dynamic_slice_in_dim(stack[:, extra], offset, rows, axis=1)
        own = own + jnp.repeat(part, 2**extra, axis=1) * 0.5**extra
    return own.reshape(seqs * 16, -1).astype(BF16)


def body(
    layer_input, qkv_weight, qv_bias, out_weight, out_bias, first_gain, first_shift, second_gain,
    second_shift, up_weight, up_bias, down_weight, down_bias, cotangent,
):
    batches, per_batch, piece, width = layer_input.shape
    seqs = batches * per_batch
    tokens = seqs * piece
    hidden = up_weight.shape[1]
    blocks = hidden // width
    devices = lax.axis_size(AXES)
    pieces = lax.axis_size("seq")
    position = lax.axis_index("seq")
    far_levels = pieces.bit_length() - 1
    local_top = (piece // 16).bit_length() - 1
    fast = devices == GROUPS and pieces == 16
    x = layer_input.reshape(tokens, width)
    cot = cotangent.reshape(tokens, width)
    consts = attention_constants(piece, far_levels, local_top)
    sizes = consts["sizes"]
    keys = sum(sizes)
    flat = (tokens, width)
    base_rows = seqs * 16
    coarse_all = np.kron(np.eye(seqs, dtype=np.float32), average(piece, piece // 16))
    pair = np.kron(np.eye(seqs, dtype=np.float32), pair_average(16))
    gather_far = far_constants(seqs)
    vectors = (
        first_gain, first_shift, out_bias, second_gain, second_shift, down_bias, qv_bias, up_bias,
    )

    down = lax.all_gather(down_weight, AXES, axis=0, tiled=True)
    base, below = pl.pallas_call(
        norm_kernel,
        out_shape=(shape((base_rows, width), BF16), shape((base_rows // 2, width), BF16)),
        in_specs=[vmem()] * 3,
        out_specs=(vmem(),) * 2,
        compiler_params=params(),
        cost_estimate=cost(1 << 24, 1 << 20),
        name="norm",
    )(x, const(coarse_all), const(pair))

    if fast:
        me = lax.axis_index(AXES)
        groups = lax.dynamic_slice_in_dim(jnp.asarray(group_table()), me, 1, axis=0)
        pack_a = jnp.pad(qkv_weight, ((0, 0), (0, 128)))
        for row, vector in enumerate(vectors):
            at = 3 * width
            item = vector.reshape(1, -1)
            lanes = (at, 128 - item.shape[1])
            pack_a = pack_a + jnp.pad(item, ((row, SMALL - 1 - row), lanes))
        a = gather_step(pack_a[None], 0)
        b = after(jnp.concatenate([out_weight, up_weight], axis=1)[None], a)
        near, half = after(base, a), after(below, a)
        a = after(a, base)
        one, two, three = exchange(near, 1), exchange(half, 2), exchange(half, 3)
        five, six = pl.pallas_call(
            far_kernel,
            out_shape=(shape((base_rows, width), BF16), shape((base_rows // 2, width), BF16)),
            in_specs=[vmem()] * 6,
            out_specs=(vmem(),) * 2,
            compiler_params=params(),
            cost_estimate=cost(1 << 20, 1 << 16),
            name="far",
        )(below, one, two, three, const(gather_far), const(pair))
        a = after(gather_step(a, 1), five, six)
        b = after(gather_step(b, 0), a)
        far = (one, two, three, exchange(five, 4), exchange(six, 8), exchange(six, 12))
        far_rows = (16, 8, 8, 16, 8, 8)
        a = gather_step(a, 2)
        b = after(gather_step(b, 1), a)
        a = gather_step(after(a, *far), 3)
        b = after(gather_step(b, 2), a)
        first_a, second_a = a, exchange(a, 1)
        b = gather_step(b, 3)
    else:
        groups = jnp.arange(GROUPS, dtype=jnp.int32)[None]

        def whole(value):
            return lax.all_gather(value, AXES, axis=0, tiled=True).reshape(
                (GROUPS, -1) + value.shape[1:]
            )

        small = [jnp.pad(v, ((0, 0), (0, 128 - v.shape[1]))) for v in map(whole, vectors)]
        small += [jnp.zeros((GROUPS, 128), BF16)] * (SMALL - len(small))
        parts = [whole(qkv_weight), jnp.stack(small, axis=1), whole(out_weight), whole(up_weight)]
        gathered = jnp.concatenate(parts, axis=2)
        split = 3 * width + 128
        first_a, second_a = gathered[:16, :, :split], gathered[16:, :, :split]
        first_b, second_b = gathered[:16, :, split:], gathered[16:, :, split:]
        far = (whole_far(base, seqs, far_levels, position),)
        far_rows = (16 * far_levels,)

    lanes_a = 3 * width + 128
    lanes_b = width + hidden
    rows_b = 16 + 16 * blocks + hidden // GROUPS
    top = len(sizes) - 1
    pairs = width // 128
    total_far = seqs * 16 * far_levels
    slots = pltpu.SemaphoreType.DMA((GROUPS,))

    vec, queries, kall, vall, weights, attended, rden = pl.pallas_call(
        partial(mix_kernel, far_rows=far_rows, sizes=sizes, local_top=local_top),
        grid=(seqs,),
        out_shape=(
            shape((16, width), F32),
            shape(flat, BF16),
            shape((seqs, keys, width), BF16),
            shape((seqs, keys, width), BF16),
            shape((seqs, pairs, piece, 2 * keys), BF16),
            shape(flat, BF16),
            shape(flat, F32),
        ),
        in_specs=[fixed(*flat), anywhere(), anywhere(), scalars()]
        + [fixed(*item.shape) for item in far]
        + [
            fixed(top * piece, piece),
            fixed(*consts["coarse"].shape),
            fixed(piece, 2 * keys),
            fixed(2 * keys, 128),
        ],
        out_specs=(
            fixed(16, width),
            moving(piece, width),
            moving(1, keys, width),
            moving(1, keys, width),
            moving(1, pairs, piece, 2 * keys),
            moving(piece, width),
            moving(piece, width),
        ),
        scratch_shapes=[
            pltpu.VMEM((GROUPS, 16, lanes_a), BF16),
            pltpu.VMEM(flat, BF16),
            pltpu.VMEM(flat, BF16),
            pltpu.VMEM(flat, BF16),
            pltpu.VMEM((total_far, width), F32),
            pltpu.VMEM((total_far, width), F32),
            pltpu.VMEM((top * piece, width), BF16),
            slots,
        ],
        compiler_params=params(),
        cost_estimate=cost(1 << 24, 1 << 18),
        name="mix",
    )(
        x, first_a, second_a, groups, *far, const(consts["averaged"]), const(consts["coarse"]),
        jnp.asarray(consts["mask"]), const(consts["ones"]),
    )

    if fast:
        b = after(b, attended)
        first_b, second_b = b, exchange(b, 1)
    half_b = (GROUPS // 2, rows_b, width)
    result, d_middle, d_attended, sums, kept_b, sent_b = pl.pallas_call(
        feed_kernel,
        out_shape=(
            shape(flat, BF16),
            shape(flat, F32),
            shape(flat, F32),
            shape((16, width), F32),
            shape(half_b, BF16),
            shape(half_b, BF16),
        ),
        in_specs=[vmem()] * 4 + [anywhere(), anywhere(), vmem(), scalars()],
        out_specs=(vmem(),) * 4 + (anywhere(),) * 2,
        scratch_shapes=[
            pltpu.VMEM((GROUPS, 16, lanes_b), BF16),
            pltpu.VMEM((tokens, hidden), BF16),
            pltpu.VMEM((tokens, hidden), BF16),
            pltpu.VMEM(flat, BF16),
            pltpu.VMEM(flat, BF16),
            pltpu.VMEM((GROUPS, rows_b, width), BF16),
            slots,
            slots,
        ],
        compiler_params=params(),
        cost_estimate=cost(8 << 30, 20 << 20),
        name="feed",
    )(x, cot, attended, vec, first_b, second_b, down, groups)

    if fast:
        other_b = exchange(sent_b, 1)
        kept_b, other_b, high_b = scatter_step(kept_b, other_b, 3, True)
        d_attended = after(d_attended, high_b)

    half_a = (GROUPS // 2, 16, lanes_a)
    outs = pl.pallas_call(
        partial(attention_back_kernel, far_rows=far_rows, sizes=sizes, local_top=local_top),
        grid=(seqs,),
        out_shape=(shape(flat, F32), shape(half_a, BF16), shape(half_a, BF16))
        + tuple(shape(item.shape, BF16) for item in far),
        in_specs=[
            moving(piece, width),
            moving(1, keys, width),
            moving(1, keys, width),
            moving(1, pairs, piece, 2 * keys),
            moving(piece, width),
            moving(piece, width),
            moving(piece, width),
            fixed(*flat),
            fixed(16, width),
            fixed(16, width),
            anywhere(),
            anywhere(),
            scalars(),
            fixed(top * piece, piece),
            fixed(piece, top * piece),
            fixed(*consts["coarse_t"].shape),
            fixed(2 * keys, 128),
        ]
        + [fixed(*item.shape) for item in far],
        out_specs=(fixed(*flat), anywhere(), anywhere())
        + tuple(fixed(*item.shape) for item in far),
        scratch_shapes=[
            pltpu.VMEM((GROUPS, 16, lanes_a), BF16),
            pltpu.VMEM((GROUPS, 16, lanes_a), BF16),
            pltpu.VMEM(flat, BF16),
            pltpu.VMEM(flat, BF16),
            pltpu.VMEM(flat, BF16),
            pltpu.VMEM((total_far, width), F32),
            pltpu.VMEM((total_far, width), F32),
            pltpu.VMEM((top * piece, width), BF16),
            pltpu.VMEM((keys, width), F32),
            pltpu.VMEM((keys, width), F32),
            pltpu.VMEM((top * piece, width), BF16),
            pltpu.VMEM((piece, width), F32),
            slots,
            slots,
        ],
        compiler_params=params(),
        cost_estimate=cost(6 << 30, 20 << 20),
        name="attention_back",
    )(
        queries, kall, vall, weights, attended, rden, d_attended, x, vec, sums, first_a, second_a,
        groups, const(consts["averaged"]), const(consts["averaged_wide"]),
        const(consts["coarse_t"]), const(consts["ones"]), *far,
    )
    scaled, kept_a, sent_a = outs[:3]
    d_far = outs[3:]

    if fast:
        other_a = exchange(sent_a, 1)
        kept_b, other_b = scatter_step(kept_b, other_b, 2)
        back = [exchange(item, bits) for item, bits in zip(d_far[3:], (4, 8, 12))]
        other_a, other_b, *back = lax.optimization_barrier((other_a, other_b, *back))
        own, out_one, out_two, out_three = pl.pallas_call(
            far_back_kernel,
            out_shape=(
                shape((base_rows // 2, width), F32),
                shape((base_rows, width), BF16),
                shape((base_rows // 2, width), BF16),
                shape((base_rows // 2, width), BF16),
            ),
            in_specs=[vmem()] * 8,
            out_specs=(vmem(),) * 4,
            compiler_params=params(),
            cost_estimate=cost(1 << 24, 1 << 19),
            name="far_back",
        )(*back, d_far[0], d_far[1], d_far[2], const(gather_far.T), const(pair.T))
        kept_a, other_a = scatter_step(kept_a, other_a, 3)
        kept_b, other_b = scatter_step(kept_b, other_b, 1)
        back_one = exchange(out_one, 1)
        back_two = exchange(out_two, 2)
        back_three = exchange(out_three, 3)
        other_a, other_b, back_one, back_two, back_three = lax.optimization_barrier(
            (other_a, other_b, back_one, back_two, back_three)
        )
        kept_a, other_a = scatter_step(kept_a, other_a, 2)
        kept_b, other_b = scatter_step(kept_b, other_b, 0)
    else:
        back_one = whole_far_back(d_far[0], seqs, far_levels, position)
        own = jnp.zeros((base_rows // 2, width), F32)
        back_two = back_three = jnp.zeros((base_rows // 2, width), BF16)

    d_input = pl.pallas_call(
        input_kernel,
        out_shape=shape(flat, F32),
        in_specs=[vmem()] * 9,
        out_specs=vmem(),
        compiler_params=params(),
        cost_estimate=cost(1 << 27, 5 << 20),
        name="input_grad",
    )(
        x, d_middle, scaled, own, back_one, back_two, back_three, const(pair.T),
        const(coarse_all.T),
    )

    up_end = 16 + 16 * blocks
    if fast:
        other_a, other_b, d_input = lax.optimization_barrier((other_a, other_b, d_input))
        kept_a, other_a = scatter_step(kept_a, other_a, 1)
        grad_out_weight, grad_up, grad_down = pl.pallas_call(
            last_feed_kernel,
            out_shape=(
                shape(out_weight.shape, F32),
                shape(up_weight.shape, F32),
                shape(down_weight.shape, F32),
            ),
            in_specs=[vmem()] * 2,
            out_specs=(vmem(),) * 3,
            compiler_params=params(),
            cost_estimate=cost(1 << 20, 1 << 20),
            name="last_feed",
        )(kept_b, other_b)
        kept_a, other_a = scatter_step(kept_a, other_a, 0)
        grad_qkv, *plain = pl.pallas_call(
            last_mix_kernel,
            out_shape=(shape(qkv_weight.shape, F32),)
            + tuple(
                shape((1, v.shape[0]), F32)
                for v in (
                    first_gain, first_shift, out_bias, second_gain, second_shift, down_bias,
                    qv_bias, up_bias,
                )
            ),
            in_specs=[vmem()] * 2,
            out_specs=(vmem(),) * 9,
            compiler_params=params(),
            cost_estimate=cost(1 << 20, 1 << 18),
            name="last_mix",
        )(kept_a, other_a)
        plain = [item.reshape(-1) for item in plain]
        grad_qv, grad_up_bias = plain[6:8]
    else:

        def reduced(item):
            return lax.psum_scatter(item.astype(F32), AXES, scatter_dimension=0, tiled=True)

        def rows_of(item):
            return reduced(item.reshape((-1,) + item.shape[2:]))

        all_a = jnp.concatenate([kept_a, sent_a])
        all_b = jnp.concatenate([kept_b, sent_b])
        grad_qkv = rows_of(all_a[:, :, : 3 * width])
        small = all_a[:, :, 3 * width :]
        chunk = width // GROUPS
        plain = [reduced(small[:, i, :chunk].reshape(-1)) for i in range(6)]
        grad_qv = reduced(jnp.sum(small[:, 6:8, : 2 * chunk], axis=1).reshape(-1))
        grad_up_bias = reduced(jnp.sum(small[:, 8:12, : 4 * chunk], axis=1).reshape(-1))
        grad_out_weight = rows_of(all_b[:, :16])
        ups = all_b[:, 16:up_end].reshape(GROUPS, blocks, 16, width)
        grad_up = reduced(ups.transpose(0, 2, 1, 3).reshape(width, hidden))
        grad_down = rows_of(all_b[:, up_end:])

    return (
        result.reshape(layer_input.shape),
        d_input.reshape(layer_input.shape),
        grad_qkv,
        grad_qv,
        grad_out_weight,
        plain[2],
        plain[0],
        plain[1],
        plain[3],
        plain[4],
        grad_up,
        grad_up_bias,
        grad_down,
        plain[5],
    )


def solution(mesh):
    tokens = P(None, "dp", "seq", None)
    matrix = P(AXES, None)
    vector = P(AXES)
    in_specs = (
        tokens, matrix, vector, matrix, vector, vector, vector, vector, vector, matrix, vector,
        matrix, vector, tokens,
    )
    out_specs = (
        tokens, tokens, matrix, vector, matrix, vector, vector, vector, vector, vector, matrix,
        vector, matrix, vector,
    )
    return jax.shard_map(body, mesh=mesh, in_specs=in_specs, out_specs=out_specs, check_vma=False)
```

```python
from functools import partial

import jax
import jax.numpy as jnp
import numpy as np
from jax import lax
from jax.experimental import pallas as pl
from jax.experimental.pallas import tpu as pltpu
from jax.sharding import PartitionSpec as P

HEADS = 8
AXES = ("dp", "seq")
F32 = jnp.float32
BF16 = jnp.bfloat16
GROUPS = 32
SMALL = 16
EPS = 1e-05
MIB = 1024 * 1024


def dot(left, right):
    return jnp.dot(left, right, preferred_element_type=F32)


def dot_right(left, right):
    return lax.dot_general(left, right, (((1,), (1,)), ((), ())), preferred_element_type=F32)


def dot_left(left, right):
    return lax.dot_general(left, right, (((0,), (0,)), ((), ())), preferred_element_type=F32)


def unit_of(values):
    centred = values - jnp.mean(values, axis=-1, keepdims=True)
    scale = lax.rsqrt(jnp.mean(centred * centred, axis=-1, keepdims=True) + EPS)
    return centred * scale, scale


def norm_back(grad, unit, scale, gain):
    scaled = grad * gain
    inner = (
        scaled
        - jnp.mean(scaled, axis=-1, keepdims=True)
        - unit * jnp.mean(scaled * unit, axis=-1, keepdims=True)
    )
    return inner * scale


def column_sum(values):
    return jnp.sum(values, axis=0, keepdims=True)


def expand_small(small, width, chunk):
    eye = lax.broadcasted_iota(jnp.int32, (128, width), 0) == (
        lax.broadcasted_iota(jnp.int32, (128, width), 1) % chunk
    )
    spread = dot(small, eye.astype(F32).astype(BF16))
    runs = GROUPS * chunk // width
    per_run = GROUPS // runs
    group = lax.broadcasted_iota(jnp.int32, (GROUPS * SMALL, width), 0) // SMALL
    column = lax.broadcasted_iota(jnp.int32, (GROUPS * SMALL, width), 1) // chunk
    kept = jnp.where(group % per_run == column, spread, 0.0).reshape(GROUPS, SMALL, width)
    return [jnp.sum(kept[run * per_run : (run + 1) * per_run], axis=0) for run in range(runs)]


def shrink_vectors(vectors, parts):
    width = vectors.shape[1]
    tiled = jnp.broadcast_to(vectors[None], (GROUPS, SMALL, width)).reshape(-1, width)
    row = lax.broadcasted_iota(jnp.int32, (GROUPS * SMALL, width), 0)
    lane = lax.broadcasted_iota(jnp.int32, (GROUPS * SMALL, width), 1)
    group = row // SMALL
    row = row % SMALL
    total = None
    for chunk, first, end in parts:
        runs = GROUPS * chunk // width
        per_run = GROUPS // runs
        keep = (group % per_run == lane // chunk) & (row >= first) & (row < end)
        if runs > 1:
            keep = keep & (row - first == group // per_run)
        eye = lax.broadcasted_iota(jnp.int32, (width, 128), 0) % chunk == lax.broadcasted_iota(
            jnp.int32, (width, 128), 1
        )
        part = dot(jnp.where(keep, tiled, 0.0).astype(BF16), eye.astype(F32).astype(BF16))
        total = part if total is None else total + part
    return total


def same_core(table_ref):
    return table_ref[0, GROUPS] == 0


def take_groups(first_ref, second_ref, table_ref, target_ref):
    even = same_core(table_ref)
    for pair in range(GROUPS // 2):
        mine = first_ref[table_ref[0, pair]]
        other = second_ref[table_ref[0, GROUPS // 2 + pair]]
        target_ref[2 * pair] = jnp.where(even, mine, other)
        target_ref[2 * pair + 1] = jnp.where(even, other, mine)


def give_groups(values, first_ref, second_ref, table_ref, tile, first_pair=0):
    even = same_core(table_ref)
    for i in range(values.shape[0] // 2):
        pair = first_pair + i
        one, two = values[2 * i], values[2 * i + 1]
        first_ref[table_ref[0, pair], tile] = jnp.where(even, one, two)
        second_ref[table_ref[0, GROUPS // 2 + pair], tile] = jnp.where(even, two, one)


def give_lanes(values, first_ref, second_ref, table_ref, at, first_pair=0):
    for tile in range(values.shape[1] // 128):
        part = values[:, tile * 128 : tile * 128 + 128].astype(BF16).reshape(-1, 16, 128)
        give_groups(part, first_ref, second_ref, table_ref, at + tile, first_pair)


def pair_average(rows):
    out = np.zeros((rows // 2, rows), np.float32)
    for i in range(rows // 2):
        out[i, 2 * i] = out[i, 2 * i + 1] = 0.5
    return out


def average(rows, factor):
    out = np.zeros((rows // factor, rows), np.float32)
    for i in range(rows // factor):
        out[i, i * factor : (i + 1) * factor] = 1.0 / factor
    return out


def attention_constants(piece, far_levels, local_top):
    top = local_top + far_levels - 1
    averaged = []
    for level in range(1, top + 1):
        averaged.append(np.repeat(average(piece, 2**level), 2**level, axis=0))
    coarse = np.concatenate([average(piece, 2**level) for level in range(1, local_top)], axis=0)
    tokens = np.arange(piece)
    masks = []
    sizes = []
    for level in range(local_top):
        keys = np.arange(piece >> level)
        block = (tokens >> level)[:, None] // 16
        if level == 0:
            mask = (block // 2) == (keys[None, :] // 32)
        else:
            mask = (block ^ 1) == (keys[None, :] // 16)
        masks += [mask, mask]
        sizes.append(piece >> level)
    for _ in range(far_levels):
        masks += [np.ones((piece, 16), bool)] * 2
        sizes.append(16)
    ones = []
    for level, size in enumerate(sizes):
        head_a = np.zeros((size, 128), np.float32)
        head_a[:, :64] = 2.0**level
        head_b = np.zeros((size, 128), np.float32)
        head_b[:, 64:] = 2.0**level
        ones += [head_a, head_b]
    return dict(
        averaged=np.concatenate(averaged, axis=0),
        averaged_wide=np.concatenate(averaged, axis=1),
        coarse=coarse,
        coarse_t=coarse.T.copy(),
        mask=np.concatenate(masks, axis=1).astype(np.float32),
        ones=np.concatenate(ones, axis=0),
        sizes=tuple(sizes),
    )


def far_constants(seqs):
    out = np.zeros((seqs * 16, seqs * (8 + 16 + 8 + 8)), np.float32)
    starts = (0, seqs * 8, seqs * 24, seqs * 32)
    for seq in range(seqs):
        for slot in range(4):
            for i in range(4):
                row = seq * 16 + slot * 4 + i
                if slot == 1:
                    at = starts[1] + seq * 16 + 4 * i
                    out[row, at : at + 4] = 0.25
                else:
                    at = starts[slot] + seq * 8 + 2 * i
                    out[row, at : at + 2] = 0.5
    return out


def lane_a(rows):
    return lax.broadcasted_iota(jnp.int32, (rows, 128), 1) < 64


def stacked(block, sizes):
    in_a = lane_a(block.shape[0])
    zero = jnp.zeros_like(block)
    head_a = jnp.where(in_a, block, zero)
    head_b = jnp.where(in_a, zero, block)
    parts = []
    at = 0
    for size in sizes:
        parts.append(head_a[at : at + size])
        parts.append(head_b[at : at + size])
        at += size
    return parts


def blocked(parts):
    levels = len(parts) // 2
    rows = []
    for level in range(2, levels):
        block = jnp.concatenate(parts[2 * level : 2 * level + 2], axis=0)
        zero = jnp.zeros_like(block)
        rows.append(
            jnp.concatenate(
                [block if other == level else zero for other in range(2, levels)], axis=1
            )
        )
    return jnp.concatenate(rows, axis=0)


def queries_of(plain_ref, averaged_ref, pair, levels):
    piece = plain_ref.shape[0]
    lanes = slice(pair * 128, pair * 128 + 128)
    rest = jnp.concatenate(
        [averaged_ref[(level - 1) * piece : level * piece, lanes] for level in range(2, levels)],
        axis=1,
    )
    return plain_ref[:, lanes], averaged_ref[0:piece, lanes], rest


def far_rows_of(refs):
    return jnp.concatenate([ref[...].astype(F32) for ref in refs], axis=0)


def pick_far(source_ref, seq, far_rows, seqs):
    parts = []
    at = 0
    for n in far_rows:
        parts.append(source_ref[pl.ds(pl.multiple_of(at + seq * n, n), n), :])
        at += seqs * n
    return jnp.concatenate(parts, axis=0)


def norm_kernel(x_ref, coarse_ref, pair_ref, base_ref, next_ref):
    unit, _ = unit_of(x_ref[...].astype(F32))
    base = dot(coarse_ref[...], unit.astype(BF16)).astype(BF16)
    base_ref[...] = base
    next_ref[...] = dot(pair_ref[...], base).astype(BF16)


def far_kernel(own_ref, one_ref, two_ref, three_ref, gather_ref, pair_ref, five_ref, six_ref):
    rows = far_rows_of((own_ref, one_ref, two_ref, three_ref)).astype(BF16)
    five = dot(gather_ref[...], rows).astype(BF16)
    five_ref[...] = five
    six_ref[...] = dot(pair_ref[...], five).astype(BF16)


def far_back_kernel(
    five_ref, six_a_ref, six_b_ref, one_ref, two_ref, three_ref, spread_ref, pair_ref,
    own_out, one_out, two_out, three_out,
):
    six = (six_a_ref[...].astype(F32) + six_b_ref[...].astype(F32)).astype(BF16)
    five = (five_ref[...].astype(F32) + dot(pair_ref[...], six)).astype(BF16)
    rows = dot(spread_ref[...], five)
    own = own_out.shape[0]
    one = own + one_ref.shape[0]
    two = one + two_ref.shape[0]
    own_out[...] = rows[:own]
    one_out[...] = (rows[own:one] + one_ref[...].astype(F32)).astype(BF16)
    two_out[...] = (rows[one:two] + two_ref[...].astype(F32)).astype(BF16)
    three_out[...] = (rows[two:] + three_ref[...].astype(F32)).astype(BF16)


def mix_kernel(*refs):
    x_ref, first_ref, second_ref, groups_ref = refs[:4]
    far_refs = refs[4:-7]
    vec_ref, q_ref, k_ref, v_ref, kf_ref, vf_ref, weight_ref = refs[-7:]
    width = x_ref.shape[1]
    take_groups(first_ref, second_ref, groups_ref, weight_ref)
    unit, _ = unit_of(x_ref[...].astype(F32))
    far = far_rows_of(far_refs)
    small = weight_ref[:, :, 3 * width :].reshape(GROUPS * SMALL, 128)
    plain = expand_small(small, width, width // GROUPS)[0]
    biases = expand_small(small, width, 2 * width // GROUPS)
    ups = expand_small(small, width, 4 * width // GROUPS)
    vec_ref[...] = jnp.concatenate(
        [plain[0:6], biases[0][6:7], biases[1][6:7]]
        + [up[7:8] for up in ups]
        + [jnp.zeros((4, width), F32)],
        axis=0,
    )
    gain, shift = plain[0:1], plain[1:2]
    query_bias, value_bias = biases[0][6:7], biases[1][6:7]
    normed = (unit * gain + shift).astype(BF16)
    far = (far * gain + shift).astype(BF16)
    weight = weight_ref[:, :, 0:width].reshape(width, width)
    queries = (dot(normed, weight) + query_bias).astype(BF16).astype(F32)
    q_ref[...] = (queries * 0.125).astype(BF16)
    weight = weight_ref[:, :, width : 2 * width].reshape(width, width)
    k_ref[...] = dot(normed, weight).astype(BF16)
    kf_ref[...] = dot(far, weight)
    weight = weight_ref[:, :, 2 * width : 3 * width].reshape(width, width)
    v_ref[...] = (dot(normed, weight) + value_bias).astype(BF16)
    vf_ref[...] = dot(far, weight) + value_bias


def attention_kernel(
    q_ref, k_ref, v_ref, kf_ref, vf_ref, averaged_ref, coarse_ref, mask_ref, ones_ref,
    kall_ref, vall_ref, p_ref, att_ref, rden_ref,
    qe_ref,
    *, far_rows, sizes, local_top,
):
    piece, width = q_ref.shape
    levels = len(sizes)
    seq = pl.program_id(0)
    count = kf_ref.shape[0] // sum(far_rows)
    queries = q_ref[...]
    qe_ref[...] = dot(averaged_ref[...], queries).astype(BF16)
    keys = k_ref[...]
    values = v_ref[...]
    coarse_keys = dot(coarse_ref[...], keys).astype(BF16)
    coarse_values = dot(coarse_ref[...], values)
    scaled = [values]
    at = 0
    for level in range(1, local_top):
        scaled.append((coarse_values[at : at + sizes[level]] * 2.0**level).astype(BF16))
        at += sizes[level]
    far_values = pick_far(vf_ref, seq, far_rows, count)
    for level in range(local_top, levels):
        at = 16 * (level - local_top)
        scaled.append((far_values[at : at + 16] * 2.0**level).astype(BF16))
    kall_ref[0] = jnp.concatenate(
        [keys, coarse_keys, pick_far(kf_ref, seq, far_rows, count).astype(BF16)], axis=0
    )
    vall_ref[0] = jnp.concatenate(scaled, axis=0)
    for pair in range(width // 128):
        lanes = slice(pair * 128, pair * 128 + 128)
        plain, one, rest = queries_of(q_ref, qe_ref, pair, levels)
        key_parts = stacked(kall_ref[0, :, lanes], sizes)
        scores = jnp.concatenate(
            [
                dot_right(plain, jnp.concatenate(key_parts[0:2], axis=0)),
                dot_right(one, jnp.concatenate(key_parts[2:4], axis=0)),
                dot_right(rest, blocked(key_parts)),
            ],
            axis=1,
        )
        weights = jnp.where(mask_ref[...] > 0.0, jnp.exp(scores), 0.0).astype(BF16)
        p_ref[0, pair] = weights
        both = jnp.concatenate(
            [jnp.concatenate(stacked(vall_ref[0, :, lanes], sizes), axis=0), ones_ref[...]], axis=1
        )
        sums = dot(weights, both)
        rden = 1.0 / sums[:, 128:]
        rden_ref[:, lanes] = rden
        att_ref[:, lanes] = (sums[:, :128] * rden).astype(BF16)


def feed_kernel(
    vec_ref, table_ref, x_hbm, cot_hbm, att_hbm, low_hbm, first_hbm, second_hbm,
    out_ref, dmid_ref, datt_ref, sum_ref, first_out, second_out,
    x_ref, cot_ref, att_ref, low_ref, first_ref, second_ref, up_ref, sems,
):
    width = x_ref.shape[1]
    pairs = (
        (first_hbm, first_ref), (second_hbm, second_ref), (att_hbm, att_ref), (low_hbm, low_ref),
        (x_hbm, x_ref), (cot_hbm, cot_ref),
    )
    copies = [
        pltpu.make_async_copy(source, target, sems.at[i])
        for i, (source, target) in enumerate(pairs)
    ]
    for copy in copies:
        copy.start()
    blocks = up_ref.shape[2] // width
    copies[0].wait()
    copies[1].wait()
    take_groups(first_ref, second_ref, table_ref, up_ref)
    for copy in copies[2:]:
        copy.wait()
    gain = vec_ref[3:4, :]
    out_weight = low_ref[:, 0:16, :].reshape(width, width)
    middle = x_ref[...].astype(F32) + dot(att_ref[...], out_weight) + vec_ref[2:3, :]
    unit, inverse = unit_of(middle)
    normed = (unit * gain + vec_ref[4:5, :]).astype(BF16)
    g_out = cot_ref[...]
    result = middle + vec_ref[5:6, :]
    d_two = jnp.zeros(x_ref.shape, F32)
    tiles = width // 128
    per_group = (low_ref.shape[1] - 16) // 16
    groups = GROUPS // blocks
    sums = []
    for block in range(blocks):
        up = up_ref[:, :, width * block : width * (block + 1)].reshape(width, width)
        down = low_ref[groups * block : groups * (block + 1), 16:, :].reshape(width, width)
        pre = dot(normed, up) + vec_ref[8 + block : 9 + block, :]
        cdf = 0.5 + 0.5 * lax.erf(pre * 0.7071067811865476)
        hidden = (pre * cdf).astype(BF16)
        slope = cdf + pre * (0.3989422804014327 * jnp.exp(-0.5 * pre * pre))
        result = result + dot(hidden, down)
        grad = dot_left(hidden, g_out).reshape(groups, per_group, 16, width)
        for part in range(per_group):
            give_lanes(
                grad[:, part].reshape(-1, width), first_out, second_out, table_ref,
                tiles * (blocks + 1 + part), groups // 2 * block,
            )
        g_pre = (dot_right(g_out, down) * slope).astype(BF16)
        sums.append(column_sum(g_pre.astype(F32)))
        grad = dot_left(normed, g_pre)
        give_lanes(grad, first_out, second_out, table_ref, tiles * (block + 1))
        d_two = d_two + dot_right(g_pre, up)
    out_ref[...] = result.astype(BF16)
    cot = g_out.astype(F32)
    d_middle = cot + norm_back(d_two, unit, inverse, gain)
    dmid_ref[...] = d_middle
    branch = d_middle.astype(BF16)
    datt_ref[...] = dot_right(branch, out_weight)
    give_lanes(dot_left(att_ref[...], branch), first_out, second_out, table_ref, 0)
    sum_ref[...] = jnp.concatenate(
        [
            jnp.zeros((2, width), F32),
            column_sum(branch.astype(F32)),
            column_sum(d_two * unit),
            column_sum(d_two),
            column_sum(cot),
            jnp.zeros((2, width), F32),
        ]
        + sums
        + [jnp.zeros((8 - blocks, width), F32)],
        axis=0,
    )


def attention_back_kernel(*refs, far_rows, sizes, local_top):
    fars = len(far_rows)
    q_ref, kall_ref, vall_ref, p_ref, att_ref, rden_ref, datt_ref = refs[:7]
    x_ref, vec_ref, sum_ref, first_in, second_in, groups_ref = refs[7:13]
    averaged_ref, wide_ref, coarse_t_ref, ones_ref = refs[13:17]
    far_refs = refs[17 : 17 + fars]
    scaled_ref, first_ref, second_ref = refs[17 + fars : 20 + fars]
    dfar_refs = refs[20 + fars : 20 + 2 * fars]
    (
        weight_ref, dq_ref, dk_ref, dv_ref, dkf_ref, dvf_ref, qe_ref, dkall_ref, dvall_ref, t_ref,
        dqacc_ref,
    ) = refs[20 + 2 * fars :]
    width = x_ref.shape[1]
    piece = q_ref.shape[0]
    seqs = x_ref.shape[0] // piece
    levels = len(sizes)
    starts = np.concatenate([[0], np.cumsum(sizes)]).tolist()
    local = starts[local_top]
    seq = pl.program_id(0)

    qe_ref[...] = dot(averaged_ref[...], q_ref[...]).astype(BF16)
    near = 2 * sizes[0]
    mid = near + 2 * sizes[1]
    for pair in range(width // 128):
        lanes = slice(pair * 128, pair * 128 + 128)
        plain, one, rest = queries_of(q_ref, qe_ref, pair, levels)
        key_parts = stacked(kall_ref[0, :, lanes], sizes)
        both = jnp.concatenate(
            [jnp.concatenate(stacked(vall_ref[0, :, lanes], sizes), axis=0), ones_ref[...]], axis=1
        )
        d_num = datt_ref[:, lanes] * rden_ref[:, lanes]
        d_den = -d_num * att_ref[:, lanes].astype(F32)
        d_num = d_num.astype(BF16)
        weights = p_ref[0, pair]
        d_weights = dot_right(jnp.concatenate([d_num, d_den.astype(BF16)], axis=1), both)
        d_scores = (weights.astype(F32) * d_weights).astype(BF16)
        d_key_near = dot_left(d_scores[:, :near], plain)
        d_key_mid = dot_left(d_scores[:, near:mid], one)
        d_key_rest = dot_left(d_scores[:, mid:], rest)
        d_value = dot_left(weights, d_num)
        dqacc_ref[:, lanes] = dot(d_scores[:, :near], jnp.concatenate(key_parts[0:2], axis=0))
        t_ref[0:piece, lanes] = dot(
            d_scores[:, near:mid], jnp.concatenate(key_parts[2:4], axis=0)
        ).astype(BF16)
        d_rest = dot(d_scores[:, mid:], blocked(key_parts)).astype(BF16)
        at = 0
        for level in range(levels):
            size = sizes[level]
            low, high = starts[level], starts[level + 1]
            in_a = lane_a(size)
            if level == 0:
                source = d_key_near
            elif level == 1:
                source = d_key_mid
            else:
                block = slice((level - 2) * 128, (level - 1) * 128)
                source = d_key_rest[at - mid : at - mid + 2 * size, block]
                t_ref[(level - 1) * piece : level * piece, lanes] = d_rest[:, block]
            dkall_ref[low:high, lanes] = jnp.where(in_a, source[:size], source[size:])
            values = d_value[at : at + 2 * size]
            dvall_ref[low:high, lanes] = jnp.where(in_a, values[:size], values[size:]) * 2.0**level
            at += 2 * size
    rows = pl.ds(pl.multiple_of(seq * piece, piece), piece)
    dq_ref[rows, :] = ((dqacc_ref[...] + dot(wide_ref[...], t_ref[...])) * 0.125).astype(BF16)
    for target, source in ((dk_ref, dkall_ref), (dv_ref, dvall_ref)):
        spread = dot(coarse_t_ref[...], source[piece:local, :].astype(BF16))
        target[rows, :] = (source[0:piece, :] + spread).astype(BF16)
    at = 0
    low = local
    for n in far_rows:
        target = pl.ds(pl.multiple_of(at + seq * n, n), n)
        dkf_ref[target, :] = dkall_ref[low : low + n, :]
        dvf_ref[target, :] = dvall_ref[low : low + n, :]
        at += seqs * n
        low += n

    @pl.when(seq == seqs - 1)
    def _():
        take_groups(first_in, second_in, groups_ref, weight_ref)
        gain = vec_ref[0:1, :]
        shift = vec_ref[1:2, :]
        unit, _ = unit_of(x_ref[...].astype(F32))
        normed = (unit * gain + shift).astype(BF16)
        far = far_rows_of(far_refs)
        far_normed = (far * gain + shift).astype(BF16)
        both = jnp.concatenate([normed, far_normed], axis=0)
        far_grads = (None, dkf_ref[...].astype(BF16), dvf_ref[...].astype(BF16))
        grads = (dq_ref[...], dk_ref[...], dv_ref[...])
        d_one = jnp.zeros(x_ref.shape, F32)
        d_far = jnp.zeros(far.shape, F32)
        for part in range(3):
            lanes = slice(part * width, part * width + width)
            weight = weight_ref[:, :, lanes].reshape(width, width)
            d_one = d_one + dot_right(grads[part], weight)
            if part == 0:
                grad = dot_left(normed, grads[part])
            else:
                d_far = d_far + dot_right(far_grads[part], weight)
                grad = dot_left(both, jnp.concatenate([grads[part], far_grads[part]], axis=0))
            give_lanes(grad, first_ref, second_ref, groups_ref, part * width // 128)
        scaled_ref[...] = d_one * gain
        at = 0
        for ref in dfar_refs:
            ref[...] = (d_far[at : at + ref.shape[0]] * gain).astype(BF16)
            at += ref.shape[0]
        vectors = jnp.concatenate(
            [
                column_sum(d_one * unit) + column_sum(d_far * far),
                column_sum(d_one) + column_sum(d_far),
                sum_ref[2:6, :],
                column_sum(grads[0].astype(F32)),
                column_sum(grads[2].astype(F32)) + column_sum(dvf_ref[...]),
                sum_ref[8:16, :],
            ],
            axis=0,
        )
        chunk = width // GROUPS
        small = shrink_vectors(vectors, ((chunk, 0, 6), (2 * chunk, 6, 8), (4 * chunk, 8, 12)))
        give_lanes(small, first_ref, second_ref, groups_ref, 3 * width // 128)


def input_kernel(
    x_ref, dmid_ref, scaled_ref, own_ref, one_ref, two_ref, three_ref, pair_ref, spread_ref,
    din_ref,
):
    unit, inverse = unit_of(x_ref[...].astype(F32))
    lower = own_ref[...] + two_ref[...].astype(F32) + three_ref[...].astype(F32)
    base = one_ref[...].astype(F32) + dot(pair_ref[...], lower.astype(BF16))
    scaled = scaled_ref[...] + dot(spread_ref[...], base.astype(BF16))
    inner = (
        scaled
        - jnp.mean(scaled, axis=-1, keepdims=True)
        - unit * jnp.mean(scaled * unit, axis=-1, keepdims=True)
    )
    din_ref[...] = dmid_ref[...] + inner * inverse


def last_kernel(
    mix_ref, other_mix_ref, feed_ref, other_feed_ref,
    matrix_ref, out_ref, up_ref, down_ref, *vector_refs,
):
    total = feed_ref[0].astype(F32) + other_feed_ref[0].astype(F32)
    at = 0
    for ref in (out_ref, up_ref):
        for lane in range(0, ref.shape[1], 128):
            ref[:, lane : lane + 128] = total[at]
            at += 1
    for row in range(0, down_ref.shape[0], 16):
        for lane in range(0, down_ref.shape[1], 128):
            down_ref[row : row + 16, lane : lane + 128] = total[at]
            at += 1
    total = mix_ref[0].astype(F32) + other_mix_ref[0].astype(F32)
    for lane in range(0, matrix_ref.shape[1], 128):
        matrix_ref[:, lane : lane + 128] = total[lane // 128]
    small = total[matrix_ref.shape[1] // 128]
    for i in range(6):
        vector_refs[i][...] = small[i : i + 1, : vector_refs[i].shape[1]]
    vector_refs[6][...] = column_sum(small[6:8])[:, : vector_refs[6].shape[1]]
    vector_refs[7][...] = column_sum(small[8:12])[:, : vector_refs[7].shape[1]]


def vmem():
    return pl.BlockSpec(memory_space=pltpu.VMEM)


def anywhere():
    return pl.BlockSpec(memory_space=pl.ANY)


def scalars():
    return pl.BlockSpec(memory_space=pltpu.SMEM)


def fixed(*dims):
    return pl.BlockSpec(dims, lambda i: (0,) * len(dims))


def moving(*dims):
    return pl.BlockSpec(dims, lambda i: (i,) + (0,) * (len(dims) - 1))


def shape(dims, dtype):
    return jax.ShapeDtypeStruct(dims, dtype)


def const(values):
    return jnp.asarray(values, BF16)


def bit_orders():
    return ((8, 4, 16, 2), (2, 8, 4, 16))


def slot_offset(slot, order):
    return sum(bit for k, bit in enumerate(order) if slot >> k & 1)


def group_table(orders):
    table = np.zeros((32, 128), np.int32)
    for device in range(32):
        core = device & 1
        table[device, GROUPS] = core
        for slot in range(16):
            table[device, (device ^ slot_offset(slot, orders[core])) // 2] = slot
            group = device ^ 1 ^ slot_offset(slot, orders[1 - core])
            table[device, GROUPS // 2 + group // 2] = slot
    return table


def exchange(value, bits):
    if isinstance(bits, int):
        bits = (bits, bits)
    count = lax.axis_size(AXES)
    return lax.ppermute(value, AXES, [(i, i ^ bits[i & 1]) for i in range(count)])


def after(value, *others):
    return lax.optimization_barrier((value,) + others)[0]


def send(buffer, k):
    orders = bit_orders()
    return exchange(buffer, (orders[0][k], orders[1][k]))


def added(left, right):
    return (left.astype(F32) + right.astype(F32)).astype(BF16)


def halves(kept, other):
    half = kept.shape[0] // 2
    return added(kept[:half], other[:half]), added(kept[half:], other[half:])


def joined(buffer, other):
    return jnp.concatenate([buffer, other], axis=0)


def call(kernel, name, outs, ins, args, work, scratch=(), grid=None, room=6):
    return pl.pallas_call(
        kernel,
        out_shape=tuple(item[0] for item in outs),
        in_specs=list(ins),
        out_specs=tuple(item[1] for item in outs),
        scratch_shapes=list(scratch),
        compiler_params=pltpu.CompilerParams(vmem_limit_bytes=room * MIB),
        cost_estimate=pl.CostEstimate(flops=work, bytes_accessed=work >> 9, transcendentals=0),
        name=name,
        **({} if grid is None else {"grid": grid}),
    )(*args)


def coarsen(values):
    return (values[:, 0::2] + values[:, 1::2]) * 0.5


def whole_far(base, seqs, far_levels, position):
    rows = base.reshape(seqs, 16, base.shape[1])
    full = lax.all_gather(rows, "seq", axis=1, tiled=True).astype(F32)
    parts = []
    for extra in range(far_levels):
        partner = (position // 2**extra) ^ 1
        parts.append(lax.dynamic_slice_in_dim(full, partner * 16, 16, axis=1))
        if extra + 1 < far_levels:
            full = coarsen(full)
    return jnp.concatenate(parts, axis=1).astype(BF16).reshape(seqs * 16 * far_levels, -1)


def whole_far_back(grad, seqs, far_levels, position):
    stack = grad.reshape(seqs, far_levels, 16, -1).astype(F32)
    ids = jnp.arange(far_levels).reshape(1, far_levels, 1, 1)
    count = lax.axis_size("seq")
    for bit in range(far_levels):
        pairs = [(i, i ^ 1 << bit) for i in range(count)]
        other = lax.ppermute(stack.astype(BF16), "seq", pairs).astype(F32)
        stack = jnp.where(ids > bit, stack + other, jnp.where(ids == bit, other, stack))
    own = jnp.zeros((seqs, 16, stack.shape[-1]), F32)
    for extra in range(far_levels):
        rows = 16 >> extra
        offset = position % 2**extra * rows
        part = lax.dynamic_slice_in_dim(stack[:, extra], offset, rows, axis=1)
        own = own + jnp.repeat(part, 2**extra, axis=1) * 0.5**extra
    return own.reshape(seqs * 16, -1).astype(BF16)


def body(
    layer_input, qkv_weight, qv_bias, out_weight, out_bias, first_gain, first_shift, second_gain,
    second_shift, up_weight, up_bias, down_weight, down_bias, cotangent,
):
    batches, per_batch, piece, width = layer_input.shape
    seqs = batches * per_batch
    tokens = seqs * piece
    hidden = up_weight.shape[1]
    blocks = hidden // width
    devices = lax.axis_size(AXES)
    pieces = lax.axis_size("seq")
    position = lax.axis_index("seq")
    far_levels = pieces.bit_length() - 1
    local_top = (piece // 16).bit_length() - 1
    fast = devices == GROUPS and pieces == 16
    x = layer_input.reshape(tokens, width)
    cot = cotangent.reshape(tokens, width)
    consts = attention_constants(piece, far_levels, local_top)
    sizes = consts["sizes"]
    keys = sum(sizes)
    flat = (tokens, width)
    base_rows = seqs * 16
    coarse_all = np.kron(np.eye(seqs, dtype=np.float32), average(piece, piece // 16))
    pair = np.kron(np.eye(seqs, dtype=np.float32), pair_average(16))
    gather_far = far_constants(seqs)
    vectors = (
        first_gain, first_shift, out_bias, second_gain, second_shift, down_bias, qv_bias, up_bias,
    )

    lows = jnp.concatenate([out_weight, down_weight])
    if fast:
        lows = lax.all_gather(lows, AXES, axis=0)
    base, below = call(
        norm_kernel,
        "norm",
        [(shape((base_rows, width), BF16), vmem()), (shape((base_rows // 2, width), BF16), vmem())],
        [vmem()] * 3,
        (x, const(coarse_all), const(pair)),
        1 << 20,
    )

    if fast:
        me = lax.axis_index(AXES)
        table = jnp.asarray(group_table(bit_orders()))
        groups = lax.dynamic_slice_in_dim(table, me, 1, axis=0)
        a = jnp.pad(qkv_weight, ((0, 0), (0, 128)))
        for row, vector in enumerate(vectors):
            item = vector.reshape(1, -1)
            lanes = (3 * width, 128 - item.shape[1])
            a = a + jnp.pad(item, ((row, SMALL - 1 - row), lanes))
        a = a[None]
        a = joined(a, send(a, 0))
        a = joined(a, send(after(a, base), 1))
        near, half = after(base, a), after(below, a)
        one, two, three = exchange(near, 1), exchange(half, 2), exchange(half, 3)
        b = after(up_weight[None], a)
        other_b = send(b, 0)
        a = joined(a, send(a, 2))
        a = after(a, one, two, three)
        five, six = call(
            far_kernel,
            "far",
            [
                (shape((base_rows, width), BF16), vmem()),
                (shape((base_rows // 2, width), BF16), vmem()),
            ],
            [vmem()] * 6,
            (after(below, a), one, two, three, const(gather_far), const(pair)),
            1 << 20,
        )
        far = (one, two, three, exchange(five, 4), exchange(six, 8), exchange(six, 12))
        far_rows = (16, 8, 8, 16, 8, 8)
        b = joined(after(b, a), other_b)
        other_b = send(b, 1)
        a = joined(a, send(a, 3))
        a = after(a, five, six)
        first_a, second_a = a, exchange(a, 1)
        b = joined(after(b, a), other_b)
        other_b = send(b, 2)
    else:
        groups = [slot % (GROUPS // 2) for slot in range(GROUPS)] + [0] * (128 - GROUPS)
        groups = jnp.asarray([groups], jnp.int32)

        def whole(value):
            return lax.all_gather(value, AXES, axis=0, tiled=True).reshape(
                (GROUPS, -1) + value.shape[1:]
            )

        small = [jnp.pad(v, ((0, 0), (0, 128 - v.shape[1]))) for v in map(whole, vectors)]
        small += [jnp.zeros((GROUPS, 128), BF16)] * (SMALL - len(small))
        gathered_a = jnp.concatenate([whole(qkv_weight), jnp.stack(small, axis=1)], axis=2)
        gathered_b = whole(up_weight)
        lows = jnp.concatenate([whole(out_weight), whole(down_weight)], axis=1)
        first_a, second_a = gathered_a[0::2], gathered_a[1::2]
        first_b, second_b = gathered_b[0::2], gathered_b[1::2]
        far = (whole_far(base, seqs, far_levels, position),)
        far_rows = (16 * far_levels,)

    lanes_a = 3 * width + 128
    tiles_a = lanes_a // 128
    tiles_b = (width + 2 * hidden) // 128
    top = len(sizes) - 1
    pairs = width // 128
    total_far = seqs * 16 * far_levels
    half_a = shape((GROUPS // 2, tiles_a, 16, 128), BF16)
    half_b = shape((GROUPS // 2, tiles_b, 16, 128), BF16)
    far_flat = shape((total_far, width), F32)
    low, high = shape(flat, BF16), shape(flat, F32)
    sixteen = shape((16, width), F32)
    level = dict(far_rows=far_rows, sizes=sizes, local_top=local_top)

    vec, queries, key, value, far_key, far_value = call(
        mix_kernel,
        "mix",
        [(sixteen, vmem())] + [(low, vmem())] * 3 + [(far_flat, vmem())] * 2,
        [vmem(), vmem(), vmem(), scalars()] + [vmem()] * len(far),
        (x, first_a, second_a, groups, *far),
        1 << 24,
        [pltpu.VMEM((GROUPS, 16, lanes_a), BF16)],
        room=14,
    )
    if fast:
        b = joined(after(b, queries), other_b)
        queries = after(queries, b)
        other_b = send(b, 3)
    rows_spec = moving(piece, width)
    keys_spec = moving(1, keys, width)
    p_spec = moving(1, pairs, piece, 2 * keys)
    keys_shape = shape((seqs, keys, width), BF16)
    kall, vall, weights, attended, rden = call(
        partial(attention_kernel, **level),
        "attention",
        [
            (keys_shape, keys_spec),
            (keys_shape, keys_spec),
            (shape((seqs, pairs, piece, 2 * keys), BF16), p_spec),
            (low, rows_spec),
            (high, rows_spec),
        ],
        [rows_spec] * 3
        + [fixed(total_far, width)] * 2
        + [
            fixed(top * piece, piece),
            fixed(*consts["coarse"].shape),
            fixed(piece, 2 * keys),
            fixed(2 * keys, 128),
        ],
        (
            queries, key, value, far_key, far_value, const(consts["averaged"]),
            const(consts["coarse"]), jnp.asarray(consts["mask"]), const(consts["ones"]),
        ),
        1 << 24,
        [pltpu.VMEM((top * piece, width), BF16)],
        (seqs,),
        room=12,
    )
    if fast:
        b = joined(after(b, attended), other_b)
        first_b, second_b = b, exchange(b, 1)

    result, d_middle, d_attended, sums, kept_b, sent_b = call(
        feed_kernel,
        "feed",
        [(low, vmem()), (high, vmem()), (high, vmem()), (sixteen, vmem())] + [(half_b, vmem())] * 2,
        [vmem(), scalars()] + [pl.BlockSpec(memory_space=pltpu.HBM)] * 6,
        (vec, groups, x, cot, attended, lows, first_b, second_b),
        8 << 30,
        [
            pltpu.VMEM(flat, BF16),
            pltpu.VMEM(flat, BF16),
            pltpu.VMEM(flat, BF16),
            pltpu.VMEM(lows.shape, BF16),
            pltpu.VMEM(first_b.shape, BF16),
            pltpu.VMEM(first_b.shape, BF16),
            pltpu.VMEM((GROUPS, 16, hidden), BF16),
            pltpu.SemaphoreType.DMA((6,)),
        ],
        room=34,
    )
    if fast:
        kept_b, upper = halves(kept_b, exchange(sent_b, 1))
        other_b = send(upper, 3)
        d_attended = after(d_attended, upper)
    outs = call(
        partial(attention_back_kernel, **level),
        "attention_back",
        [(high, fixed(*flat))] + [(half_a, fixed(*half_a.shape))] * 2
        + [(shape(item.shape, BF16), fixed(*item.shape)) for item in far],
        [rows_spec, keys_spec, keys_spec, p_spec, rows_spec, rows_spec, rows_spec]
        + [fixed(*flat), fixed(16, width), fixed(16, width)]
        + [fixed(*first_a.shape), fixed(*first_a.shape), scalars()]
        + [
            fixed(top * piece, piece),
            fixed(piece, top * piece),
            fixed(*consts["coarse_t"].shape),
            fixed(2 * keys, 128),
        ]
        + [fixed(*item.shape) for item in far],
        (
            queries, kall, vall, weights, attended, rden, d_attended, x, vec, sums, first_a,
            second_a, groups, const(consts["averaged"]),
            const(consts["averaged_wide"]), const(consts["coarse_t"]), const(consts["ones"]), *far,
        ),
        6 << 30,
        [
            pltpu.VMEM((GROUPS, 16, lanes_a), BF16),
            pltpu.VMEM(flat, BF16),
            pltpu.VMEM(flat, BF16),
            pltpu.VMEM(flat, BF16),
            pltpu.VMEM((total_far, width), F32),
            pltpu.VMEM((total_far, width), F32),
            pltpu.VMEM((top * piece, width), BF16),
            pltpu.VMEM((keys, width), F32),
            pltpu.VMEM((keys, width), F32),
            pltpu.VMEM((top * piece, width), BF16),
            pltpu.VMEM((piece, width), F32),
        ],
        (seqs,),
        room=28,
    )
    scaled, kept_a, sent_a = outs[:3]
    d_far = outs[3:]

    if fast:
        other_a = exchange(sent_a, 1)
        kept_b, upper = halves(after(kept_b, scaled), other_b)
        other_b = send(upper, 2)
        back = [exchange(item, bits) for item, bits in zip(d_far[3:], (4, 8, 12))]
        other_a, other_b, *back = lax.optimization_barrier((other_a, other_b, *back))
        own, out_one, out_two, out_three = call(
            far_back_kernel,
            "far_back",
            [
                (shape((base_rows // 2, width), F32), vmem()),
                (shape((base_rows, width), BF16), vmem()),
                (shape((base_rows // 2, width), BF16), vmem()),
                (shape((base_rows // 2, width), BF16), vmem()),
            ],
            [vmem()] * 8,
            (*back, d_far[0], d_far[1], d_far[2], const(gather_far.T), const(pair.T)),
            1 << 20,
        )

        kept_a, upper = halves(kept_a, other_a)
        other_a = send(upper, 3)
        kept_b, upper = halves(kept_b, other_b)
        other_b = send(upper, 1)
        back_one = exchange(out_one, 1)
        back_two = exchange(out_two, 2)
        back_three = exchange(out_three, 3)
        other_a, other_b, back_one, back_two, back_three = lax.optimization_barrier(
            (other_a, other_b, back_one, back_two, back_three)
        )
        kept_a, upper = halves(kept_a, other_a)
        other_a = send(upper, 2)
        kept_b, upper = halves(kept_b, other_b)
        other_b = send(upper, 0)
    else:
        back_one = whole_far_back(d_far[0], seqs, far_levels, position)
        own = jnp.zeros((base_rows // 2, width), F32)
        back_two = back_three = jnp.zeros((base_rows // 2, width), BF16)

    (d_input,) = call(
        input_kernel,
        "input_grad",
        [(high, vmem())],
        [vmem()] * 9,
        (
            x, d_middle, scaled, own, back_one, back_two, back_three, const(pair.T),
            const(coarse_all.T),
        ),
        1 << 20,
    )

    if fast:
        other_a, other_b, d_input = lax.optimization_barrier((other_a, other_b, d_input))
        for k in (1, 0):
            kept_a, upper = halves(kept_a, other_a)
            other_a = send(upper, k)
        grad_qkv, grad_out_weight, grad_up, grad_down, *plain = call(
            last_kernel,
            "last",
            [
                (shape(item.shape, F32), vmem())
                for item in (qkv_weight, out_weight, up_weight, down_weight)
            ]
            + [(shape((1, v.shape[0]), F32), vmem()) for v in vectors],
            [vmem()] * 4,
            (kept_a, other_a, kept_b, other_b),
            1 << 16,
        )
        plain = [item.reshape(-1) for item in plain]
        grad_qv, grad_up_bias = plain[6:8]
    else:

        def reduced(item):
            return lax.psum_scatter(item.astype(F32), AXES, scatter_dimension=0, tiled=True)

        def rows_of(item):
            return reduced(item.transpose(0, 2, 1, 3).reshape(GROUPS * 16, -1))

        all_a = jnp.stack([kept_a, sent_a], axis=1).reshape(GROUPS, *half_a.shape[1:])
        all_b = jnp.stack([kept_b, sent_b], axis=1).reshape(GROUPS, *half_b.shape[1:])
        grad_qkv = rows_of(all_a[:, :-1])
        small = all_a[:, -1]
        chunk = width // GROUPS
        plain = [reduced(small[:, i, :chunk].reshape(-1)) for i in range(6)]
        grad_qv = reduced(jnp.sum(small[:, 6:8, : 2 * chunk], axis=1).reshape(-1))
        grad_up_bias = reduced(jnp.sum(small[:, 8:12, : 4 * chunk], axis=1).reshape(-1))
        split = width // 128
        grad_out_weight = rows_of(all_b[:, :split])
        grad_up = rows_of(all_b[:, split : split * (blocks + 1)])
        downs = all_b[:, split * (blocks + 1) :].reshape(GROUPS, -1, split, 16, 128)
        grad_down = reduced(downs.transpose(0, 1, 3, 2, 4).reshape(hidden, width))

    return (
        result.reshape(layer_input.shape),
        d_input.reshape(layer_input.shape),
        grad_qkv,
        grad_qv,
        grad_out_weight,
        plain[2],
        plain[0],
        plain[1],
        plain[3],
        plain[4],
        grad_up,
        grad_up_bias,
        grad_down,
        plain[5],
    )


def solution(mesh):
    tokens = P(None, "dp", "seq", None)
    matrix = P(AXES, None)
    vector = P(AXES)
    in_specs = (
        tokens, matrix, vector, matrix, vector, vector, vector, vector, vector, matrix, vector,
        matrix, vector, tokens,
    )
    out_specs = (
        tokens, tokens, matrix, vector, matrix, vector, vector, vector, vector, vector, matrix,
        vector, matrix, vector,
    )
    return jax.shard_map(body, mesh=mesh, in_specs=in_specs, out_specs=out_specs, check_vma=False)
```

```python
from functools import partial

import jax
import jax.numpy as jnp
import numpy as np
from jax import lax
from jax.experimental import pallas as pl
from jax.experimental.pallas import tpu as pltpu
from jax.sharding import PartitionSpec as P

HEADS = 8
AXES = ("dp", "seq")
F32 = jnp.float32
BF16 = jnp.bfloat16
GROUPS = 32
SMALL = 16
EPS = 1e-05
MIB = 1024 * 1024


def dot(left, right):
    return jnp.dot(left, right, preferred_element_type=F32)


def dot_right(left, right):
    return lax.dot_general(left, right, (((1,), (1,)), ((), ())), preferred_element_type=F32)


def dot_left(left, right):
    return lax.dot_general(left, right, (((0,), (0,)), ((), ())), preferred_element_type=F32)


def unit_of(values):
    centred = values - jnp.mean(values, axis=-1, keepdims=True)
    scale = lax.rsqrt(jnp.mean(centred * centred, axis=-1, keepdims=True) + EPS)
    return centred * scale, scale


def norm_back(grad, unit, scale, gain):
    scaled = grad * gain
    inner = (
        scaled
        - jnp.mean(scaled, axis=-1, keepdims=True)
        - unit * jnp.mean(scaled * unit, axis=-1, keepdims=True)
    )
    return inner * scale


def column_sum(values):
    return jnp.sum(values, axis=0, keepdims=True)


def expand_small(small, width, chunk):
    eye = lax.broadcasted_iota(jnp.int32, (128, width), 0) == (
        lax.broadcasted_iota(jnp.int32, (128, width), 1) % chunk
    )
    spread = dot(small, eye.astype(F32).astype(BF16))
    runs = GROUPS * chunk // width
    per_run = GROUPS // runs
    group = lax.broadcasted_iota(jnp.int32, (GROUPS * SMALL, width), 0) // SMALL
    column = lax.broadcasted_iota(jnp.int32, (GROUPS * SMALL, width), 1) // chunk
    kept = jnp.where(group % per_run == column, spread, 0.0).reshape(GROUPS, SMALL, width)
    return [jnp.sum(kept[run * per_run : (run + 1) * per_run], axis=0) for run in range(runs)]


def shrink_vectors(vectors, parts):
    width = vectors.shape[1]
    tiled = jnp.broadcast_to(vectors[None], (GROUPS, SMALL, width)).reshape(-1, width)
    row = lax.broadcasted_iota(jnp.int32, (GROUPS * SMALL, width), 0)
    lane = lax.broadcasted_iota(jnp.int32, (GROUPS * SMALL, width), 1)
    group = row // SMALL
    row = row % SMALL
    total = None
    for chunk, first, end in parts:
        runs = GROUPS * chunk // width
        per_run = GROUPS // runs
        keep = (group % per_run == lane // chunk) & (row >= first) & (row < end)
        if runs > 1:
            keep = keep & (row - first == group // per_run)
        eye = lax.broadcasted_iota(jnp.int32, (width, 128), 0) % chunk == lax.broadcasted_iota(
            jnp.int32, (width, 128), 1
        )
        part = dot(jnp.where(keep, tiled, 0.0).astype(BF16), eye.astype(F32).astype(BF16))
        total = part if total is None else total + part
    return total


MIX_TABLE = 128


def same_core(table_ref):
    return table_ref[0, GROUPS] == 0


def take_groups(parts, table_ref, target_ref):
    even = same_core(table_ref)
    half = parts[0].shape[0]

    def slot_of(at, low_ref, high_ref):
        slot = table_ref[0, at]
        index = lax.rem(slot, half)
        return jnp.where(slot >= half, high_ref[index], low_ref[index])

    for pair in range(GROUPS // 2):
        mine = slot_of(pair, *parts[0:2])
        other = slot_of(GROUPS // 2 + pair, *parts[2:4])
        target_ref[2 * pair] = jnp.where(even, mine, other)
        target_ref[2 * pair + 1] = jnp.where(even, other, mine)


def give_groups(values, first_ref, second_ref, table_ref, tile, first_pair=0, table=0):
    even = same_core(table_ref)
    for i in range(values.shape[0] // 2):
        pair = first_pair + i
        one, two = values[2 * i], values[2 * i + 1]
        first_ref[table_ref[0, table + pair], tile] = jnp.where(even, one, two)
        second_ref[table_ref[0, table + GROUPS // 2 + pair], tile] = jnp.where(even, two, one)


def give_lanes(values, first_ref, second_ref, table_ref, at, first_pair=0, table=0):
    for tile in range(values.shape[1] // 128):
        part = values[:, tile * 128 : tile * 128 + 128].astype(BF16).reshape(-1, 16, 128)
        give_groups(part, first_ref, second_ref, table_ref, at + tile, first_pair, table)


def pair_average(rows):
    out = np.zeros((rows // 2, rows), np.float32)
    for i in range(rows // 2):
        out[i, 2 * i] = out[i, 2 * i + 1] = 0.5
    return out


def average(rows, factor):
    out = np.zeros((rows // factor, rows), np.float32)
    for i in range(rows // factor):
        out[i, i * factor : (i + 1) * factor] = 1.0 / factor
    return out


def attention_constants(piece, far_levels, local_top):
    top = local_top + far_levels - 1
    averaged = []
    for level in range(1, top + 1):
        averaged.append(np.repeat(average(piece, 2**level), 2**level, axis=0))
    coarse = np.concatenate([average(piece, 2**level) for level in range(1, local_top)], axis=0)
    tokens = np.arange(piece)
    masks = []
    sizes = []
    for level in range(local_top):
        keys = np.arange(piece >> level)
        block = (tokens >> level)[:, None] // 16
        if level == 0:
            mask = (block // 2) == (keys[None, :] // 32)
        else:
            mask = (block ^ 1) == (keys[None, :] // 16)
        masks += [mask, mask]
        sizes.append(piece >> level)
    for _ in range(far_levels):
        masks += [np.ones((piece, 16), bool)] * 2
        sizes.append(16)
    ones = []
    for level, size in enumerate(sizes):
        head_a = np.zeros((size, 128), np.float32)
        head_a[:, :64] = 2.0**level
        head_b = np.zeros((size, 128), np.float32)
        head_b[:, 64:] = 2.0**level
        ones += [head_a, head_b]
    return dict(
        averaged=np.concatenate(averaged, axis=0),
        averaged_wide=np.concatenate(averaged, axis=1),
        coarse=coarse,
        coarse_t=coarse.T.copy(),
        mask=np.concatenate(masks, axis=1).astype(np.float32),
        ones=np.concatenate(ones, axis=0),
        sizes=tuple(sizes),
    )


def far_constants(seqs):
    out = np.zeros((seqs * 16, seqs * (8 + 16 + 8 + 8)), np.float32)
    starts = (0, seqs * 8, seqs * 24, seqs * 32)
    for seq in range(seqs):
        for slot in range(4):
            for i in range(4):
                row = seq * 16 + slot * 4 + i
                if slot == 1:
                    at = starts[1] + seq * 16 + 4 * i
                    out[row, at : at + 4] = 0.25
                else:
                    at = starts[slot] + seq * 8 + 2 * i
                    out[row, at : at + 2] = 0.5
    return out


def lane_a(rows):
    return lax.broadcasted_iota(jnp.int32, (rows, 128), 1) < 64


def stacked(block, sizes):
    in_a = lane_a(block.shape[0])
    zero = jnp.zeros_like(block)
    head_a = jnp.where(in_a, block, zero)
    head_b = jnp.where(in_a, zero, block)
    parts = []
    at = 0
    for size in sizes:
        parts.append(head_a[at : at + size])
        parts.append(head_b[at : at + size])
        at += size
    return parts


def blocked(parts):
    levels = len(parts) // 2
    rows = []
    for level in range(2, levels):
        block = jnp.concatenate(parts[2 * level : 2 * level + 2], axis=0)
        zero = jnp.zeros_like(block)
        rows.append(
            jnp.concatenate(
                [block if other == level else zero for other in range(2, levels)], axis=1
            )
        )
    return jnp.concatenate(rows, axis=0)


def queries_of(plain_ref, averaged_ref, pair, levels):
    piece = plain_ref.shape[0]
    lanes = slice(pair * 128, pair * 128 + 128)
    rest = jnp.concatenate(
        [averaged_ref[(level - 1) * piece : level * piece, lanes] for level in range(2, levels)],
        axis=1,
    )
    return plain_ref[:, lanes], averaged_ref[0:piece, lanes], rest


def far_rows_of(refs):
    return jnp.concatenate([ref[...].astype(F32) for ref in refs], axis=0)


def pick_far(source_ref, seq, far_rows, seqs):
    parts = []
    at = 0
    for n in far_rows:
        parts.append(source_ref[pl.ds(pl.multiple_of(at + seq * n, n), n), :])
        at += seqs * n
    return jnp.concatenate(parts, axis=0)


def even_average(rows, factor):
    row = lax.broadcasted_iota(jnp.int32, (rows // factor, rows), 0)
    column = lax.broadcasted_iota(jnp.int32, (rows // factor, rows), 1)
    return jnp.where(column // factor == row, 1.0 / factor, 0.0).astype(BF16)


def norm_kernel(x_ref, out_ref, up_ref, down_ref, base_ref, next_ref, pack_ref):
    rows = x_ref.shape[0]
    unit, _ = unit_of(x_ref[...].astype(F32))
    base = dot(even_average(rows, rows // base_ref.shape[0]), unit.astype(BF16)).astype(BF16)
    base_ref[...] = base
    next_ref[...] = dot(even_average(base.shape[0], 2), base).astype(BF16)
    width = out_ref.shape[1]
    pack_ref[:, 0:width] = out_ref[...]
    at = width + up_ref.shape[1]
    pack_ref[:, width:at] = up_ref[...]
    for row in range(0, down_ref.shape[0], 16):
        pack_ref[:, at : at + width] = down_ref[row : row + 16, :]
        at += width


def far_kernel(own_ref, one_ref, two_ref, three_ref, gather_ref, pair_ref, five_ref, six_ref):
    rows = far_rows_of((own_ref, one_ref, two_ref, three_ref)).astype(BF16)
    five = dot(gather_ref[...], rows).astype(BF16)
    five_ref[...] = five
    six_ref[...] = dot(pair_ref[...], five).astype(BF16)


def far_back_kernel(
    five_ref, six_a_ref, six_b_ref, one_ref, two_ref, three_ref, spread_ref, pair_ref,
    own_out, one_out, two_out, three_out,
):
    six = (six_a_ref[...].astype(F32) + six_b_ref[...].astype(F32)).astype(BF16)
    five = (five_ref[...].astype(F32) + dot(pair_ref[...], six)).astype(BF16)
    rows = dot(spread_ref[...], five)
    own = own_out.shape[0]
    one = own + one_ref.shape[0]
    two = one + two_ref.shape[0]
    own_out[...] = rows[:own]
    one_out[...] = (rows[own:one] + one_ref[...].astype(F32)).astype(BF16)
    two_out[...] = (rows[one:two] + two_ref[...].astype(F32)).astype(BF16)
    three_out[...] = (rows[two:] + three_ref[...].astype(F32)).astype(BF16)


def mix_kernel(*refs):
    x_ref = refs[0]
    parts = refs[1:5]
    groups_ref = refs[5]
    far_refs = refs[6:-7]
    vec_ref, q_ref, k_ref, v_ref, kf_ref, vf_ref, weight_ref = refs[-7:]
    width = x_ref.shape[1]
    take_groups(parts, groups_ref, weight_ref)
    unit, _ = unit_of(x_ref[...].astype(F32))
    far = far_rows_of(far_refs)
    small = weight_ref[:, :, 3 * width :].reshape(GROUPS * SMALL, 128)
    plain = expand_small(small, width, width // GROUPS)[0]
    biases = expand_small(small, width, 2 * width // GROUPS)
    ups = expand_small(small, width, 4 * width // GROUPS)
    vec_ref[...] = jnp.concatenate(
        [plain[0:6], biases[0][6:7], biases[1][6:7]]
        + [up[7:8] for up in ups]
        + [jnp.zeros((4, width), F32)],
        axis=0,
    )
    gain, shift = plain[0:1], plain[1:2]
    query_bias, value_bias = biases[0][6:7], biases[1][6:7]
    normed = (unit * gain + shift).astype(BF16)
    far = (far * gain + shift).astype(BF16)
    weight = weight_ref[:, :, 0:width].reshape(width, width)
    queries = (dot(normed, weight) + query_bias).astype(BF16).astype(F32)
    q_ref[...] = (queries * 0.125).astype(BF16)
    weight = weight_ref[:, :, width : 2 * width].reshape(width, width)
    k_ref[...] = dot(normed, weight).astype(BF16)
    kf_ref[...] = dot(far, weight)
    weight = weight_ref[:, :, 2 * width : 3 * width].reshape(width, width)
    v_ref[...] = (dot(normed, weight) + value_bias).astype(BF16)
    vf_ref[...] = dot(far, weight) + value_bias


def attention_kernel(
    q_ref, k_ref, v_ref, kf_ref, vf_ref, averaged_ref, coarse_ref, mask_ref, ones_ref,
    kall_ref, vall_ref, p_ref, att_ref, rden_ref,
    qe_ref,
    *, far_rows, sizes, local_top,
):
    piece, width = q_ref.shape
    levels = len(sizes)
    seq = pl.program_id(0)
    count = kf_ref.shape[0] // sum(far_rows)
    queries = q_ref[...]
    qe_ref[...] = dot(averaged_ref[...], queries).astype(BF16)
    keys = k_ref[...]
    values = v_ref[...]
    coarse_keys = dot(coarse_ref[...], keys).astype(BF16)
    coarse_values = dot(coarse_ref[...], values)
    scaled = [values]
    at = 0
    for level in range(1, local_top):
        scaled.append((coarse_values[at : at + sizes[level]] * 2.0**level).astype(BF16))
        at += sizes[level]
    far_values = pick_far(vf_ref, seq, far_rows, count)
    for level in range(local_top, levels):
        at = 16 * (level - local_top)
        scaled.append((far_values[at : at + 16] * 2.0**level).astype(BF16))
    kall_ref[0] = jnp.concatenate(
        [keys, coarse_keys, pick_far(kf_ref, seq, far_rows, count).astype(BF16)], axis=0
    )
    vall_ref[0] = jnp.concatenate(scaled, axis=0)
    for pair in range(width // 128):
        lanes = slice(pair * 128, pair * 128 + 128)
        plain, one, rest = queries_of(q_ref, qe_ref, pair, levels)
        key_parts = stacked(kall_ref[0, :, lanes], sizes)
        scores = jnp.concatenate(
            [
                dot_right(plain, jnp.concatenate(key_parts[0:2], axis=0)),
                dot_right(one, jnp.concatenate(key_parts[2:4], axis=0)),
                dot_right(rest, blocked(key_parts)),
            ],
            axis=1,
        )
        weights = jnp.where(mask_ref[...] > 0.0, jnp.exp(scores), 0.0).astype(BF16)
        p_ref[0, pair] = weights
        both = jnp.concatenate(
            [jnp.concatenate(stacked(vall_ref[0, :, lanes], sizes), axis=0), ones_ref[...]], axis=1
        )
        sums = dot(weights, both)
        rden = 1.0 / sums[:, 128:]
        rden_ref[:, lanes] = rden
        att_ref[:, lanes] = (sums[:, :128] * rden).astype(BF16)


def feed_kernel(
    vec_ref, table_ref, x_ref, cot_ref, att_ref, part_one, part_two, part_three, part_four,
    out_ref, dmid_ref, datt_ref, sum_ref, first_out, second_out,
    weight_ref,
):
    width = x_ref.shape[1]
    blocks = (weight_ref.shape[2] // width - 1) // 2
    take_groups((part_one, part_two, part_three, part_four), table_ref, weight_ref)
    gain = vec_ref[3:4, :]
    out_weight = weight_ref[:, :, 0:width].reshape(width, width)
    middle = x_ref[...].astype(F32) + dot(att_ref[...], out_weight) + vec_ref[2:3, :]
    unit, inverse = unit_of(middle)
    normed = (unit * gain + vec_ref[4:5, :]).astype(BF16)
    g_out = cot_ref[...]
    result = middle + vec_ref[5:6, :]
    d_two = jnp.zeros(x_ref.shape, F32)
    tiles = width // 128
    per_group = blocks * width // GROUPS // 16
    groups = GROUPS // blocks
    sums = []
    for block in range(blocks):
        up = weight_ref[:, :, width * (block + 1) : width * (block + 2)].reshape(width, width)
        down = jnp.concatenate(
            [
                weight_ref[groups * block + group, :, width * at : width * (at + 1)]
                for group in range(groups)
                for at in range(blocks + 1, blocks + 1 + per_group)
            ],
            axis=0,
        )
        pre = dot(normed, up) + vec_ref[8 + block : 9 + block, :]
        cdf = 0.5 + 0.5 * lax.erf(pre * 0.7071067811865476)
        hidden = (pre * cdf).astype(BF16)
        slope = cdf + pre * (0.3989422804014327 * jnp.exp(-0.5 * pre * pre))
        result = result + dot(hidden, down)
        grad = dot_left(hidden, g_out).reshape(groups, per_group, 16, width)
        for part in range(per_group):
            give_lanes(
                grad[:, part].reshape(-1, width), first_out, second_out, table_ref,
                tiles * (blocks + 1 + part), groups // 2 * block,
            )
        g_pre = (dot_right(g_out, down) * slope).astype(BF16)
        sums.append(column_sum(g_pre.astype(F32)))
        grad = dot_left(normed, g_pre)
        give_lanes(grad, first_out, second_out, table_ref, tiles * (block + 1))
        d_two = d_two + dot_right(g_pre, up)
    out_ref[...] = result.astype(BF16)
    cot = g_out.astype(F32)
    d_middle = cot + norm_back(d_two, unit, inverse, gain)
    dmid_ref[...] = d_middle
    branch = d_middle.astype(BF16)
    datt_ref[...] = dot_right(branch, out_weight)
    give_lanes(dot_left(att_ref[...], branch), first_out, second_out, table_ref, 0)
    sum_ref[...] = jnp.concatenate(
        [
            jnp.zeros((2, width), F32),
            column_sum(branch.astype(F32)),
            column_sum(d_two * unit),
            column_sum(d_two),
            column_sum(cot),
            jnp.zeros((2, width), F32),
        ]
        + sums
        + [jnp.zeros((8 - blocks, width), F32)],
        axis=0,
    )


def attention_back_kernel(*refs, far_rows, sizes, local_top):
    fars = len(far_rows)
    q_ref, kall_ref, vall_ref, p_ref, att_ref, rden_ref, datt_ref = refs[:7]
    x_ref, vec_ref, sum_ref = refs[7:10]
    parts = refs[10:14]
    groups_ref = refs[14]
    averaged_ref, wide_ref, coarse_t_ref, ones_ref = refs[15:19]
    far_refs = refs[19 : 19 + fars]
    scaled_ref, first_ref, second_ref = refs[19 + fars : 22 + fars]
    dfar_refs = refs[22 + fars : 22 + 2 * fars]
    (
        weight_ref, dq_ref, dk_ref, dv_ref, dkf_ref, dvf_ref, qe_ref, dkall_ref, dvall_ref, t_ref,
        dqacc_ref,
    ) = refs[22 + 2 * fars :]
    width = x_ref.shape[1]
    piece = q_ref.shape[0]
    seqs = x_ref.shape[0] // piece
    levels = len(sizes)
    starts = np.concatenate([[0], np.cumsum(sizes)]).tolist()
    local = starts[local_top]
    seq = pl.program_id(0)

    qe_ref[...] = dot(averaged_ref[...], q_ref[...]).astype(BF16)
    near = 2 * sizes[0]
    mid = near + 2 * sizes[1]
    for pair in range(width // 128):
        lanes = slice(pair * 128, pair * 128 + 128)
        plain, one, rest = queries_of(q_ref, qe_ref, pair, levels)
        key_parts = stacked(kall_ref[0, :, lanes], sizes)
        both = jnp.concatenate(
            [jnp.concatenate(stacked(vall_ref[0, :, lanes], sizes), axis=0), ones_ref[...]], axis=1
        )
        d_num = datt_ref[:, lanes] * rden_ref[:, lanes]
        d_den = -d_num * att_ref[:, lanes].astype(F32)
        d_num = d_num.astype(BF16)
        weights = p_ref[0, pair]
        d_weights = dot_right(jnp.concatenate([d_num, d_den.astype(BF16)], axis=1), both)
        d_scores = (weights.astype(F32) * d_weights).astype(BF16)
        d_key_near = dot_left(d_scores[:, :near], plain)
        d_key_mid = dot_left(d_scores[:, near:mid], one)
        d_key_rest = dot_left(d_scores[:, mid:], rest)
        d_value = dot_left(weights, d_num)
        dqacc_ref[:, lanes] = dot(d_scores[:, :near], jnp.concatenate(key_parts[0:2], axis=0))
        t_ref[0:piece, lanes] = dot(
            d_scores[:, near:mid], jnp.concatenate(key_parts[2:4], axis=0)
        ).astype(BF16)
        d_rest = dot(d_scores[:, mid:], blocked(key_parts)).astype(BF16)
        at = 0
        for level in range(levels):
            size = sizes[level]
            low, high = starts[level], starts[level + 1]
            in_a = lane_a(size)
            if level == 0:
                source = d_key_near
            elif level == 1:
                source = d_key_mid
            else:
                block = slice((level - 2) * 128, (level - 1) * 128)
                source = d_key_rest[at - mid : at - mid + 2 * size, block]
                t_ref[(level - 1) * piece : level * piece, lanes] = d_rest[:, block]
            dkall_ref[low:high, lanes] = jnp.where(in_a, source[:size], source[size:])
            values = d_value[at : at + 2 * size]
            dvall_ref[low:high, lanes] = jnp.where(in_a, values[:size], values[size:]) * 2.0**level
            at += 2 * size
    rows = pl.ds(pl.multiple_of(seq * piece, piece), piece)
    dq_ref[rows, :] = ((dqacc_ref[...] + dot(wide_ref[...], t_ref[...])) * 0.125).astype(BF16)
    for target, source in ((dk_ref, dkall_ref), (dv_ref, dvall_ref)):
        spread = dot(coarse_t_ref[...], source[piece:local, :].astype(BF16))
        target[rows, :] = (source[0:piece, :] + spread).astype(BF16)
    at = 0
    low = local
    for n in far_rows:
        target = pl.ds(pl.multiple_of(at + seq * n, n), n)
        dkf_ref[target, :] = dkall_ref[low : low + n, :]
        dvf_ref[target, :] = dvall_ref[low : low + n, :]
        at += seqs * n
        low += n

    @pl.when(seq == seqs - 1)
    def _():
        take_groups(parts, groups_ref, weight_ref)
        gain = vec_ref[0:1, :]
        shift = vec_ref[1:2, :]
        unit, _ = unit_of(x_ref[...].astype(F32))
        normed = (unit * gain + shift).astype(BF16)
        far = far_rows_of(far_refs)
        far_normed = (far * gain + shift).astype(BF16)
        both = jnp.concatenate([normed, far_normed], axis=0)
        far_grads = (None, dkf_ref[...].astype(BF16), dvf_ref[...].astype(BF16))
        grads = (dq_ref[...], dk_ref[...], dv_ref[...])
        d_one = jnp.zeros(x_ref.shape, F32)
        d_far = jnp.zeros(far.shape, F32)
        for part in range(3):
            lanes = slice(part * width, part * width + width)
            weight = weight_ref[:, :, lanes].reshape(width, width)
            d_one = d_one + dot_right(grads[part], weight)
            if part == 0:
                grad = dot_left(normed, grads[part])
            else:
                d_far = d_far + dot_right(far_grads[part], weight)
                grad = dot_left(both, jnp.concatenate([grads[part], far_grads[part]], axis=0))
            at = part * width // 128
            give_lanes(grad, first_ref, second_ref, groups_ref, at, table=MIX_TABLE)
        scaled_ref[...] = d_one * gain
        at = 0
        for ref in dfar_refs:
            ref[...] = (d_far[at : at + ref.shape[0]] * gain).astype(BF16)
            at += ref.shape[0]
        vectors = jnp.concatenate(
            [
                column_sum(d_one * unit) + column_sum(d_far * far),
                column_sum(d_one) + column_sum(d_far),
                sum_ref[2:6, :],
                column_sum(grads[0].astype(F32)),
                column_sum(grads[2].astype(F32)) + column_sum(dvf_ref[...]),
                sum_ref[8:16, :],
            ],
            axis=0,
        )
        chunk = width // GROUPS
        small = shrink_vectors(vectors, ((chunk, 0, 6), (2 * chunk, 6, 8), (4 * chunk, 8, 12)))
        at = 3 * width // 128
        give_lanes(small, first_ref, second_ref, groups_ref, at, table=MIX_TABLE)


def input_kernel(
    x_ref, dmid_ref, scaled_ref, own_ref, one_ref, two_ref, three_ref, pair_ref, spread_ref,
    din_ref,
):
    unit, inverse = unit_of(x_ref[...].astype(F32))
    lower = own_ref[...] + two_ref[...].astype(F32) + three_ref[...].astype(F32)
    base = one_ref[...].astype(F32) + dot(pair_ref[...], lower.astype(BF16))
    scaled = scaled_ref[...] + dot(spread_ref[...], base.astype(BF16))
    inner = (
        scaled
        - jnp.mean(scaled, axis=-1, keepdims=True)
        - unit * jnp.mean(scaled * unit, axis=-1, keepdims=True)
    )
    din_ref[...] = dmid_ref[...] + inner * inverse


def last_kernel(
    mix_one, mix_two, mix_three, mix_four, feed_ref, other_feed_ref,
    matrix_ref, out_ref, up_ref, down_ref, *vector_refs,
):
    total = feed_ref[0].astype(F32) + other_feed_ref[0].astype(F32)
    at = 0
    for ref in (out_ref, up_ref):
        for lane in range(0, ref.shape[1], 128):
            ref[:, lane : lane + 128] = total[at]
            at += 1
    for row in range(0, down_ref.shape[0], 16):
        for lane in range(0, down_ref.shape[1], 128):
            down_ref[row : row + 16, lane : lane + 128] = total[at]
            at += 1
    total = mix_one[0].astype(F32) + mix_two[0].astype(F32)
    total += mix_three[0].astype(F32) + mix_four[0].astype(F32)
    for lane in range(0, matrix_ref.shape[1], 128):
        matrix_ref[:, lane : lane + 128] = total[lane // 128]
    small = total[matrix_ref.shape[1] // 128]
    for i in range(6):
        vector_refs[i][...] = small[i : i + 1, : vector_refs[i].shape[1]]
    vector_refs[6][...] = column_sum(small[6:8])[:, : vector_refs[6].shape[1]]
    vector_refs[7][...] = column_sum(small[8:12])[:, : vector_refs[7].shape[1]]


def vmem():
    return pl.BlockSpec(memory_space=pltpu.VMEM)


def anywhere():
    return pl.BlockSpec(memory_space=pl.ANY)


def scalars():
    return pl.BlockSpec(memory_space=pltpu.SMEM)


def fixed(*dims):
    return pl.BlockSpec(dims, lambda i: (0,) * len(dims))


def moving(*dims):
    return pl.BlockSpec(dims, lambda i: (i,) + (0,) * (len(dims) - 1))


def shape(dims, dtype):
    return jax.ShapeDtypeStruct(dims, dtype)


def const(values):
    return jnp.asarray(values, BF16)


def bit_orders():
    return ((8, 4, 16, 2), (2, 8, 4, 16))


def mix_orders():
    return ((8, 4, 16, 2), (8, 4, 2, 16))


def slot_offset(slot, order):
    return sum(bit for k, bit in enumerate(order) if slot >> k & 1)


def group_table(orders):
    table = np.zeros((32, 128), np.int32)
    for device in range(32):
        core = device & 1
        table[device, GROUPS] = core
        for slot in range(16):
            table[device, (device ^ slot_offset(slot, orders[core])) // 2] = slot
            group = device ^ 1 ^ slot_offset(slot, orders[1 - core])
            table[device, GROUPS // 2 + group // 2] = slot
    return table


def exchange(value, bits):
    if isinstance(bits, int):
        bits = (bits, bits)
    count = lax.axis_size(AXES)
    return lax.ppermute(value, AXES, [(i, i ^ bits[i & 1]) for i in range(count)])


def after(value, *others):
    return lax.optimization_barrier((value,) + others)[0]


def added(left, right):
    return (left.astype(F32) + right.astype(F32)).astype(BF16)


def send(buffer, k, orders=None):
    orders = orders or bit_orders()
    return exchange(buffer, (orders[0][k], orders[1][k]))


def halves(kept, other):
    half = kept.shape[0] // 2
    return added(kept[:half], other[:half]), added(kept[half:], other[half:])


def joined(buffer, other):
    return jnp.concatenate([buffer, other], axis=0)


def call(kernel, name, outs, ins, args, work, scratch=(), grid=None, room=6):
    return pl.pallas_call(
        kernel,
        out_shape=tuple(item[0] for item in outs),
        in_specs=list(ins),
        out_specs=tuple(item[1] for item in outs),
        scratch_shapes=list(scratch),
        compiler_params=pltpu.CompilerParams(vmem_limit_bytes=room * MIB),
        cost_estimate=pl.CostEstimate(flops=work, bytes_accessed=work >> 9, transcendentals=0),
        name=name,
        **({} if grid is None else {"grid": grid}),
    )(*args)


def coarsen(values):
    return (values[:, 0::2] + values[:, 1::2]) * 0.5


def whole_far(base, seqs, far_levels, position):
    rows = base.reshape(seqs, 16, base.shape[1])
    full = lax.all_gather(rows, "seq", axis=1, tiled=True).astype(F32)
    parts = []
    for extra in range(far_levels):
        partner = (position // 2**extra) ^ 1
        parts.append(lax.dynamic_slice_in_dim(full, partner * 16, 16, axis=1))
        if extra + 1 < far_levels:
            full = coarsen(full)
    return jnp.concatenate(parts, axis=1).astype(BF16).reshape(seqs * 16 * far_levels, -1)


def whole_far_back(grad, seqs, far_levels, position):
    stack = grad.reshape(seqs, far_levels, 16, -1).astype(F32)
    ids = jnp.arange(far_levels).reshape(1, far_levels, 1, 1)
    count = lax.axis_size("seq")
    for bit in range(far_levels):
        pairs = [(i, i ^ 1 << bit) for i in range(count)]
        other = lax.ppermute(stack.astype(BF16), "seq", pairs).astype(F32)
        stack = jnp.where(ids > bit, stack + other, jnp.where(ids == bit, other, stack))
    own = jnp.zeros((seqs, 16, stack.shape[-1]), F32)
    for extra in range(far_levels):
        rows = 16 >> extra
        offset = position % 2**extra * rows
        part = lax.dynamic_slice_in_dim(stack[:, extra], offset, rows, axis=1)
        own = own + jnp.repeat(part, 2**extra, axis=1) * 0.5**extra
    return own.reshape(seqs * 16, -1).astype(BF16)


def body(
    layer_input, qkv_weight, qv_bias, out_weight, out_bias, first_gain, first_shift, second_gain,
    second_shift, up_weight, up_bias, down_weight, down_bias, cotangent,
):
    batches, per_batch, piece, width = layer_input.shape
    seqs = batches * per_batch
    tokens = seqs * piece
    hidden = up_weight.shape[1]
    blocks = hidden // width
    devices = lax.axis_size(AXES)
    pieces = lax.axis_size("seq")
    position = lax.axis_index("seq")
    far_levels = pieces.bit_length() - 1
    local_top = (piece // 16).bit_length() - 1
    fast = devices == GROUPS and pieces == 16
    x = layer_input.reshape(tokens, width)
    cot = cotangent.reshape(tokens, width)
    consts = attention_constants(piece, far_levels, local_top)
    sizes = consts["sizes"]
    keys = sum(sizes)
    flat = (tokens, width)
    base_rows = seqs * 16
    coarse_all = np.kron(np.eye(seqs, dtype=np.float32), average(piece, piece // 16))
    pair = np.kron(np.eye(seqs, dtype=np.float32), pair_average(16))
    gather_far = far_constants(seqs)
    vectors = (
        first_gain, first_shift, out_bias, second_gain, second_shift, down_bias, qv_bias, up_bias,
    )

    shards = (out_weight, up_weight, down_weight)
    if not fast:
        sizes_of = ((16, width), (16, hidden), (hidden // GROUPS, width))
        shards = tuple(jnp.zeros(dims, BF16) for dims in sizes_of)
    base, below, pack_b = call(
        norm_kernel,
        "norm",
        [
            (shape((base_rows, width), BF16), vmem()),
            (shape((base_rows // 2, width), BF16), vmem()),
            (shape((16, width + 2 * hidden), BF16), vmem()),
        ],
        [vmem()] * 4,
        (x, *shards),
        1 << 20,
    )

    if fast:
        me = lax.axis_index(AXES)
        table = np.concatenate([group_table(bit_orders()), group_table(mix_orders())], axis=1)
        groups = lax.dynamic_slice_in_dim(jnp.asarray(table), me, 1, axis=0)
        a = jnp.pad(qkv_weight, ((0, 0), (0, 128)))
        for row, vector in enumerate(vectors):
            item = vector.reshape(1, -1)
            lanes = (3 * width, 128 - item.shape[1])
            a = a + jnp.pad(item, ((row, SMALL - 1 - row), lanes))
        a = a[None]
        a = joined(a, send(a, 0))
        other_a = send(after(a, base), 1)
        b = after(pack_b[None], a)
        other_b = send(b, 0)
        a = joined(a, other_a)
        other_a = send(a, 2)
        b = joined(after(b, a), other_b)
        other_b = send(b, 1)
        near, half = after(base, a), after(below, a)
        one, two, three = exchange(near, 1), exchange(half, 2), exchange(half, 3)
        a = joined(a, other_a)
        a = after(a, one, two, three)
        other_a = send(a, 3)
        five, six = call(
            far_kernel,
            "far",
            [
                (shape((base_rows, width), BF16), vmem()),
                (shape((base_rows // 2, width), BF16), vmem()),
            ],
            [vmem()] * 6,
            (after(below, a), one, two, three, const(gather_far), const(pair)),
            1 << 20,
        )
        far = (one, two, three, exchange(five, 4), exchange(six, 8), exchange(six, 12))
        far_rows = (16, 8, 8, 16, 8, 8)
        b = joined(after(b, a), other_b)
        other_b = send(b, 2)
        lower = exchange(after(a, five), 1)
        other_a = after(other_a, five, six)
        parts_a = (a, other_a, lower, exchange(other_a, 1))
        b = joined(after(b, other_a, *far), other_b)
        other_b = send(b, 3)
        lower = exchange(after(b, other_a), 1)
    else:
        groups = [slot % (GROUPS // 2) for slot in range(GROUPS)] + [0] * (128 - GROUPS)
        groups = jnp.asarray([groups * 2], jnp.int32)

        def whole(value):
            return lax.all_gather(value, AXES, axis=0, tiled=True).reshape(
                (GROUPS, -1) + value.shape[1:]
            )

        small = [jnp.pad(v, ((0, 0), (0, 128 - v.shape[1]))) for v in map(whole, vectors)]
        small += [jnp.zeros((GROUPS, 128), BF16)] * (SMALL - len(small))
        gathered_a = jnp.concatenate([whole(qkv_weight), jnp.stack(small, axis=1)], axis=2)
        downs = whole(down_weight).reshape(GROUPS, -1, 16, width).transpose(0, 2, 1, 3)
        parts = [whole(out_weight), whole(up_weight), downs.reshape(GROUPS, 16, -1)]
        gathered_b = jnp.concatenate(parts, axis=2)

        def quarters(item):
            return item[0:16:2], item[16::2], item[1:16:2], item[17::2]

        parts_a, parts_b = quarters(gathered_a), quarters(gathered_b)
        far = (whole_far(base, seqs, far_levels, position),)
        far_rows = (16 * far_levels,)

    lanes_a = 3 * width + 128
    tiles_a = lanes_a // 128
    tiles_b = (width + 2 * hidden) // 128
    top = len(sizes) - 1
    pairs = width // 128
    total_far = seqs * 16 * far_levels
    half_a = shape((GROUPS // 2, tiles_a, 16, 128), BF16)
    half_b = shape((GROUPS // 2, tiles_b, 16, 128), BF16)
    far_flat = shape((total_far, width), F32)
    low, high = shape(flat, BF16), shape(flat, F32)
    sixteen = shape((16, width), F32)
    level = dict(far_rows=far_rows, sizes=sizes, local_top=local_top)

    vec, queries, key, value, far_key, far_value = call(
        mix_kernel,
        "mix",
        [(sixteen, vmem())] + [(low, vmem())] * 3 + [(far_flat, vmem())] * 2,
        [vmem()] * 5 + [scalars()] + [vmem()] * len(far),
        (x, *parts_a, groups, *far),
        1 << 24,
        [pltpu.VMEM((GROUPS, 16, lanes_a), BF16)],
        room=14,
    )
    rows_spec = moving(piece, width)
    keys_spec = moving(1, keys, width)
    p_spec = moving(1, pairs, piece, 2 * keys)
    keys_shape = shape((seqs, keys, width), BF16)
    kall, vall, weights, attended, rden = call(
        partial(attention_kernel, **level),
        "attention",
        [
            (keys_shape, keys_spec),
            (keys_shape, keys_spec),
            (shape((seqs, pairs, piece, 2 * keys), BF16), p_spec),
            (low, rows_spec),
            (high, rows_spec),
        ],
        [rows_spec] * 3
        + [fixed(total_far, width)] * 2
        + [
            fixed(top * piece, piece),
            fixed(*consts["coarse"].shape),
            fixed(piece, 2 * keys),
            fixed(2 * keys, 128),
        ],
        (
            queries, key, value, far_key, far_value, const(consts["averaged"]),
            const(consts["coarse"]), jnp.asarray(consts["mask"]), const(consts["ones"]),
        ),
        1 << 24,
        [pltpu.VMEM((top * piece, width), BF16)],
        (seqs,),
        room=12,
    )
    if fast:
        other_b = after(other_b, attended)
        parts_b = (b, other_b, lower, exchange(other_b, 1))

    result, d_middle, d_attended, sums, kept_b, sent_b = call(
        feed_kernel,
        "feed",
        [(low, vmem()), (high, vmem()), (high, vmem()), (sixteen, vmem())] + [(half_b, vmem())] * 2,
        [vmem(), scalars()] + [vmem()] * 7,
        (vec, groups, x, cot, attended, *parts_b),
        8 << 30,
        [
            pltpu.VMEM((GROUPS, 16, width + 2 * hidden), BF16),
        ],
        room=30,
    )
    if fast:
        kept_b, upper = halves(kept_b, exchange(sent_b, 1))
        other_b = send(upper, 3)
        d_attended = after(d_attended, upper)
    outs = call(
        partial(attention_back_kernel, **level),
        "attention_back",
        [(high, fixed(*flat))] + [(half_a, fixed(*half_a.shape))] * 2
        + [(shape(item.shape, BF16), fixed(*item.shape)) for item in far],
        [rows_spec, keys_spec, keys_spec, p_spec, rows_spec, rows_spec, rows_spec]
        + [fixed(*flat), fixed(16, width), fixed(16, width)]
        + [fixed(*item.shape) for item in parts_a]
        + [scalars()]
        + [
            fixed(top * piece, piece),
            fixed(piece, top * piece),
            fixed(*consts["coarse_t"].shape),
            fixed(2 * keys, 128),
        ]
        + [fixed(*item.shape) for item in far],
        (
            queries, kall, vall, weights, attended, rden, d_attended, x, vec, sums,
            *parts_a, groups, const(consts["averaged"]),
            const(consts["averaged_wide"]), const(consts["coarse_t"]), const(consts["ones"]), *far,
        ),
        6 << 30,
        [
            pltpu.VMEM((GROUPS, 16, lanes_a), BF16),
            pltpu.VMEM(flat, BF16),
            pltpu.VMEM(flat, BF16),
            pltpu.VMEM(flat, BF16),
            pltpu.VMEM((total_far, width), F32),
            pltpu.VMEM((total_far, width), F32),
            pltpu.VMEM((top * piece, width), BF16),
            pltpu.VMEM((keys, width), F32),
            pltpu.VMEM((keys, width), F32),
            pltpu.VMEM((top * piece, width), BF16),
            pltpu.VMEM((piece, width), F32),
        ],
        (seqs,),
        room=28,
    )
    scaled, kept_a, sent_a = outs[:3]
    d_far = outs[3:]

    if fast:
        kept_b, upper_b = halves(after(kept_b, scaled), other_b)
        other_b = send(upper_b, 2)
        other_a = exchange(after(sent_a, upper_b), 1)
        kept_a, upper_a = halves(kept_a, other_a)
        other_a = send(upper_a, 3, mix_orders())
        back = [after(item, upper_a) for item in d_far[3:]]
        back = [exchange(item, bits) for item, bits in zip(back, (4, 8, 12))]
        kept_b, upper_b = halves(after(kept_b, *back), other_b)
        other_b = send(upper_b, 1)
        kept_a, upper_a = halves(after(kept_a, upper_b), other_a)
        other_a = send(upper_a, 2, mix_orders())
        back = [after(item, upper_a) for item in back]
        own, out_one, out_two, out_three = call(
            far_back_kernel,
            "far_back",
            [
                (shape((base_rows // 2, width), F32), vmem()),
                (shape((base_rows, width), BF16), vmem()),
                (shape((base_rows // 2, width), BF16), vmem()),
                (shape((base_rows // 2, width), BF16), vmem()),
            ],
            [vmem()] * 8,
            (*back, d_far[0], d_far[1], d_far[2], const(gather_far.T), const(pair.T)),
            1 << 20,
        )
        back_one = exchange(out_one, 1)
        back_two = exchange(out_two, 2)
        back_three = exchange(out_three, 3)
        own_a, far_a = halves(after(kept_a, own), other_a)
        one_a, two_a = own_a[0:1], own_a[1:2]
        lasts_a = (
            one_a,
            exchange(two_a, 8),
            exchange(far_a[0:1], 4),
            exchange(far_a[1:2], 12),
        )
        kept_b, upper_b = halves(after(kept_b, own_a), other_b)
        other_b = send(upper_b, 0)
    else:
        back_one = whole_far_back(d_far[0], seqs, far_levels, position)
        own = jnp.zeros((base_rows // 2, width), F32)
        back_two = back_three = jnp.zeros((base_rows // 2, width), BF16)

    (d_input,) = call(
        input_kernel,
        "input_grad",
        [(high, vmem())],
        [vmem()] * 9,
        (
            x, d_middle, scaled, own, back_one, back_two, back_three, const(pair.T),
            const(coarse_all.T),
        ),
        1 << 20,
    )

    if fast:
        grad_qkv, grad_out_weight, grad_up, grad_down, *plain = call(
            last_kernel,
            "last",
            [
                (shape(item.shape, F32), vmem())
                for item in (qkv_weight, out_weight, up_weight, down_weight)
            ]
            + [(shape((1, v.shape[0]), F32), vmem()) for v in vectors],
            [vmem()] * 6,
            (*lasts_a, kept_b, other_b),
            1 << 16,
        )
        plain = [item.reshape(-1) for item in plain]
        grad_qv, grad_up_bias = plain[6:8]
    else:

        def reduced(item):
            return lax.psum_scatter(item.astype(F32), AXES, scatter_dimension=0, tiled=True)

        def rows_of(item):
            return reduced(item.transpose(0, 2, 1, 3).reshape(GROUPS * 16, -1))

        all_a = jnp.stack([kept_a, sent_a], axis=1).reshape(GROUPS, *half_a.shape[1:])
        all_b = jnp.stack([kept_b, sent_b], axis=1).reshape(GROUPS, *half_b.shape[1:])
        grad_qkv = rows_of(all_a[:, :-1])
        small = all_a[:, -1]
        chunk = width // GROUPS
        plain = [reduced(small[:, i, :chunk].reshape(-1)) for i in range(6)]
        grad_qv = reduced(jnp.sum(small[:, 6:8, : 2 * chunk], axis=1).reshape(-1))
        grad_up_bias = reduced(jnp.sum(small[:, 8:12, : 4 * chunk], axis=1).reshape(-1))
        split = width // 128
        grad_out_weight = rows_of(all_b[:, :split])
        grad_up = rows_of(all_b[:, split : split * (blocks + 1)])
        downs = all_b[:, split * (blocks + 1) :].reshape(GROUPS, -1, split, 16, 128)
        grad_down = reduced(downs.transpose(0, 1, 3, 2, 4).reshape(hidden, width))

    return (
        result.reshape(layer_input.shape),
        d_input.reshape(layer_input.shape),
        grad_qkv,
        grad_qv,
        grad_out_weight,
        plain[2],
        plain[0],
        plain[1],
        plain[3],
        plain[4],
        grad_up,
        grad_up_bias,
        grad_down,
        plain[5],
    )


def solution(mesh):
    tokens = P(None, "dp", "seq", None)
    matrix = P(AXES, None)
    vector = P(AXES)
    in_specs = (
        tokens, matrix, vector, matrix, vector, vector, vector, vector, vector, matrix, vector,
        matrix, vector, tokens,
    )
    out_specs = (
        tokens, tokens, matrix, vector, matrix, vector, vector, vector, vector, vector, matrix,
        vector, matrix, vector,
    )
    return jax.shard_map(body, mesh=mesh, in_specs=in_specs, out_specs=out_specs, check_vma=False)
```

```python
from functools import partial

import jax
import jax.numpy as jnp
import numpy as np
from jax import lax
from jax.experimental import pallas as pl
from jax.experimental.pallas import tpu as pltpu
from jax.sharding import PartitionSpec as P

HEADS = 8
AXES = ("dp", "seq")
F32 = jnp.float32
BF16 = jnp.bfloat16
GROUPS = 32
SMALL = 16
EPS = 1e-05
MIB = 1024 * 1024


def dot(left, right):
    return jnp.dot(left, right, preferred_element_type=F32)


def dot_right(left, right):
    return lax.dot_general(left, right, (((1,), (1,)), ((), ())), preferred_element_type=F32)


def dot_left(left, right):
    return lax.dot_general(left, right, (((0,), (0,)), ((), ())), preferred_element_type=F32)


def unit_of(values):
    centred = values - jnp.mean(values, axis=-1, keepdims=True)
    scale = lax.rsqrt(jnp.mean(centred * centred, axis=-1, keepdims=True) + EPS)
    return centred * scale, scale


def norm_back(grad, unit, scale, gain):
    scaled = grad * gain
    inner = (
        scaled
        - jnp.mean(scaled, axis=-1, keepdims=True)
        - unit * jnp.mean(scaled * unit, axis=-1, keepdims=True)
    )
    return inner * scale


def column_sum(values):
    return jnp.sum(values, axis=0, keepdims=True)


def expand_small(small, width, chunk):
    eye = lax.broadcasted_iota(jnp.int32, (128, width), 0) == (
        lax.broadcasted_iota(jnp.int32, (128, width), 1) % chunk
    )
    spread = dot(small, eye.astype(F32).astype(BF16))
    runs = GROUPS * chunk // width
    per_run = GROUPS // runs
    group = lax.broadcasted_iota(jnp.int32, (GROUPS * SMALL, width), 0) // SMALL
    column = lax.broadcasted_iota(jnp.int32, (GROUPS * SMALL, width), 1) // chunk
    kept = jnp.where(group % per_run == column, spread, 0.0).reshape(GROUPS, SMALL, width)
    return [jnp.sum(kept[run * per_run : (run + 1) * per_run], axis=0) for run in range(runs)]


def shrink_vectors(vectors, parts):
    width = vectors.shape[1]
    tiled = jnp.broadcast_to(vectors[None], (GROUPS, SMALL, width)).reshape(-1, width)
    row = lax.broadcasted_iota(jnp.int32, (GROUPS * SMALL, width), 0)
    lane = lax.broadcasted_iota(jnp.int32, (GROUPS * SMALL, width), 1)
    group = row // SMALL
    row = row % SMALL
    total = None
    for chunk, first, end in parts:
        runs = GROUPS * chunk // width
        per_run = GROUPS // runs
        keep = (group % per_run == lane // chunk) & (row >= first) & (row < end)
        if runs > 1:
            keep = keep & (row - first == group // per_run)
        eye = lax.broadcasted_iota(jnp.int32, (width, 128), 0) % chunk == lax.broadcasted_iota(
            jnp.int32, (width, 128), 1
        )
        part = dot(jnp.where(keep, tiled, 0.0).astype(BF16), eye.astype(F32).astype(BF16))
        total = part if total is None else total + part
    return total


MIX_TABLE = 128
MIX_BACK_TABLE = 256


def same_core(table_ref):
    return table_ref[0, GROUPS] == 0


def take_groups(parts, table_ref, target_ref, table=0):
    even = same_core(table_ref)
    half = parts[0].shape[0]

    def slot_of(at, low_ref, high_ref):
        slot = table_ref[0, table + at]
        index = lax.rem(slot, half)
        return jnp.where(slot >= half, high_ref[index], low_ref[index])

    for pair in range(GROUPS // 2):
        mine = slot_of(pair, *parts[0:2])
        other = slot_of(GROUPS // 2 + pair, *parts[2:4])
        target_ref[2 * pair] = jnp.where(even, mine, other)
        target_ref[2 * pair + 1] = jnp.where(even, other, mine)


def give_groups(values, first_ref, second_ref, table_ref, tile, first_pair=0, table=0):
    even = same_core(table_ref)
    for i in range(values.shape[0] // 2):
        pair = first_pair + i
        one, two = values[2 * i], values[2 * i + 1]
        first_ref[table_ref[0, table + pair], tile] = jnp.where(even, one, two)
        second_ref[table_ref[0, table + GROUPS // 2 + pair], tile] = jnp.where(even, two, one)


def give_lanes(values, first_ref, second_ref, table_ref, at, first_pair=0, table=0):
    for tile in range(values.shape[1] // 128):
        part = values[:, tile * 128 : tile * 128 + 128].astype(BF16).reshape(-1, 16, 128)
        give_groups(part, first_ref, second_ref, table_ref, at + tile, first_pair, table)


def pair_average(rows):
    out = np.zeros((rows // 2, rows), np.float32)
    for i in range(rows // 2):
        out[i, 2 * i] = out[i, 2 * i + 1] = 0.5
    return out


def average(rows, factor):
    out = np.zeros((rows // factor, rows), np.float32)
    for i in range(rows // factor):
        out[i, i * factor : (i + 1) * factor] = 1.0 / factor
    return out


def level_sizes(piece, far_levels, local_top):
    return tuple(piece >> level for level in range(local_top)) + (16,) * far_levels


def far_constants(seqs):
    out = np.zeros((seqs * 16, seqs * (8 + 16 + 8 + 8)), np.float32)
    starts = (0, seqs * 8, seqs * 24, seqs * 32)
    for seq in range(seqs):
        for slot in range(4):
            for i in range(4):
                row = seq * 16 + slot * 4 + i
                if slot == 1:
                    at = starts[1] + seq * 16 + 4 * i
                    out[row, at : at + 4] = 0.25
                else:
                    at = starts[slot] + seq * 8 + 2 * i
                    out[row, at : at + 2] = 0.5
    return out


def lane_a(rows):
    return lax.broadcasted_iota(jnp.int32, (rows, 128), 1) < 64


def stacked(block, sizes):
    in_a = lane_a(block.shape[0])
    zero = jnp.zeros_like(block)
    head_a = jnp.where(in_a, block, zero)
    head_b = jnp.where(in_a, zero, block)
    parts = []
    at = 0
    for size in sizes:
        parts.append(head_a[at : at + size])
        parts.append(head_b[at : at + size])
        at += size
    return parts


def blocked(parts):
    levels = len(parts) // 2
    rows = []
    for level in range(2, levels):
        block = jnp.concatenate(parts[2 * level : 2 * level + 2], axis=0)
        zero = jnp.zeros_like(block)
        rows.append(
            jnp.concatenate(
                [block if other == level else zero for other in range(2, levels)], axis=1
            )
        )
    return jnp.concatenate(rows, axis=0)


def queries_of(plain_ref, averaged_ref, pair, levels):
    piece = plain_ref.shape[0]
    lanes = slice(pair * 128, pair * 128 + 128)
    rest = jnp.concatenate(
        [averaged_ref[(level - 1) * piece : level * piece, lanes] for level in range(2, levels)],
        axis=1,
    )
    return plain_ref[:, lanes], averaged_ref[0:piece, lanes], rest


def far_rows_of(refs):
    return jnp.concatenate([ref[...].astype(F32) for ref in refs], axis=0)


def pick_far(source_ref, seq, far_rows, seqs):
    parts = []
    at = 0
    for n in far_rows:
        parts.append(source_ref[pl.ds(pl.multiple_of(at + seq * n, n), n), :])
        at += seqs * n
    return jnp.concatenate(parts, axis=0)


def even_average(rows, factor):
    row = lax.broadcasted_iota(jnp.int32, (rows // factor, rows), 0)
    column = lax.broadcasted_iota(jnp.int32, (rows // factor, rows), 1)
    return jnp.where(column // factor == row, 1.0 / factor, 0.0).astype(BF16)


def made_kernel(
    averaged_ref, wide_ref, coarse_ref, coarse_t_ref, mask_ref, ones_ref, *, sizes, local_top
):
    piece = wide_ref.shape[0]
    shape = (piece, piece)
    row = lax.broadcasted_iota(jnp.int32, shape, 0)
    column = lax.broadcasted_iota(jnp.int32, shape, 1)
    for level in range(1, len(sizes)):
        part = jnp.where(row >> level == column >> level, 0.5**level, 0.0).astype(BF16)
        averaged_ref[(level - 1) * piece : level * piece, :] = part
        wide_ref[:, (level - 1) * piece : level * piece] = part
    coarse = [even_average(piece, 2**level) for level in range(1, local_top)]
    coarse_ref[...] = jnp.concatenate(coarse, axis=0)
    at = 0
    for level in range(1, local_top):
        shape = (piece, sizes[level])
        row = lax.broadcasted_iota(jnp.int32, shape, 0)
        column = lax.broadcasted_iota(jnp.int32, shape, 1)
        part = jnp.where(row >> level == column, 0.5**level, 0.0).astype(BF16)
        coarse_t_ref[:, at : at + sizes[level]] = part
        at += sizes[level]
    row = lax.broadcasted_iota(jnp.int32, mask_ref.shape, 0)
    column = lax.broadcasted_iota(jnp.int32, mask_ref.shape, 1)
    keep = column >= 0
    at = 0
    for level in range(local_top):
        key = (column - at) % sizes[level]
        block = (row >> level) // 16
        if level == 0:
            good = block // 2 == key // 32
        else:
            good = block + 1 - 2 * (block % 2) == key // 16
        inside = (column >= at) & (column < at + 2 * sizes[level])
        keep = keep & (good | jnp.logical_not(inside))
        at += 2 * sizes[level]
    mask_ref[...] = jnp.where(keep, 1.0, 0.0)
    at = 0
    for level, size in enumerate(sizes):
        left = lax.broadcasted_iota(jnp.int32, (size, 128), 1) < 64
        ones_ref[at : at + size, :] = jnp.where(left, 2.0**level, 0.0).astype(BF16)
        ones_ref[at + size : at + 2 * size, :] = jnp.where(left, 0.0, 2.0**level).astype(BF16)
        at += 2 * size


def norm_kernel(x_ref, base_ref, next_ref):
    rows = x_ref.shape[0]
    unit, _ = unit_of(x_ref[...].astype(F32))
    base = dot(even_average(rows, rows // base_ref.shape[0]), unit.astype(BF16)).astype(BF16)
    base_ref[...] = base
    next_ref[...] = dot(even_average(base.shape[0], 2), base).astype(BF16)


def pack_kernel(out_ref, up_ref, down_ref, pack_ref):
    width = out_ref.shape[1]
    pack_ref[:, 0:width] = out_ref[...]
    at = width + up_ref.shape[1]
    pack_ref[:, width:at] = up_ref[...]
    for row in range(0, down_ref.shape[0], 16):
        pack_ref[:, at : at + width] = down_ref[row : row + 16, :]
        at += width


def far_kernel(own_ref, one_ref, two_ref, three_ref, gather_ref, pair_ref, five_ref, six_ref):
    rows = far_rows_of((own_ref, one_ref, two_ref, three_ref)).astype(BF16)
    five = dot(gather_ref[...], rows).astype(BF16)
    five_ref[...] = five
    six_ref[...] = dot(pair_ref[...], five).astype(BF16)


def far_back_kernel(
    five_ref, six_a_ref, six_b_ref, one_ref, two_ref, three_ref, spread_ref, pair_ref,
    own_out, one_out, two_out, three_out,
):
    six = (six_a_ref[...].astype(F32) + six_b_ref[...].astype(F32)).astype(BF16)
    five = (five_ref[...].astype(F32) + dot(pair_ref[...], six)).astype(BF16)
    rows = dot(spread_ref[...], five)
    own = own_out.shape[0]
    one = own + one_ref.shape[0]
    two = one + two_ref.shape[0]
    own_out[...] = rows[:own]
    one_out[...] = (rows[own:one] + one_ref[...].astype(F32)).astype(BF16)
    two_out[...] = (rows[one:two] + two_ref[...].astype(F32)).astype(BF16)
    three_out[...] = (rows[two:] + three_ref[...].astype(F32)).astype(BF16)


def mix_kernel(*refs):
    x_ref = refs[0]
    parts = refs[1:5]
    groups_ref = refs[5]
    far_refs = refs[6:-7]
    vec_ref, q_ref, k_ref, v_ref, kf_ref, vf_ref, weight_ref = refs[-7:]
    width = x_ref.shape[1]
    take_groups(parts, groups_ref, weight_ref, MIX_TABLE)
    unit, _ = unit_of(x_ref[...].astype(F32))
    far = far_rows_of(far_refs)
    small = weight_ref[:, :, 3 * width :].reshape(GROUPS * SMALL, 128)
    plain = expand_small(small, width, width // GROUPS)[0]
    biases = expand_small(small, width, 2 * width // GROUPS)
    ups = expand_small(small, width, 4 * width // GROUPS)
    vec_ref[...] = jnp.concatenate(
        [plain[0:6], biases[0][6:7], biases[1][6:7]]
        + [up[7:8] for up in ups]
        + [jnp.zeros((4, width), F32)],
        axis=0,
    )
    gain, shift = plain[0:1], plain[1:2]
    query_bias, value_bias = biases[0][6:7], biases[1][6:7]
    normed = (unit * gain + shift).astype(BF16)
    far = (far * gain + shift).astype(BF16)
    weight = weight_ref[:, :, 0:width].reshape(width, width)
    queries = (dot(normed, weight) + query_bias).astype(BF16).astype(F32)
    q_ref[...] = (queries * 0.125).astype(BF16)
    weight = weight_ref[:, :, width : 2 * width].reshape(width, width)
    k_ref[...] = dot(normed, weight).astype(BF16)
    kf_ref[...] = dot(far, weight)
    weight = weight_ref[:, :, 2 * width : 3 * width].reshape(width, width)
    v_ref[...] = (dot(normed, weight) + value_bias).astype(BF16)
    vf_ref[...] = dot(far, weight) + value_bias


def attention_kernel(
    q_ref, k_ref, v_ref, kf_ref, vf_ref, averaged_ref, coarse_ref, mask_ref, ones_ref,
    kall_ref, vall_ref, p_ref, att_ref, rden_ref,
    qe_ref,
    *, far_rows, sizes, local_top,
):
    piece, width = q_ref.shape
    levels = len(sizes)
    seq = pl.program_id(0)
    count = kf_ref.shape[0] // sum(far_rows)
    queries = q_ref[...]
    qe_ref[...] = dot(averaged_ref[...], queries).astype(BF16)
    keys = k_ref[...]
    values = v_ref[...]
    coarse_keys = dot(coarse_ref[...], keys).astype(BF16)
    coarse_values = dot(coarse_ref[...], values)
    scaled = [values]
    at = 0
    for level in range(1, local_top):
        scaled.append((coarse_values[at : at + sizes[level]] * 2.0**level).astype(BF16))
        at += sizes[level]
    far_values = pick_far(vf_ref, seq, far_rows, count)
    for level in range(local_top, levels):
        at = 16 * (level - local_top)
        scaled.append((far_values[at : at + 16] * 2.0**level).astype(BF16))
    kall_ref[0] = jnp.concatenate(
        [keys, coarse_keys, pick_far(kf_ref, seq, far_rows, count).astype(BF16)], axis=0
    )
    vall_ref[0] = jnp.concatenate(scaled, axis=0)
    for pair in range(width // 128):
        lanes = slice(pair * 128, pair * 128 + 128)
        plain, one, rest = queries_of(q_ref, qe_ref, pair, levels)
        key_parts = stacked(kall_ref[0, :, lanes], sizes)
        scores = jnp.concatenate(
            [
                dot_right(plain, jnp.concatenate(key_parts[0:2], axis=0)),
                dot_right(one, jnp.concatenate(key_parts[2:4], axis=0)),
                dot_right(rest, blocked(key_parts)),
            ],
            axis=1,
        )
        weights = jnp.where(mask_ref[...] > 0.0, jnp.exp(scores), 0.0).astype(BF16)
        p_ref[0, pair] = weights
        both = jnp.concatenate(
            [jnp.concatenate(stacked(vall_ref[0, :, lanes], sizes), axis=0), ones_ref[...]], axis=1
        )
        sums = dot(weights, both)
        rden = 1.0 / sums[:, 128:]
        rden_ref[:, lanes] = rden
        att_ref[:, lanes] = (sums[:, :128] * rden).astype(BF16)


def feed_kernel(
    vec_ref, table_ref, x_ref, cot_ref, att_ref, part_one, part_two, part_three, part_four,
    out_ref, dmid_ref, datt_ref, sum_ref, first_out, second_out,
    weight_ref,
):
    width = x_ref.shape[1]
    blocks = (weight_ref.shape[2] // width - 1) // 2
    take_groups((part_one, part_two, part_three, part_four), table_ref, weight_ref)
    gain = vec_ref[3:4, :]
    out_weight = weight_ref[:, :, 0:width].reshape(width, width)
    middle = x_ref[...].astype(F32) + dot(att_ref[...], out_weight) + vec_ref[2:3, :]
    unit, inverse = unit_of(middle)
    normed = (unit * gain + vec_ref[4:5, :]).astype(BF16)
    g_out = cot_ref[...]
    result = middle + vec_ref[5:6, :]
    d_two = jnp.zeros(x_ref.shape, F32)
    tiles = width // 128
    per_group = blocks * width // GROUPS // 16
    groups = GROUPS // blocks
    sums = []
    for block in range(blocks):
        up = weight_ref[:, :, width * (block + 1) : width * (block + 2)].reshape(width, width)
        down = jnp.concatenate(
            [
                weight_ref[groups * block + group, :, width * at : width * (at + 1)]
                for group in range(groups)
                for at in range(blocks + 1, blocks + 1 + per_group)
            ],
            axis=0,
        )
        pre = dot(normed, up) + vec_ref[8 + block : 9 + block, :]
        cdf = 0.5 + 0.5 * lax.erf(pre * 0.7071067811865476)
        hidden = (pre * cdf).astype(BF16)
        slope = cdf + pre * (0.3989422804014327 * jnp.exp(-0.5 * pre * pre))
        result = result + dot(hidden, down)
        grad = dot_left(hidden, g_out).reshape(groups, per_group, 16, width)
        for part in range(per_group):
            give_lanes(
                grad[:, part].reshape(-1, width), first_out, second_out, table_ref,
                tiles * (blocks + 1 + part), groups // 2 * block,
            )
        g_pre = (dot_right(g_out, down) * slope).astype(BF16)
        sums.append(column_sum(g_pre.astype(F32)))
        grad = dot_left(normed, g_pre)
        give_lanes(grad, first_out, second_out, table_ref, tiles * (block + 1))
        d_two = d_two + dot_right(g_pre, up)
    out_ref[...] = result.astype(BF16)
    cot = g_out.astype(F32)
    d_middle = cot + norm_back(d_two, unit, inverse, gain)
    dmid_ref[...] = d_middle
    branch = d_middle.astype(BF16)
    datt_ref[...] = dot_right(branch, out_weight)
    give_lanes(dot_left(att_ref[...], branch), first_out, second_out, table_ref, 0)
    sum_ref[...] = jnp.concatenate(
        [
            jnp.zeros((2, width), F32),
            column_sum(branch.astype(F32)),
            column_sum(d_two * unit),
            column_sum(d_two),
            column_sum(cot),
            jnp.zeros((2, width), F32),
        ]
        + sums
        + [jnp.zeros((8 - blocks, width), F32)],
        axis=0,
    )


def attention_back_kernel(
    q_ref, kall_ref, vall_ref, p_ref, att_ref, rden_ref, datt_ref, averaged_ref, wide_ref,
    coarse_t_ref, ones_ref,
    dq_ref, dk_ref, dv_ref, dkf_ref, dvf_ref,
    qe_ref, dkall_ref, dvall_ref, t_ref, dqacc_ref,
    *, sizes, local_top,
):
    piece, width = q_ref.shape
    levels = len(sizes)
    starts = np.concatenate([[0], np.cumsum(sizes)]).tolist()
    local = starts[local_top]

    qe_ref[...] = dot(averaged_ref[...], q_ref[...]).astype(BF16)
    near = 2 * sizes[0]
    mid = near + 2 * sizes[1]
    for pair in range(width // 128):
        lanes = slice(pair * 128, pair * 128 + 128)
        plain, one, rest = queries_of(q_ref, qe_ref, pair, levels)
        key_parts = stacked(kall_ref[0, :, lanes], sizes)
        both = jnp.concatenate(
            [jnp.concatenate(stacked(vall_ref[0, :, lanes], sizes), axis=0), ones_ref[...]], axis=1
        )
        d_num = datt_ref[:, lanes] * rden_ref[:, lanes]
        d_den = -d_num * att_ref[:, lanes].astype(F32)
        d_num = d_num.astype(BF16)
        weights = p_ref[0, pair]
        d_weights = dot_right(jnp.concatenate([d_num, d_den.astype(BF16)], axis=1), both)
        d_scores = (weights.astype(F32) * d_weights).astype(BF16)
        d_key_near = dot_left(d_scores[:, :near], plain)
        d_key_mid = dot_left(d_scores[:, near:mid], one)
        d_key_rest = dot_left(d_scores[:, mid:], rest)
        d_value = dot_left(weights, d_num)
        dqacc_ref[:, lanes] = dot(d_scores[:, :near], jnp.concatenate(key_parts[0:2], axis=0))
        t_ref[0:piece, lanes] = dot(
            d_scores[:, near:mid], jnp.concatenate(key_parts[2:4], axis=0)
        ).astype(BF16)
        d_rest = dot(d_scores[:, mid:], blocked(key_parts)).astype(BF16)
        at = 0
        for level in range(levels):
            size = sizes[level]
            low, high = starts[level], starts[level + 1]
            in_a = lane_a(size)
            if level == 0:
                source = d_key_near
            elif level == 1:
                source = d_key_mid
            else:
                block = slice((level - 2) * 128, (level - 1) * 128)
                source = d_key_rest[at - mid : at - mid + 2 * size, block]
                t_ref[(level - 1) * piece : level * piece, lanes] = d_rest[:, block]
            dkall_ref[low:high, lanes] = jnp.where(in_a, source[:size], source[size:])
            values = d_value[at : at + 2 * size]
            dvall_ref[low:high, lanes] = jnp.where(in_a, values[:size], values[size:]) * 2.0**level
            at += 2 * size
    dq_ref[...] = ((dqacc_ref[...] + dot(wide_ref[...], t_ref[...])) * 0.125).astype(BF16)
    for target, source in ((dk_ref, dkall_ref), (dv_ref, dvall_ref)):
        spread = dot(coarse_t_ref[...], source[piece:local, :].astype(BF16))
        target[...] = (source[0:piece, :] + spread).astype(BF16)
    dkf_ref[0] = dkall_ref[local:, :]
    dvf_ref[0] = dvall_ref[local:, :]


def mix_back_kernel(*refs, far_rows):
    fars = len(far_rows)
    x_ref, vec_ref, sum_ref = refs[:3]
    parts = refs[3:7]
    groups_ref = refs[7]
    grad_refs = [refs[8 + 2 * i : 10 + 2 * i] for i in range(5)]
    far_refs = refs[18 : 18 + fars]
    scaled_ref, first_ref, second_ref = refs[18 + fars : 21 + fars]
    dfar_refs = refs[21 + fars : 21 + 2 * fars]
    weight_ref = refs[-1]
    width = x_ref.shape[1]
    grads = [jnp.concatenate([ref[...] for ref in pair], axis=0) for pair in grad_refs[:3]]

    def by_ref(pair):
        rows = []
        at = 0
        for n in far_rows:
            for ref in pair:
                rows += [ref[seq, at : at + n, :] for seq in range(ref.shape[0])]
            at += n
        return jnp.concatenate(rows, axis=0)

    take_groups(parts, groups_ref, weight_ref, MIX_TABLE)
    gain = vec_ref[0:1, :]
    shift = vec_ref[1:2, :]
    unit, _ = unit_of(x_ref[...].astype(F32))
    normed = (unit * gain + shift).astype(BF16)
    far = far_rows_of(far_refs)
    far_normed = (far * gain + shift).astype(BF16)
    both = jnp.concatenate([normed, far_normed], axis=0)
    far_values = by_ref(grad_refs[4])
    far_grads = (None, by_ref(grad_refs[3]).astype(BF16), far_values.astype(BF16))
    d_one = jnp.zeros(x_ref.shape, F32)
    d_far = jnp.zeros(far.shape, F32)
    for part in range(3):
        lanes = slice(part * width, part * width + width)
        weight = weight_ref[:, :, lanes].reshape(width, width)
        d_one = d_one + dot_right(grads[part], weight)
        if part == 0:
            grad = dot_left(normed, grads[part])
        else:
            d_far = d_far + dot_right(far_grads[part], weight)
            grad = dot_left(both, jnp.concatenate([grads[part], far_grads[part]], axis=0))
        at = part * width // 128
        give_lanes(grad, first_ref, second_ref, groups_ref, at, table=MIX_BACK_TABLE)
    scaled_ref[...] = d_one * gain
    at = 0
    for ref in dfar_refs:
        ref[...] = (d_far[at : at + ref.shape[0]] * gain).astype(BF16)
        at += ref.shape[0]
    vectors = jnp.concatenate(
        [
            column_sum(d_one * unit) + column_sum(d_far * far),
            column_sum(d_one) + column_sum(d_far),
            sum_ref[2:6, :],
            column_sum(grads[0].astype(F32)),
            column_sum(grads[2].astype(F32)) + column_sum(far_values),
            sum_ref[8:16, :],
        ],
        axis=0,
    )
    chunk = width // GROUPS
    small = shrink_vectors(vectors, ((chunk, 0, 6), (2 * chunk, 6, 8), (4 * chunk, 8, 12)))
    at = 3 * width // 128
    give_lanes(small, first_ref, second_ref, groups_ref, at, table=MIX_BACK_TABLE)


def input_kernel(
    x_ref, dmid_ref, scaled_ref, own_ref, one_ref, two_ref, three_ref, pair_ref, spread_ref,
    din_ref,
):
    unit, inverse = unit_of(x_ref[...].astype(F32))
    lower = own_ref[...] + two_ref[...].astype(F32) + three_ref[...].astype(F32)
    base = one_ref[...].astype(F32) + dot(pair_ref[...], lower.astype(BF16))
    scaled = scaled_ref[...] + dot(spread_ref[...], base.astype(BF16))
    inner = (
        scaled
        - jnp.mean(scaled, axis=-1, keepdims=True)
        - unit * jnp.mean(scaled * unit, axis=-1, keepdims=True)
    )
    din_ref[...] = dmid_ref[...] + inner * inverse


def last_kernel(
    mix_one, mix_two, mix_three, mix_four, feed_ref, other_feed_ref,
    matrix_ref, out_ref, up_ref, down_ref, *vector_refs,
):
    total = feed_ref[0].astype(F32) + other_feed_ref[0].astype(F32)
    at = 0
    for ref in (out_ref, up_ref):
        for lane in range(0, ref.shape[1], 128):
            ref[:, lane : lane + 128] = total[at]
            at += 1
    for row in range(0, down_ref.shape[0], 16):
        for lane in range(0, down_ref.shape[1], 128):
            down_ref[row : row + 16, lane : lane + 128] = total[at]
            at += 1
    total = mix_one[0].astype(F32) + mix_two[0].astype(F32)
    total += mix_three[0].astype(F32) + mix_four[0].astype(F32)
    for lane in range(0, matrix_ref.shape[1], 128):
        matrix_ref[:, lane : lane + 128] = total[lane // 128]
    small = total[matrix_ref.shape[1] // 128]
    for i in range(6):
        vector_refs[i][...] = small[i : i + 1, : vector_refs[i].shape[1]]
    vector_refs[6][...] = column_sum(small[6:8])[:, : vector_refs[6].shape[1]]
    vector_refs[7][...] = column_sum(small[8:12])[:, : vector_refs[7].shape[1]]


def vmem():
    return pl.BlockSpec(memory_space=pltpu.VMEM)


def anywhere():
    return pl.BlockSpec(memory_space=pl.ANY)


def scalars():
    return pl.BlockSpec(memory_space=pltpu.SMEM)


def fixed(*dims):
    return pl.BlockSpec(dims, lambda i: (0,) * len(dims))


def moving(*dims):
    return pl.BlockSpec(dims, lambda i: (i,) + (0,) * (len(dims) - 1))


def shape(dims, dtype):
    return jax.ShapeDtypeStruct(dims, dtype)


def const(values):
    return jnp.asarray(values, BF16)


def bit_orders():
    return ((8, 4, 16, 2), (2, 8, 4, 16))


def mix_orders():
    return ((8, 4, 16, 2), (8, 4, 16, 2))


def mix_back_orders():
    return ((8, 4, 16, 2), (8, 4, 2, 16))


def slot_offset(slot, order):
    return sum(bit for k, bit in enumerate(order) if slot >> k & 1)


def group_table(orders):
    table = np.zeros((32, 128), np.int32)
    for device in range(32):
        core = device & 1
        table[device, GROUPS] = core
        for slot in range(16):
            table[device, (device ^ slot_offset(slot, orders[core])) // 2] = slot
            group = device ^ 1 ^ slot_offset(slot, orders[1 - core])
            table[device, GROUPS // 2 + group // 2] = slot
    return table


def exchange(value, bits):
    if isinstance(bits, int):
        bits = (bits, bits)
    count = lax.axis_size(AXES)
    return lax.ppermute(value, AXES, [(i, i ^ bits[i & 1]) for i in range(count)])


def after(value, *others):
    return lax.optimization_barrier((value,) + others)[0]


def added(*parts):
    total = parts[0].astype(F32)
    for part in parts[1:]:
        total = total + part.astype(F32)
    return total.astype(BF16)


def send(buffer, k, orders=None):
    orders = orders or bit_orders()
    return exchange(buffer, (orders[0][k], orders[1][k]))


def halves(kept, other):
    half = kept.shape[0] // 2
    return added(kept[:half], other[:half]), added(kept[half:], other[half:])


def joined(buffer, other):
    return jnp.concatenate([buffer, other], axis=0)


def call(kernel, name, outs, ins, args, work, scratch=(), grid=None, room=6):
    return pl.pallas_call(
        kernel,
        out_shape=tuple(item[0] for item in outs),
        in_specs=list(ins),
        out_specs=tuple(item[1] for item in outs),
        scratch_shapes=list(scratch),
        compiler_params=pltpu.CompilerParams(vmem_limit_bytes=room * MIB),
        cost_estimate=pl.CostEstimate(flops=work, bytes_accessed=work >> 9, transcendentals=0),
        name=name,
        **({} if grid is None else {"grid": grid}),
    )(*args)


def coarsen(values):
    return (values[:, 0::2] + values[:, 1::2]) * 0.5


def whole_far(base, seqs, far_levels, position):
    rows = base.reshape(seqs, 16, base.shape[1])
    full = lax.all_gather(rows, "seq", axis=1, tiled=True).astype(F32)
    parts = []
    for extra in range(far_levels):
        partner = (position // 2**extra) ^ 1
        parts.append(lax.dynamic_slice_in_dim(full, partner * 16, 16, axis=1))
        if extra + 1 < far_levels:
            full = coarsen(full)
    return jnp.concatenate(parts, axis=1).astype(BF16).reshape(seqs * 16 * far_levels, -1)


def whole_far_back(grad, seqs, far_levels, position):
    stack = grad.reshape(seqs, far_levels, 16, -1).astype(F32)
    ids = jnp.arange(far_levels).reshape(1, far_levels, 1, 1)
    count = lax.axis_size("seq")
    for bit in range(far_levels):
        pairs = [(i, i ^ 1 << bit) for i in range(count)]
        other = lax.ppermute(stack.astype(BF16), "seq", pairs).astype(F32)
        stack = jnp.where(ids > bit, stack + other, jnp.where(ids == bit, other, stack))
    own = jnp.zeros((seqs, 16, stack.shape[-1]), F32)
    for extra in range(far_levels):
        rows = 16 >> extra
        offset = position % 2**extra * rows
        part = lax.dynamic_slice_in_dim(stack[:, extra], offset, rows, axis=1)
        own = own + jnp.repeat(part, 2**extra, axis=1) * 0.5**extra
    return own.reshape(seqs * 16, -1).astype(BF16)


def body(
    layer_input, qkv_weight, qv_bias, out_weight, out_bias, first_gain, first_shift, second_gain,
    second_shift, up_weight, up_bias, down_weight, down_bias, cotangent,
):
    batches, per_batch, piece, width = layer_input.shape
    seqs = batches * per_batch
    tokens = seqs * piece
    hidden = up_weight.shape[1]
    blocks = hidden // width
    devices = lax.axis_size(AXES)
    pieces = lax.axis_size("seq")
    position = lax.axis_index("seq")
    far_levels = pieces.bit_length() - 1
    local_top = (piece // 16).bit_length() - 1
    fast = devices == GROUPS and pieces == 16
    x = layer_input.reshape(tokens, width)
    cot = cotangent.reshape(tokens, width)
    sizes = level_sizes(piece, far_levels, local_top)
    keys = sum(sizes)
    flat = (tokens, width)
    base_rows = seqs * 16
    coarse_all = np.kron(np.eye(seqs, dtype=np.float32), average(piece, piece // 16))
    pair = np.kron(np.eye(seqs, dtype=np.float32), pair_average(16))
    gather_far = far_constants(seqs)
    vectors = (
        first_gain, first_shift, out_bias, second_gain, second_shift, down_bias, qv_bias, up_bias,
    )

    if fast:
        me = lax.axis_index(AXES)
        orders = (bit_orders(), mix_orders(), mix_back_orders())
        table = np.concatenate([group_table(item) for item in orders], axis=1)
        groups = lax.dynamic_slice_in_dim(jnp.asarray(table), me, 1, axis=0)
    if fast:
        (pack_b,) = call(
            pack_kernel,
            "pack",
            [(shape((16, width + 2 * hidden), BF16), vmem())],
            [vmem()] * 3,
            (out_weight, up_weight, down_weight),
            1 << 16,
            room=60,
        )
    base, below = call(
        norm_kernel,
        "norm",
        [(shape((base_rows, width), BF16), vmem()), (shape((base_rows // 2, width), BF16), vmem())],
        [vmem()],
        (after(x, groups, pack_b) if fast else x,),
        1 << 20,
    )
    coarse_rows = sum(sizes[1:local_top])
    top = len(sizes) - 1
    made = (
        ((top * piece, piece), BF16),
        ((piece, top * piece), BF16),
        ((coarse_rows, piece), BF16),
        ((piece, coarse_rows), BF16),
        ((piece, 2 * keys), F32),
        ((2 * keys, 128), BF16),
    )
    averaged, averaged_wide, coarse, coarse_t, mask, ones = call(
        partial(made_kernel, sizes=sizes, local_top=local_top),
        "made",
        [(shape(*item), vmem()) for item in made],
        [],
        (),
        1 << 20,
    )

    if fast:
        a = jnp.pad(qkv_weight, ((0, 0), (0, 128)))
        for row, vector in enumerate(vectors):
            item = vector.reshape(1, -1)
            lanes = (3 * width, 128 - item.shape[1])
            a = a + jnp.pad(item, ((row, SMALL - 1 - row), lanes))
        a = a[None]
        b = pack_b[None]
        other_a = send(a, 0, mix_orders())
        other_b = send(b, 0)
        a = joined(a, other_a)
        other_a = send(after(a, base), 1, mix_orders())
        a = joined(a, other_a)
        other_a = send(a, 2, mix_orders())
        b = joined(after(b, a), other_b)
        other_b = send(b, 1)
        near, half = after(base, a), after(below, a)
        one, two, three = exchange(near, 1), exchange(half, 2), exchange(half, 3)
        a = joined(a, other_a)
        a = after(a, one, two, three)
        other_a = send(a, 3, mix_orders())
        five, six = call(
            far_kernel,
            "far",
            [
                (shape((base_rows, width), BF16), vmem()),
                (shape((base_rows // 2, width), BF16), vmem()),
            ],
            [vmem()] * 6,
            (after(below, a, mask), one, two, three, const(gather_far), const(pair)),
            1 << 20,
        )
        far = (one, two, three, exchange(five, 4), exchange(six, 8), exchange(six, 12))
        far_rows = (16, 8, 8, 16, 8, 8)
        b = joined(after(b, a), other_b)
        other_b = send(b, 2)
        lower = exchange(after(a, five), 1)
        other_a = after(other_a, five, six)
        parts_a = (a, other_a, lower, exchange(other_a, 1))
        b = joined(after(b, other_a, *far), other_b)
        other_b = send(b, 3)
        lower = exchange(after(b, other_a), 1)
    else:
        groups = [slot % (GROUPS // 2) for slot in range(GROUPS)] + [0] * (128 - GROUPS)
        groups = jnp.asarray([groups * 3], jnp.int32)

        def whole(value):
            return lax.all_gather(value, AXES, axis=0, tiled=True).reshape(
                (GROUPS, -1) + value.shape[1:]
            )

        small = [jnp.pad(v, ((0, 0), (0, 128 - v.shape[1]))) for v in map(whole, vectors)]
        small += [jnp.zeros((GROUPS, 128), BF16)] * (SMALL - len(small))
        gathered_a = jnp.concatenate([whole(qkv_weight), jnp.stack(small, axis=1)], axis=2)
        downs = whole(down_weight).reshape(GROUPS, -1, 16, width).transpose(0, 2, 1, 3)
        parts = [whole(out_weight), whole(up_weight), downs.reshape(GROUPS, 16, -1)]
        gathered_b = jnp.concatenate(parts, axis=2)

        def quarters(item):
            return item[0:16:2], item[16::2], item[1:16:2], item[17::2]

        parts_a, parts_b = quarters(gathered_a), quarters(gathered_b)
        far = (whole_far(base, seqs, far_levels, position),)
        far_rows = (16 * far_levels,)

    lanes_a = 3 * width + 128
    tiles_a = lanes_a // 128
    tiles_b = (width + 2 * hidden) // 128
    top = len(sizes) - 1
    pairs = width // 128
    total_far = seqs * 16 * far_levels
    half_a = shape((GROUPS // 2, tiles_a, 16, 128), BF16)
    half_b = shape((GROUPS // 2, tiles_b, 16, 128), BF16)
    far_flat = shape((total_far, width), F32)
    low, high = shape(flat, BF16), shape(flat, F32)
    sixteen = shape((16, width), F32)
    level = dict(far_rows=far_rows, sizes=sizes, local_top=local_top)

    vec, queries, key, value, far_key, far_value = call(
        mix_kernel,
        "mix",
        [(sixteen, vmem())] + [(low, vmem())] * 3 + [(far_flat, vmem())] * 2,
        [vmem()] * 5 + [scalars()] + [vmem()] * len(far),
        (x, *parts_a, groups, *far),
        1 << 24,
        [pltpu.VMEM((GROUPS, 16, lanes_a), BF16)],
        room=14,
    )
    rows_spec = moving(piece, width)
    keys_spec = moving(1, keys, width)
    p_spec = moving(1, pairs, piece, 2 * keys)
    keys_shape = shape((seqs, keys, width), BF16)
    kall, vall, weights, attended, rden = call(
        partial(attention_kernel, **level),
        "attention",
        [
            (keys_shape, keys_spec),
            (keys_shape, keys_spec),
            (shape((seqs, pairs, piece, 2 * keys), BF16), p_spec),
            (low, rows_spec),
            (high, rows_spec),
        ],
        [rows_spec] * 3
        + [fixed(total_far, width)] * 2
        + [
            fixed(top * piece, piece),
            fixed(coarse_rows, piece),
            fixed(piece, 2 * keys),
            fixed(2 * keys, 128),
        ],
        (
            queries, key, value, far_key, far_value, averaged, coarse, mask, ones,
        ),
        1 << 24,
        [pltpu.VMEM((top * piece, width), BF16)],
        (seqs,),
        room=12,
    )
    if fast:
        other_b = after(other_b, attended)
        parts_b = (b, other_b, lower, exchange(other_b, 1))

    result, d_middle, d_attended, sums, kept_b, sent_b = call(
        feed_kernel,
        "feed",
        [(low, vmem()), (high, vmem()), (high, vmem()), (sixteen, vmem())] + [(half_b, vmem())] * 2,
        [vmem(), scalars()] + [vmem()] * 7,
        (vec, groups, x, cot, attended, *parts_b),
        8 << 30,
        [
            pltpu.VMEM((GROUPS, 16, width + 2 * hidden), BF16),
        ],
        room=30,
    )
    def back_call(seq, count, d_attended):
        def later(*dims):
            return pl.BlockSpec(dims, lambda i: (i + seq,) + (0,) * (len(dims) - 1))

        rows, wide_keys = later(piece, width), later(1, keys, width)
        half = (shape((count * piece, width), BF16), rows_spec)
        far_half = shape((count, keys - local, width), F32), moving(1, keys - local, width)
        return call(
            partial(attention_back_kernel, sizes=sizes, local_top=local_top),
            "attention_back",
            [half] * 3 + [far_half] * 2,
            [rows, wide_keys, wide_keys, later(1, pairs, piece, 2 * keys), rows, rows, rows]
            + [
                fixed(top * piece, piece),
                fixed(piece, top * piece),
                fixed(piece, coarse_rows),
                fixed(2 * keys, 128),
            ],
            (
                queries, kall, vall, weights, attended, rden, d_attended, averaged, averaged_wide,
                coarse_t, ones,
            ),
            6 << 30,
            [
                pltpu.VMEM((top * piece, width), BF16),
                pltpu.VMEM((keys, width), F32),
                pltpu.VMEM((keys, width), F32),
                pltpu.VMEM((top * piece, width), BF16),
                pltpu.VMEM((piece, width), F32),
            ],
            (count,),
            room=16,
        )

    local = sum(sizes[:local_top])
    if fast:
        late = exchange(sent_b[12:], 1)
        rest = exchange(after(sent_b, late)[:12], 1)
        upper_b = added(kept_b[12:], late)
        late_b = send(upper_b, 3)
        d_attended = after(d_attended, upper_b)
    most = max(1, seqs * 3 // 4)
    back_one = back_call(0, most, d_attended)
    if fast:
        rest, *back_one = lax.optimization_barrier((rest, *back_one))
        upper_b = added(kept_b[8:12], rest[8:])
        early_b = send(upper_b, 3)
        d_attended = after(d_attended, upper_b)
    back_two = back_call(most, seqs - most, d_attended)
    outs = call(
        partial(mix_back_kernel, far_rows=far_rows),
        "mix_back",
        [(high, vmem())]
        + [(half_a, vmem())] * 2
        + [(shape(item.shape, BF16), vmem()) for item in far],
        [vmem()] * 7 + [scalars()] + [vmem()] * (10 + len(far)),
        (
            x, vec, sums, *parts_a, groups,
            *[item for pair in zip(back_one, back_two) for item in pair], *far,
        ),
        16 << 30,
        [pltpu.VMEM((GROUPS, 16, lanes_a), BF16)],
        room=24,
    )
    scaled, kept_a, sent_a = outs[:3]
    d_far = outs[3:]

    if fast:
        upper_b = added(after(kept_b[4:8], scaled, early_b), rest[4:8], late_b)
        middle_b = send(upper_b, 2)
        other_a = exchange(after(sent_a, upper_b), 1)
        kept_a, upper_a = halves(kept_a, other_a)
        other_a = send(upper_a, 3, mix_back_orders())
        back = [after(item, upper_a) for item in d_far[3:]]
        back = [exchange(item, bits) for item, bits in zip(back, (4, 8, 12))]
        kept_b = added(after(kept_b, upper_a, *back)[:4], rest[:4], early_b, middle_b)
        kept_b, upper_b = kept_b[:2], kept_b[2:]
        other_b = send(upper_b, 1)
        kept_a, upper_a = halves(after(kept_a, upper_b), other_a)
        other_a = send(upper_a, 2, mix_back_orders())
        back = [after(item, upper_b) for item in back]
        own, out_one, out_two, out_three = call(
            far_back_kernel,
            "far_back",
            [
                (shape((base_rows // 2, width), F32), vmem()),
                (shape((base_rows, width), BF16), vmem()),
                (shape((base_rows // 2, width), BF16), vmem()),
                (shape((base_rows // 2, width), BF16), vmem()),
            ],
            [vmem()] * 8,
            (*back, d_far[0], d_far[1], d_far[2], const(gather_far.T), const(pair.T)),
            1 << 20,
        )
        far_one = exchange(out_one, 1)
        far_two = exchange(out_two, 2)
        far_three = exchange(out_three, 3)
        own_a, far_a = halves(after(kept_a, own, other_b), other_a)
        one_a, two_a = own_a[0:1], own_a[1:2]
        lasts_a = (
            one_a,
            exchange(two_a, 8),
            exchange(far_a[0:1], 4),
            exchange(far_a[1:2], 12),
        )
        kept_b, upper_b = halves(after(kept_b, own_a), other_b)
        other_b = send(upper_b, 0)
    else:
        far_one = whole_far_back(d_far[0], seqs, far_levels, position)
        own = jnp.zeros((base_rows // 2, width), F32)
        far_two = far_three = jnp.zeros((base_rows // 2, width), BF16)

    (d_input,) = call(
        input_kernel,
        "input_grad",
        [(high, vmem())],
        [vmem()] * 9,
        (
            x, d_middle, scaled, own, far_one, far_two, far_three, const(pair.T),
            const(coarse_all.T),
        ),
        1 << 20,
    )

    if fast:
        grad_qkv, grad_out_weight, grad_up, grad_down, *plain = call(
            last_kernel,
            "last",
            [
                (shape(item.shape, F32), vmem())
                for item in (qkv_weight, out_weight, up_weight, down_weight)
            ]
            + [(shape((1, v.shape[0]), F32), vmem()) for v in vectors],
            [vmem()] * 6,
            (*lasts_a, kept_b, other_b),
            1 << 16,
        )
        plain = [item.reshape(-1) for item in plain]
        grad_qv, grad_up_bias = plain[6:8]
    else:

        def reduced(item):
            return lax.psum_scatter(item.astype(F32), AXES, scatter_dimension=0, tiled=True)

        def rows_of(item):
            return reduced(item.transpose(0, 2, 1, 3).reshape(GROUPS * 16, -1))

        all_a = jnp.stack([kept_a, sent_a], axis=1).reshape(GROUPS, *half_a.shape[1:])
        all_b = jnp.stack([kept_b, sent_b], axis=1).reshape(GROUPS, *half_b.shape[1:])
        grad_qkv = rows_of(all_a[:, :-1])
        small = all_a[:, -1]
        chunk = width // GROUPS
        plain = [reduced(small[:, i, :chunk].reshape(-1)) for i in range(6)]
        grad_qv = reduced(jnp.sum(small[:, 6:8, : 2 * chunk], axis=1).reshape(-1))
        grad_up_bias = reduced(jnp.sum(small[:, 8:12, : 4 * chunk], axis=1).reshape(-1))
        split = width // 128
        grad_out_weight = rows_of(all_b[:, :split])
        grad_up = rows_of(all_b[:, split : split * (blocks + 1)])
        downs = all_b[:, split * (blocks + 1) :].reshape(GROUPS, -1, split, 16, 128)
        grad_down = reduced(downs.transpose(0, 1, 3, 2, 4).reshape(hidden, width))

    return (
        result.reshape(layer_input.shape),
        d_input.reshape(layer_input.shape),
        grad_qkv,
        grad_qv,
        grad_out_weight,
        plain[2],
        plain[0],
        plain[1],
        plain[3],
        plain[4],
        grad_up,
        grad_up_bias,
        grad_down,
        plain[5],
    )


def solution(mesh):
    tokens = P(None, "dp", "seq", None)
    matrix = P(AXES, None)
    vector = P(AXES)
    in_specs = (
        tokens, matrix, vector, matrix, vector, vector, vector, vector, vector, matrix, vector,
        matrix, vector, tokens,
    )
    out_specs = (
        tokens, tokens, matrix, vector, matrix, vector, vector, vector, vector, vector, matrix,
        vector, matrix, vector,
    )
    return jax.shard_map(body, mesh=mesh, in_specs=in_specs, out_specs=out_specs, check_vma=False)
```

```python
from functools import partial

import jax
import jax.numpy as jnp
import numpy as np
from jax import lax
from jax.experimental import pallas as pl
from jax.experimental.pallas import tpu as pltpu
from jax.sharding import PartitionSpec as P

HEADS = 8
AXES = ("dp", "seq")
F32 = jnp.float32
BF16 = jnp.bfloat16
GROUPS = 32
SMALL = 16
EPS = 1e-05
MIB = 1024 * 1024


def dot(left, right):
    return jnp.dot(left, right, preferred_element_type=F32)


def dot_right(left, right):
    return lax.dot_general(left, right, (((1,), (1,)), ((), ())), preferred_element_type=F32)


def dot_left(left, right):
    return lax.dot_general(left, right, (((0,), (0,)), ((), ())), preferred_element_type=F32)


def unit_of(values):
    centred = values - jnp.mean(values, axis=-1, keepdims=True)
    scale = lax.rsqrt(jnp.mean(centred * centred, axis=-1, keepdims=True) + EPS)
    return centred * scale, scale


def norm_back(grad, unit, scale, gain):
    scaled = grad * gain
    inner = (
        scaled
        - jnp.mean(scaled, axis=-1, keepdims=True)
        - unit * jnp.mean(scaled * unit, axis=-1, keepdims=True)
    )
    return inner * scale


def column_sum(values):
    return jnp.sum(values, axis=0, keepdims=True)


def expand_small(small, width, chunk):
    eye = lax.broadcasted_iota(jnp.int32, (128, width), 0) == (
        lax.broadcasted_iota(jnp.int32, (128, width), 1) % chunk
    )
    spread = dot(small, eye.astype(F32).astype(BF16))
    runs = GROUPS * chunk // width
    per_run = GROUPS // runs
    group = lax.broadcasted_iota(jnp.int32, (GROUPS * SMALL, width), 0) // SMALL
    column = lax.broadcasted_iota(jnp.int32, (GROUPS * SMALL, width), 1) // chunk
    kept = jnp.where(group % per_run == column, spread, 0.0).reshape(GROUPS, SMALL, width)
    return [jnp.sum(kept[run * per_run : (run + 1) * per_run], axis=0) for run in range(runs)]


def shrink_vectors(vectors, parts):
    width = vectors.shape[1]
    tiled = jnp.broadcast_to(vectors[None], (GROUPS, SMALL, width)).reshape(-1, width)
    row = lax.broadcasted_iota(jnp.int32, (GROUPS * SMALL, width), 0)
    lane = lax.broadcasted_iota(jnp.int32, (GROUPS * SMALL, width), 1)
    group = row // SMALL
    row = row % SMALL
    total = None
    for chunk, first, end in parts:
        runs = GROUPS * chunk // width
        per_run = GROUPS // runs
        keep = (group % per_run == lane // chunk) & (row >= first) & (row < end)
        if runs > 1:
            keep = keep & (row - first == group // per_run)
        eye = lax.broadcasted_iota(jnp.int32, (width, 128), 0) % chunk == lax.broadcasted_iota(
            jnp.int32, (width, 128), 1
        )
        part = dot(jnp.where(keep, tiled, 0.0).astype(BF16), eye.astype(F32).astype(BF16))
        total = part if total is None else total + part
    return total


MIX_TABLE = 128
MIX_BACK_TABLE = 256


def same_core(table_ref):
    return table_ref[0, GROUPS] == 0


def take_groups(parts, table_ref, target_ref, table=0):
    even = same_core(table_ref)
    half = parts[0].shape[0]

    def slot_of(at, low_ref, high_ref):
        slot = table_ref[0, table + at]
        index = lax.rem(slot, half)
        return jnp.where(slot >= half, high_ref[index], low_ref[index])

    for pair in range(GROUPS // 2):
        mine = slot_of(pair, *parts[0:2])
        other = slot_of(GROUPS // 2 + pair, *parts[2:4])
        target_ref[2 * pair] = jnp.where(even, mine, other)
        target_ref[2 * pair + 1] = jnp.where(even, other, mine)


def give_groups(values, first_ref, second_ref, table_ref, tile, first_pair=0, table=0):
    even = same_core(table_ref)
    for i in range(values.shape[0] // 2):
        pair = first_pair + i
        one, two = values[2 * i], values[2 * i + 1]
        first_ref[table_ref[0, table + pair], tile] = jnp.where(even, one, two)
        second_ref[table_ref[0, table + GROUPS // 2 + pair], tile] = jnp.where(even, two, one)


def give_lanes(values, first_ref, second_ref, table_ref, at, first_pair=0, table=0):
    for tile in range(values.shape[1] // 128):
        part = values[:, tile * 128 : tile * 128 + 128].astype(BF16).reshape(-1, 16, 128)
        give_groups(part, first_ref, second_ref, table_ref, at + tile, first_pair, table)


def pair_average(rows):
    out = np.zeros((rows // 2, rows), np.float32)
    for i in range(rows // 2):
        out[i, 2 * i] = out[i, 2 * i + 1] = 0.5
    return out


def average(rows, factor):
    out = np.zeros((rows // factor, rows), np.float32)
    for i in range(rows // factor):
        out[i, i * factor : (i + 1) * factor] = 1.0 / factor
    return out


def level_sizes(piece, far_levels, local_top):
    return tuple(piece >> level for level in range(local_top)) + (16,) * far_levels


def far_constants(seqs):
    out = np.zeros((seqs * 16, seqs * (8 + 16 + 8 + 8)), np.float32)
    starts = (0, seqs * 8, seqs * 24, seqs * 32)
    for seq in range(seqs):
        for slot in range(4):
            for i in range(4):
                row = seq * 16 + slot * 4 + i
                if slot == 1:
                    at = starts[1] + seq * 16 + 4 * i
                    out[row, at : at + 4] = 0.25
                else:
                    at = starts[slot] + seq * 8 + 2 * i
                    out[row, at : at + 2] = 0.5
    return out


def lane_a(rows):
    return lax.broadcasted_iota(jnp.int32, (rows, 128), 1) < 64


def stacked(block, sizes):
    in_a = lane_a(block.shape[0])
    zero = jnp.zeros_like(block)
    head_a = jnp.where(in_a, block, zero)
    head_b = jnp.where(in_a, zero, block)
    parts = []
    at = 0
    for size in sizes:
        parts.append(head_a[at : at + size])
        parts.append(head_b[at : at + size])
        at += size
    return parts


def blocked(parts):
    levels = len(parts) // 2
    rows = []
    for level in range(2, levels):
        block = jnp.concatenate(parts[2 * level : 2 * level + 2], axis=0)
        zero = jnp.zeros_like(block)
        rows.append(
            jnp.concatenate(
                [block if other == level else zero for other in range(2, levels)], axis=1
            )
        )
    return jnp.concatenate(rows, axis=0)


def queries_of(plain_ref, averaged_ref, pair, levels):
    piece = plain_ref.shape[0]
    lanes = slice(pair * 128, pair * 128 + 128)
    rest = jnp.concatenate(
        [averaged_ref[(level - 1) * piece : level * piece, lanes] for level in range(2, levels)],
        axis=1,
    )
    return plain_ref[:, lanes], averaged_ref[0:piece, lanes], rest


def far_rows_of(refs):
    return jnp.concatenate([ref[...].astype(F32) for ref in refs], axis=0)


def pick_far(source_ref, seq, far_rows, seqs):
    parts = []
    at = 0
    for n in far_rows:
        parts.append(source_ref[pl.ds(pl.multiple_of(at + seq * n, n), n), :])
        at += seqs * n
    return jnp.concatenate(parts, axis=0)


def even_average(rows, factor):
    row = lax.broadcasted_iota(jnp.int32, (rows // factor, rows), 0)
    column = lax.broadcasted_iota(jnp.int32, (rows // factor, rows), 1)
    return jnp.where(column // factor == row, 1.0 / factor, 0.0).astype(BF16)


def made_kernel(
    averaged_ref, wide_ref, coarse_ref, coarse_t_ref, mask_ref, ones_ref, *, sizes, local_top
):
    piece = wide_ref.shape[0]
    shape = (piece, piece)
    row = lax.broadcasted_iota(jnp.int32, shape, 0)
    column = lax.broadcasted_iota(jnp.int32, shape, 1)
    for level in range(1, len(sizes)):
        part = jnp.where(row >> level == column >> level, 0.5**level, 0.0).astype(BF16)
        averaged_ref[(level - 1) * piece : level * piece, :] = part
        wide_ref[:, (level - 1) * piece : level * piece] = part
    coarse = [even_average(piece, 2**level) for level in range(1, local_top)]
    coarse_ref[...] = jnp.concatenate(coarse, axis=0)
    at = 0
    for level in range(1, local_top):
        shape = (piece, sizes[level])
        row = lax.broadcasted_iota(jnp.int32, shape, 0)
        column = lax.broadcasted_iota(jnp.int32, shape, 1)
        part = jnp.where(row >> level == column, 0.5**level, 0.0).astype(BF16)
        coarse_t_ref[:, at : at + sizes[level]] = part
        at += sizes[level]
    row = lax.broadcasted_iota(jnp.int32, mask_ref.shape, 0)
    column = lax.broadcasted_iota(jnp.int32, mask_ref.shape, 1)
    keep = column >= 0
    at = 0
    for level in range(local_top):
        key = (column - at) % sizes[level]
        block = (row >> level) // 16
        if level == 0:
            good = block // 2 == key // 32
        else:
            good = block + 1 - 2 * (block % 2) == key // 16
        inside = (column >= at) & (column < at + 2 * sizes[level])
        keep = keep & (good | jnp.logical_not(inside))
        at += 2 * sizes[level]
    mask_ref[...] = jnp.where(keep, 1.0, 0.0)
    at = 0
    for level, size in enumerate(sizes):
        left = lax.broadcasted_iota(jnp.int32, (size, 128), 1) < 64
        ones_ref[at : at + size, :] = jnp.where(left, 2.0**level, 0.0).astype(BF16)
        ones_ref[at + size : at + 2 * size, :] = jnp.where(left, 0.0, 2.0**level).astype(BF16)
        at += 2 * size


def norm_kernel(x_ref, base_ref, next_ref):
    rows = x_ref.shape[0]
    unit, _ = unit_of(x_ref[...].astype(F32))
    base = dot(even_average(rows, rows // base_ref.shape[0]), unit.astype(BF16)).astype(BF16)
    base_ref[...] = base
    next_ref[...] = dot(even_average(base.shape[0], 2), base).astype(BF16)


def pack_kernel(out_ref, up_ref, down_ref, pack_ref):
    width = out_ref.shape[1]
    pack_ref[:, 0:width] = out_ref[...]
    at = width + up_ref.shape[1]
    pack_ref[:, width:at] = up_ref[...]
    for row in range(0, down_ref.shape[0], 16):
        pack_ref[:, at : at + width] = down_ref[row : row + 16, :]
        at += width


def far_kernel(own_ref, one_ref, two_ref, three_ref, gather_ref, pair_ref, five_ref, six_ref):
    rows = far_rows_of((own_ref, one_ref, two_ref, three_ref)).astype(BF16)
    five = dot(gather_ref[...], rows).astype(BF16)
    five_ref[...] = five
    six_ref[...] = dot(pair_ref[...], five).astype(BF16)


def far_back_kernel(
    five_ref, six_a_ref, six_b_ref, one_ref, two_ref, three_ref, spread_ref, pair_ref,
    own_out, one_out, two_out, three_out,
):
    six = (six_a_ref[...].astype(F32) + six_b_ref[...].astype(F32)).astype(BF16)
    five = (five_ref[...].astype(F32) + dot(pair_ref[...], six)).astype(BF16)
    rows = dot(spread_ref[...], five)
    own = own_out.shape[0]
    one = own + one_ref.shape[0]
    two = one + two_ref.shape[0]
    own_out[...] = rows[:own]
    one_out[...] = (rows[own:one] + one_ref[...].astype(F32)).astype(BF16)
    two_out[...] = (rows[one:two] + two_ref[...].astype(F32)).astype(BF16)
    three_out[...] = (rows[two:] + three_ref[...].astype(F32)).astype(BF16)


def mix_kernel(*refs):
    x_ref = refs[0]
    parts = refs[1:5]
    groups_ref = refs[5]
    far_refs = refs[6:-7]
    vec_ref, q_ref, k_ref, v_ref, kf_ref, vf_ref, weight_ref = refs[-7:]
    width = x_ref.shape[1]
    take_groups(parts, groups_ref, weight_ref, MIX_TABLE)
    unit, _ = unit_of(x_ref[...].astype(F32))
    far = far_rows_of(far_refs)
    small = weight_ref[:, :, 3 * width :].reshape(GROUPS * SMALL, 128)
    plain = expand_small(small, width, width // GROUPS)[0]
    biases = expand_small(small, width, 2 * width // GROUPS)
    ups = expand_small(small, width, 4 * width // GROUPS)
    vec_ref[...] = jnp.concatenate(
        [plain[0:6], biases[0][6:7], biases[1][6:7]]
        + [up[7:8] for up in ups]
        + [jnp.zeros((4, width), F32)],
        axis=0,
    )
    gain, shift = plain[0:1], plain[1:2]
    query_bias, value_bias = biases[0][6:7], biases[1][6:7]
    normed = (unit * gain + shift).astype(BF16)
    far = (far * gain + shift).astype(BF16)
    weight = weight_ref[:, :, 0:width].reshape(width, width)
    queries = (dot(normed, weight) + query_bias).astype(BF16).astype(F32)
    q_ref[...] = (queries * 0.125).astype(BF16)
    weight = weight_ref[:, :, width : 2 * width].reshape(width, width)
    k_ref[...] = dot(normed, weight).astype(BF16)
    kf_ref[...] = dot(far, weight)
    weight = weight_ref[:, :, 2 * width : 3 * width].reshape(width, width)
    v_ref[...] = (dot(normed, weight) + value_bias).astype(BF16)
    vf_ref[...] = dot(far, weight) + value_bias


def attention_kernel(
    q_ref, k_ref, v_ref, kf_ref, vf_ref, averaged_ref, coarse_ref, mask_ref, ones_ref,
    kall_ref, vall_ref, p_ref, att_ref, rden_ref,
    qe_ref,
    *, far_rows, sizes, local_top,
):
    piece, width = q_ref.shape
    levels = len(sizes)
    seq = pl.program_id(0)
    count = kf_ref.shape[0] // sum(far_rows)
    queries = q_ref[...]
    qe_ref[...] = dot(averaged_ref[...], queries).astype(BF16)
    keys = k_ref[...]
    values = v_ref[...]
    coarse_keys = dot(coarse_ref[...], keys).astype(BF16)
    coarse_values = dot(coarse_ref[...], values)
    scaled = [values]
    at = 0
    for level in range(1, local_top):
        scaled.append((coarse_values[at : at + sizes[level]] * 2.0**level).astype(BF16))
        at += sizes[level]
    far_values = pick_far(vf_ref, seq, far_rows, count)
    for level in range(local_top, levels):
        at = 16 * (level - local_top)
        scaled.append((far_values[at : at + 16] * 2.0**level).astype(BF16))
    kall_ref[0] = jnp.concatenate(
        [keys, coarse_keys, pick_far(kf_ref, seq, far_rows, count).astype(BF16)], axis=0
    )
    vall_ref[0] = jnp.concatenate(scaled, axis=0)
    for pair in range(width // 128):
        lanes = slice(pair * 128, pair * 128 + 128)
        plain, one, rest = queries_of(q_ref, qe_ref, pair, levels)
        key_parts = stacked(kall_ref[0, :, lanes], sizes)
        scores = jnp.concatenate(
            [
                dot_right(plain, jnp.concatenate(key_parts[0:2], axis=0)),
                dot_right(one, jnp.concatenate(key_parts[2:4], axis=0)),
                dot_right(rest, blocked(key_parts)),
            ],
            axis=1,
        )
        weights = jnp.where(mask_ref[...] > 0.0, jnp.exp(scores), 0.0).astype(BF16)
        p_ref[0, pair] = weights
        both = jnp.concatenate(
            [jnp.concatenate(stacked(vall_ref[0, :, lanes], sizes), axis=0), ones_ref[...]], axis=1
        )
        sums = dot(weights, both)
        rden = 1.0 / sums[:, 128:]
        rden_ref[:, lanes] = rden
        att_ref[:, lanes] = (sums[:, :128] * rden).astype(BF16)


def feed_kernel(
    vec_ref, table_ref, x_ref, cot_ref, att_ref, part_one, part_two, part_three, part_four,
    out_ref, dmid_ref, datt_ref, sum_ref, first_out, second_out,
    weight_ref,
):
    width = x_ref.shape[1]
    blocks = (weight_ref.shape[2] // width - 1) // 2
    take_groups((part_one, part_two, part_three, part_four), table_ref, weight_ref)
    gain = vec_ref[3:4, :]
    out_weight = weight_ref[:, :, 0:width].reshape(width, width)
    middle = x_ref[...].astype(F32) + dot(att_ref[...], out_weight) + vec_ref[2:3, :]
    unit, inverse = unit_of(middle)
    normed = (unit * gain + vec_ref[4:5, :]).astype(BF16)
    g_out = cot_ref[...]
    result = middle + vec_ref[5:6, :]
    d_two = jnp.zeros(x_ref.shape, F32)
    tiles = width // 128
    per_group = blocks * width // GROUPS // 16
    groups = GROUPS // blocks
    sums = []
    for block in range(blocks):
        up = weight_ref[:, :, width * (block + 1) : width * (block + 2)].reshape(width, width)
        down = jnp.concatenate(
            [
                weight_ref[groups * block + group, :, width * at : width * (at + 1)]
                for group in range(groups)
                for at in range(blocks + 1, blocks + 1 + per_group)
            ],
            axis=0,
        )
        pre = dot(normed, up) + vec_ref[8 + block : 9 + block, :]
        cdf = 0.5 + 0.5 * lax.erf(pre * 0.7071067811865476)
        hidden = (pre * cdf).astype(BF16)
        slope = cdf + pre * (0.3989422804014327 * jnp.exp(-0.5 * pre * pre))
        result = result + dot(hidden, down)
        grad = dot_left(hidden, g_out).reshape(groups, per_group, 16, width)
        for part in range(per_group):
            give_lanes(
                grad[:, part].reshape(-1, width), first_out, second_out, table_ref,
                tiles * (blocks + 1 + part), groups // 2 * block,
            )
        g_pre = (dot_right(g_out, down) * slope).astype(BF16)
        sums.append(column_sum(g_pre.astype(F32)))
        grad = dot_left(normed, g_pre)
        give_lanes(grad, first_out, second_out, table_ref, tiles * (block + 1))
        d_two = d_two + dot_right(g_pre, up)
    out_ref[...] = result.astype(BF16)
    cot = g_out.astype(F32)
    d_middle = cot + norm_back(d_two, unit, inverse, gain)
    dmid_ref[...] = d_middle
    branch = d_middle.astype(BF16)
    datt_ref[...] = dot_right(branch, out_weight)
    give_lanes(dot_left(att_ref[...], branch), first_out, second_out, table_ref, 0)
    sum_ref[...] = jnp.concatenate(
        [
            jnp.zeros((2, width), F32),
            column_sum(branch.astype(F32)),
            column_sum(d_two * unit),
            column_sum(d_two),
            column_sum(cot),
            jnp.zeros((2, width), F32),
        ]
        + sums
        + [jnp.zeros((8 - blocks, width), F32)],
        axis=0,
    )


def attention_back_kernel(
    q_ref, kall_ref, vall_ref, p_ref, att_ref, rden_ref, datt_ref, averaged_ref, wide_ref,
    coarse_t_ref, ones_ref,
    dq_ref, dk_ref, dv_ref, dkf_ref, dvf_ref,
    qe_ref, dkall_ref, dvall_ref, t_ref, dqacc_ref,
    *, sizes, local_top,
):
    piece, width = q_ref.shape
    levels = len(sizes)
    starts = np.concatenate([[0], np.cumsum(sizes)]).tolist()
    local = starts[local_top]

    qe_ref[...] = dot(averaged_ref[...], q_ref[...]).astype(BF16)
    near = 2 * sizes[0]
    mid = near + 2 * sizes[1]
    for pair in range(width // 128):
        lanes = slice(pair * 128, pair * 128 + 128)
        plain, one, rest = queries_of(q_ref, qe_ref, pair, levels)
        key_parts = stacked(kall_ref[0, :, lanes], sizes)
        both = jnp.concatenate(
            [jnp.concatenate(stacked(vall_ref[0, :, lanes], sizes), axis=0), ones_ref[...]], axis=1
        )
        d_num = datt_ref[:, lanes] * rden_ref[:, lanes]
        d_den = -d_num * att_ref[:, lanes].astype(F32)
        d_num = d_num.astype(BF16)
        weights = p_ref[0, pair]
        d_weights = dot_right(jnp.concatenate([d_num, d_den.astype(BF16)], axis=1), both)
        d_scores = (weights.astype(F32) * d_weights).astype(BF16)
        d_key_near = dot_left(d_scores[:, :near], plain)
        d_key_mid = dot_left(d_scores[:, near:mid], one)
        d_key_rest = dot_left(d_scores[:, mid:], rest)
        d_value = dot_left(weights, d_num)
        dqacc_ref[:, lanes] = dot(d_scores[:, :near], jnp.concatenate(key_parts[0:2], axis=0))
        t_ref[0:piece, lanes] = dot(
            d_scores[:, near:mid], jnp.concatenate(key_parts[2:4], axis=0)
        ).astype(BF16)
        d_rest = dot(d_scores[:, mid:], blocked(key_parts)).astype(BF16)
        at = 0
        for level in range(levels):
            size = sizes[level]
            low, high = starts[level], starts[level + 1]
            in_a = lane_a(size)
            if level == 0:
                source = d_key_near
            elif level == 1:
                source = d_key_mid
            else:
                block = slice((level - 2) * 128, (level - 1) * 128)
                source = d_key_rest[at - mid : at - mid + 2 * size, block]
                t_ref[(level - 1) * piece : level * piece, lanes] = d_rest[:, block]
            dkall_ref[low:high, lanes] = jnp.where(in_a, source[:size], source[size:])
            values = d_value[at : at + 2 * size]
            dvall_ref[low:high, lanes] = jnp.where(in_a, values[:size], values[size:]) * 2.0**level
            at += 2 * size
    dq_ref[...] = ((dqacc_ref[...] + dot(wide_ref[...], t_ref[...])) * 0.125).astype(BF16)
    for target, source in ((dk_ref, dkall_ref), (dv_ref, dvall_ref)):
        spread = dot(coarse_t_ref[...], source[piece:local, :].astype(BF16))
        target[...] = (source[0:piece, :] + spread).astype(BF16)
    dkf_ref[0] = dkall_ref[local:, :]
    dvf_ref[0] = dvall_ref[local:, :]


def mix_back_kernel(*refs, far_rows):
    fars = len(far_rows)
    x_ref, vec_ref, sum_ref = refs[:3]
    parts = refs[3:7]
    groups_ref = refs[7]
    grad_refs = [refs[8 + 2 * i : 10 + 2 * i] for i in range(5)]
    far_refs = refs[18 : 18 + fars]
    scaled_ref, first_ref, second_ref = refs[18 + fars : 21 + fars]
    dfar_refs = refs[21 + fars : 21 + 2 * fars]
    weight_ref = refs[-1]
    width = x_ref.shape[1]
    grads = [jnp.concatenate([ref[...] for ref in pair], axis=0) for pair in grad_refs[:3]]

    def by_ref(pair):
        rows = []
        at = 0
        for n in far_rows:
            for ref in pair:
                rows += [ref[seq, at : at + n, :] for seq in range(ref.shape[0])]
            at += n
        return jnp.concatenate(rows, axis=0)

    take_groups(parts, groups_ref, weight_ref, MIX_TABLE)
    gain = vec_ref[0:1, :]
    shift = vec_ref[1:2, :]
    unit, _ = unit_of(x_ref[...].astype(F32))
    normed = (unit * gain + shift).astype(BF16)
    far = far_rows_of(far_refs)
    far_normed = (far * gain + shift).astype(BF16)
    both = jnp.concatenate([normed, far_normed], axis=0)
    far_values = by_ref(grad_refs[4])
    far_grads = (None, by_ref(grad_refs[3]).astype(BF16), far_values.astype(BF16))
    d_one = jnp.zeros(x_ref.shape, F32)
    d_far = jnp.zeros(far.shape, F32)
    for part in range(3):
        lanes = slice(part * width, part * width + width)
        weight = weight_ref[:, :, lanes].reshape(width, width)
        d_one = d_one + dot_right(grads[part], weight)
        if part == 0:
            grad = dot_left(normed, grads[part])
        else:
            d_far = d_far + dot_right(far_grads[part], weight)
            grad = dot_left(both, jnp.concatenate([grads[part], far_grads[part]], axis=0))
        at = part * width // 128
        give_lanes(grad, first_ref, second_ref, groups_ref, at, table=MIX_BACK_TABLE)
    scaled_ref[...] = d_one * gain
    at = 0
    for ref in dfar_refs:
        ref[...] = (d_far[at : at + ref.shape[0]] * gain).astype(BF16)
        at += ref.shape[0]
    vectors = jnp.concatenate(
        [
            column_sum(d_one * unit) + column_sum(d_far * far),
            column_sum(d_one) + column_sum(d_far),
            sum_ref[2:6, :],
            column_sum(grads[0].astype(F32)),
            column_sum(grads[2].astype(F32)) + column_sum(far_values),
            sum_ref[8:16, :],
        ],
        axis=0,
    )
    chunk = width // GROUPS
    small = shrink_vectors(vectors, ((chunk, 0, 6), (2 * chunk, 6, 8), (4 * chunk, 8, 12)))
    at = 3 * width // 128
    give_lanes(small, first_ref, second_ref, groups_ref, at, table=MIX_BACK_TABLE)


def input_kernel(
    x_ref, dmid_ref, scaled_ref, own_ref, one_ref, two_ref, three_ref, pair_ref, spread_ref,
    din_ref,
):
    unit, inverse = unit_of(x_ref[...].astype(F32))
    lower = own_ref[...] + two_ref[...].astype(F32) + three_ref[...].astype(F32)
    base = one_ref[...].astype(F32) + dot(pair_ref[...], lower.astype(BF16))
    scaled = scaled_ref[...] + dot(spread_ref[...], base.astype(BF16))
    inner = (
        scaled
        - jnp.mean(scaled, axis=-1, keepdims=True)
        - unit * jnp.mean(scaled * unit, axis=-1, keepdims=True)
    )
    din_ref[...] = dmid_ref[...] + inner * inverse


def last_kernel(
    mix_one, mix_two, mix_three, mix_four, feed_ref, other_feed_ref,
    matrix_ref, out_ref, up_ref, down_ref, *vector_refs,
):
    total = feed_ref[0].astype(F32) + other_feed_ref[0].astype(F32)
    at = 0
    for ref in (out_ref, up_ref):
        for lane in range(0, ref.shape[1], 128):
            ref[:, lane : lane + 128] = total[at]
            at += 1
    for row in range(0, down_ref.shape[0], 16):
        for lane in range(0, down_ref.shape[1], 128):
            down_ref[row : row + 16, lane : lane + 128] = total[at]
            at += 1
    total = mix_one[0].astype(F32) + mix_two[0].astype(F32)
    total += mix_three[0].astype(F32) + mix_four[0].astype(F32)
    for lane in range(0, matrix_ref.shape[1], 128):
        matrix_ref[:, lane : lane + 128] = total[lane // 128]
    small = total[matrix_ref.shape[1] // 128]
    for i in range(6):
        vector_refs[i][...] = small[i : i + 1, : vector_refs[i].shape[1]]
    vector_refs[6][...] = column_sum(small[6:8])[:, : vector_refs[6].shape[1]]
    vector_refs[7][...] = column_sum(small[8:12])[:, : vector_refs[7].shape[1]]


def vmem():
    return pl.BlockSpec(memory_space=pltpu.VMEM)


def anywhere():
    return pl.BlockSpec(memory_space=pl.ANY)


def scalars():
    return pl.BlockSpec(memory_space=pltpu.SMEM)


def fixed(*dims):
    return pl.BlockSpec(dims, lambda i: (0,) * len(dims))


def moving(*dims):
    return pl.BlockSpec(dims, lambda i: (i,) + (0,) * (len(dims) - 1))


def shape(dims, dtype):
    return jax.ShapeDtypeStruct(dims, dtype)


def const(values):
    return jnp.asarray(values, BF16)


def bit_orders():
    return ((8, 4, 16, 2), (2, 8, 4, 16))


def mix_orders():
    return ((8, 4, 16, 2), (8, 4, 16, 2))


def mix_back_orders():
    return ((8, 4, 16, 2), (8, 4, 2, 16))


def slot_offset(slot, order):
    return sum(bit for k, bit in enumerate(order) if slot >> k & 1)


def group_table(orders):
    table = np.zeros((32, 128), np.int32)
    for device in range(32):
        core = device & 1
        table[device, GROUPS] = core
        for slot in range(16):
            table[device, (device ^ slot_offset(slot, orders[core])) // 2] = slot
            group = device ^ 1 ^ slot_offset(slot, orders[1 - core])
            table[device, GROUPS // 2 + group // 2] = slot
    return table


def exchange(value, bits):
    if isinstance(bits, int):
        bits = (bits, bits)
    count = lax.axis_size(AXES)
    return lax.ppermute(value, AXES, [(i, i ^ bits[i & 1]) for i in range(count)])


def after(value, *others):
    return lax.optimization_barrier((value,) + others)[0]


def added(*parts):
    total = parts[0].astype(F32)
    for part in parts[1:]:
        total = total + part.astype(F32)
    return total.astype(BF16)


def send(buffer, k, orders=None):
    orders = orders or bit_orders()
    return exchange(buffer, (orders[0][k], orders[1][k]))


def halves(kept, other):
    half = kept.shape[0] // 2
    return added(kept[:half], other[:half]), added(kept[half:], other[half:])


def joined(buffer, other):
    return jnp.concatenate([buffer, other], axis=0)


def call(kernel, name, outs, ins, args, work, scratch=(), grid=None, room=6):
    return pl.pallas_call(
        kernel,
        out_shape=tuple(item[0] for item in outs),
        in_specs=list(ins),
        out_specs=tuple(item[1] for item in outs),
        scratch_shapes=list(scratch),
        compiler_params=pltpu.CompilerParams(vmem_limit_bytes=room * MIB),
        cost_estimate=pl.CostEstimate(flops=work, bytes_accessed=work >> 9, transcendentals=0),
        name=name,
        **({} if grid is None else {"grid": grid}),
    )(*args)


def coarsen(values):
    return (values[:, 0::2] + values[:, 1::2]) * 0.5


def whole_far(base, seqs, far_levels, position):
    rows = base.reshape(seqs, 16, base.shape[1])
    full = lax.all_gather(rows, "seq", axis=1, tiled=True).astype(F32)
    parts = []
    for extra in range(far_levels):
        partner = (position // 2**extra) ^ 1
        parts.append(lax.dynamic_slice_in_dim(full, partner * 16, 16, axis=1))
        if extra + 1 < far_levels:
            full = coarsen(full)
    return jnp.concatenate(parts, axis=1).astype(BF16).reshape(seqs * 16 * far_levels, -1)


def whole_far_back(grad, seqs, far_levels, position):
    stack = grad.reshape(seqs, far_levels, 16, -1).astype(F32)
    ids = jnp.arange(far_levels).reshape(1, far_levels, 1, 1)
    count = lax.axis_size("seq")
    for bit in range(far_levels):
        pairs = [(i, i ^ 1 << bit) for i in range(count)]
        other = lax.ppermute(stack.astype(BF16), "seq", pairs).astype(F32)
        stack = jnp.where(ids > bit, stack + other, jnp.where(ids == bit, other, stack))
    own = jnp.zeros((seqs, 16, stack.shape[-1]), F32)
    for extra in range(far_levels):
        rows = 16 >> extra
        offset = position % 2**extra * rows
        part = lax.dynamic_slice_in_dim(stack[:, extra], offset, rows, axis=1)
        own = own + jnp.repeat(part, 2**extra, axis=1) * 0.5**extra
    return own.reshape(seqs * 16, -1).astype(BF16)


def body(
    layer_input, qkv_weight, qv_bias, out_weight, out_bias, first_gain, first_shift, second_gain,
    second_shift, up_weight, up_bias, down_weight, down_bias, cotangent,
):
    batches, per_batch, piece, width = layer_input.shape
    seqs = batches * per_batch
    tokens = seqs * piece
    hidden = up_weight.shape[1]
    blocks = hidden // width
    devices = lax.axis_size(AXES)
    pieces = lax.axis_size("seq")
    position = lax.axis_index("seq")
    far_levels = pieces.bit_length() - 1
    local_top = (piece // 16).bit_length() - 1
    fast = devices == GROUPS and pieces == 16
    x = layer_input.reshape(tokens, width)
    cot = cotangent.reshape(tokens, width)
    sizes = level_sizes(piece, far_levels, local_top)
    keys = sum(sizes)
    flat = (tokens, width)
    base_rows = seqs * 16
    coarse_all = np.kron(np.eye(seqs, dtype=np.float32), average(piece, piece // 16))
    pair = np.kron(np.eye(seqs, dtype=np.float32), pair_average(16))
    gather_far = far_constants(seqs)
    vectors = (
        first_gain, first_shift, out_bias, second_gain, second_shift, down_bias, qv_bias, up_bias,
    )

    if fast:
        me = lax.axis_index(AXES)
        orders = (bit_orders(), mix_orders(), mix_back_orders())
        table = np.concatenate([group_table(item) for item in orders], axis=1)
        groups = lax.dynamic_slice_in_dim(jnp.asarray(table), me, 1, axis=0)
    if fast:
        (pack_b,) = call(
            pack_kernel,
            "pack",
            [(shape((16, width + 2 * hidden), BF16), vmem())],
            [vmem()] * 3,
            (out_weight, up_weight, down_weight),
            1 << 16,
            room=60,
        )
    base, below = call(
        norm_kernel,
        "norm",
        [(shape((base_rows, width), BF16), vmem()), (shape((base_rows // 2, width), BF16), vmem())],
        [vmem()],
        (after(x, groups, pack_b) if fast else x,),
        1 << 20,
    )
    coarse_rows = sum(sizes[1:local_top])
    top = len(sizes) - 1
    made = (
        ((top * piece, piece), BF16),
        ((piece, top * piece), BF16),
        ((coarse_rows, piece), BF16),
        ((piece, coarse_rows), BF16),
        ((piece, 2 * keys), F32),
        ((2 * keys, 128), BF16),
    )
    averaged, averaged_wide, coarse, coarse_t, mask, ones = call(
        partial(made_kernel, sizes=sizes, local_top=local_top),
        "made",
        [(shape(*item), vmem()) for item in made],
        [],
        (),
        1 << 20,
    )

    if fast:
        a = jnp.pad(qkv_weight, ((0, 0), (0, 128)))
        for row, vector in enumerate(vectors):
            item = vector.reshape(1, -1)
            lanes = (3 * width, 128 - item.shape[1])
            a = a + jnp.pad(item, ((row, SMALL - 1 - row), lanes))
        a = a[None]
        b = pack_b[None]
        other_a = send(a, 0, mix_orders())
        other_b = send(b, 0)
        a = joined(a, other_a)
        other_a = send(after(a, base), 1, mix_orders())
        a = joined(a, other_a)
        other_a = send(a, 2, mix_orders())
        b = joined(after(b, a), other_b)
        other_b = send(b, 1)
        near, half = after(base, a), after(below, a)
        one, two, three = exchange(near, 1), exchange(half, 2), exchange(half, 3)
        a = joined(a, other_a)
        a = after(a, one, two, three)
        other_a = send(a, 3, mix_orders())
        five, six = call(
            far_kernel,
            "far",
            [
                (shape((base_rows, width), BF16), vmem()),
                (shape((base_rows // 2, width), BF16), vmem()),
            ],
            [vmem()] * 6,
            (after(below, a, mask), one, two, three, const(gather_far), const(pair)),
            1 << 20,
        )
        far = (one, two, three, exchange(five, 4), exchange(six, 8), exchange(six, 12))
        far_rows = (16, 8, 8, 16, 8, 8)
        b = joined(after(b, a), other_b)
        other_b = send(b, 2)
        lower = exchange(a, 1)
        other_a = after(other_a, five, six)
        parts_a = (a, other_a, lower, exchange(other_a, 1))
        b = joined(after(b, other_a, *far), other_b)
        other_b = send(b, 3)
        lower = exchange(after(b, other_a), 1)
    else:
        groups = [slot % (GROUPS // 2) for slot in range(GROUPS)] + [0] * (128 - GROUPS)
        groups = jnp.asarray([groups * 3], jnp.int32)

        def whole(value):
            return lax.all_gather(value, AXES, axis=0, tiled=True).reshape(
                (GROUPS, -1) + value.shape[1:]
            )

        small = [jnp.pad(v, ((0, 0), (0, 128 - v.shape[1]))) for v in map(whole, vectors)]
        small += [jnp.zeros((GROUPS, 128), BF16)] * (SMALL - len(small))
        gathered_a = jnp.concatenate([whole(qkv_weight), jnp.stack(small, axis=1)], axis=2)
        downs = whole(down_weight).reshape(GROUPS, -1, 16, width).transpose(0, 2, 1, 3)
        parts = [whole(out_weight), whole(up_weight), downs.reshape(GROUPS, 16, -1)]
        gathered_b = jnp.concatenate(parts, axis=2)

        def quarters(item):
            return item[0:16:2], item[16::2], item[1:16:2], item[17::2]

        parts_a, parts_b = quarters(gathered_a), quarters(gathered_b)
        far = (whole_far(base, seqs, far_levels, position),)
        far_rows = (16 * far_levels,)

    lanes_a = 3 * width + 128
    tiles_a = lanes_a // 128
    tiles_b = (width + 2 * hidden) // 128
    top = len(sizes) - 1
    pairs = width // 128
    total_far = seqs * 16 * far_levels
    half_a = shape((GROUPS // 2, tiles_a, 16, 128), BF16)
    half_b = shape((GROUPS // 2, tiles_b, 16, 128), BF16)
    far_flat = shape((total_far, width), F32)
    low, high = shape(flat, BF16), shape(flat, F32)
    sixteen = shape((16, width), F32)
    level = dict(far_rows=far_rows, sizes=sizes, local_top=local_top)

    vec, queries, key, value, far_key, far_value = call(
        mix_kernel,
        "mix",
        [(sixteen, vmem())] + [(low, vmem())] * 3 + [(far_flat, vmem())] * 2,
        [vmem()] * 5 + [scalars()] + [vmem()] * len(far),
        (x, *parts_a, groups, *far),
        1 << 24,
        [pltpu.VMEM((GROUPS, 16, lanes_a), BF16)],
        room=14,
    )
    rows_spec = moving(piece, width)
    keys_spec = moving(1, keys, width)
    p_spec = moving(1, pairs, piece, 2 * keys)
    keys_shape = shape((seqs, keys, width), BF16)
    kall, vall, weights, attended, rden = call(
        partial(attention_kernel, **level),
        "attention",
        [
            (keys_shape, keys_spec),
            (keys_shape, keys_spec),
            (shape((seqs, pairs, piece, 2 * keys), BF16), p_spec),
            (low, rows_spec),
            (high, rows_spec),
        ],
        [rows_spec] * 3
        + [fixed(total_far, width)] * 2
        + [
            fixed(top * piece, piece),
            fixed(coarse_rows, piece),
            fixed(piece, 2 * keys),
            fixed(2 * keys, 128),
        ],
        (
            queries, key, value, far_key, far_value, averaged, coarse, mask, ones,
        ),
        1 << 24,
        [pltpu.VMEM((top * piece, width), BF16)],
        (seqs,),
        room=12,
    )
    if fast:
        other_b = after(other_b, attended)
        parts_b = (b, other_b, lower, exchange(other_b, 1))

    result, d_middle, d_attended, sums, kept_b, sent_b = call(
        feed_kernel,
        "feed",
        [(low, vmem()), (high, vmem()), (high, vmem()), (sixteen, vmem())] + [(half_b, vmem())] * 2,
        [vmem(), scalars()] + [vmem()] * 7,
        (vec, groups, x, cot, attended, *parts_b),
        8 << 30,
        [
            pltpu.VMEM((GROUPS, 16, width + 2 * hidden), BF16),
        ],
        room=30,
    )
    def back_call(seq, count, d_attended):
        def later(*dims):
            return pl.BlockSpec(dims, lambda i: (i + seq,) + (0,) * (len(dims) - 1))

        rows, wide_keys = later(piece, width), later(1, keys, width)
        half = (shape((count * piece, width), BF16), rows_spec)
        far_half = shape((count, keys - local, width), F32), moving(1, keys - local, width)
        return call(
            partial(attention_back_kernel, sizes=sizes, local_top=local_top),
            "attention_back",
            [half] * 3 + [far_half] * 2,
            [rows, wide_keys, wide_keys, later(1, pairs, piece, 2 * keys), rows, rows, rows]
            + [
                fixed(top * piece, piece),
                fixed(piece, top * piece),
                fixed(piece, coarse_rows),
                fixed(2 * keys, 128),
            ],
            (
                queries, kall, vall, weights, attended, rden, d_attended, averaged, averaged_wide,
                coarse_t, ones,
            ),
            6 << 30,
            [
                pltpu.VMEM((top * piece, width), BF16),
                pltpu.VMEM((keys, width), F32),
                pltpu.VMEM((keys, width), F32),
                pltpu.VMEM((top * piece, width), BF16),
                pltpu.VMEM((piece, width), F32),
            ],
            (count,),
            room=16,
        )

    local = sum(sizes[:local_top])
    if fast:
        late = exchange(sent_b[12:], 1)
        rest = exchange(after(sent_b, late)[:12], 1)
        upper_b = added(kept_b[12:], late)
        late_b = send(upper_b, 3)
        d_attended = after(d_attended, upper_b)
    most = max(1, seqs // 2)
    back_one = back_call(0, most, d_attended)
    if fast:
        rest, *back_one = lax.optimization_barrier((rest, *back_one))
        upper_b = added(kept_b[8:12], rest[8:])
        early_b = send(upper_b, 3)
        d_attended = after(d_attended, upper_b)
    back_two = back_call(most, seqs - most, d_attended)
    outs = call(
        partial(mix_back_kernel, far_rows=far_rows),
        "mix_back",
        [(high, vmem())]
        + [(half_a, vmem())] * 2
        + [(shape(item.shape, BF16), vmem()) for item in far],
        [vmem()] * 7 + [scalars()] + [vmem()] * (10 + len(far)),
        (
            x, vec, sums, *parts_a, groups,
            *[item for pair in zip(back_one, back_two) for item in pair], *far,
        ),
        16 << 30,
        [pltpu.VMEM((GROUPS, 16, lanes_a), BF16)],
        room=24,
    )
    scaled, kept_a, sent_a = outs[:3]
    d_far = outs[3:]

    if fast:
        upper_b = added(after(kept_b[4:8], scaled, early_b), rest[4:8], late_b)
        middle_b = send(upper_b, 2)
        other_a = exchange(after(sent_a, upper_b), 1)
        kept_a, upper_a = halves(kept_a, other_a)
        other_a = send(upper_a, 3, mix_back_orders())
        back = [after(item, upper_a) for item in d_far[3:]]
        back = [exchange(item, bits) for item, bits in zip(back, (4, 8, 12))]
        kept_b = added(after(kept_b, upper_a, *back)[:4], rest[:4], early_b, middle_b)
        kept_b, upper_b = kept_b[:2], kept_b[2:]
        other_b = send(upper_b, 1)
        kept_a, upper_a = halves(after(kept_a, upper_b), other_a)
        other_a = send(upper_a, 2, mix_back_orders())
        back = [after(item, upper_b) for item in back]
        own, out_one, out_two, out_three = call(
            far_back_kernel,
            "far_back",
            [
                (shape((base_rows // 2, width), F32), vmem()),
                (shape((base_rows, width), BF16), vmem()),
                (shape((base_rows // 2, width), BF16), vmem()),
                (shape((base_rows // 2, width), BF16), vmem()),
            ],
            [vmem()] * 8,
            (*back, d_far[0], d_far[1], d_far[2], const(gather_far.T), const(pair.T)),
            1 << 20,
        )
        far_one = exchange(out_one, 1)
        far_two = exchange(out_two, 2)
        far_three = exchange(out_three, 3)
        own_a, far_a = halves(after(kept_a, own, other_b), other_a)
        one_a, two_a = own_a[0:1], own_a[1:2]
        lasts_a = (
            one_a,
            exchange(two_a, 8),
            exchange(far_a[0:1], 4),
            exchange(far_a[1:2], 12),
        )
        kept_b, upper_b = halves(after(kept_b, own_a), other_b)
        other_b = send(upper_b, 0)
    else:
        far_one = whole_far_back(d_far[0], seqs, far_levels, position)
        own = jnp.zeros((base_rows // 2, width), F32)
        far_two = far_three = jnp.zeros((base_rows // 2, width), BF16)

    (d_input,) = call(
        input_kernel,
        "input_grad",
        [(high, vmem())],
        [vmem()] * 9,
        (
            x, d_middle, scaled, own, far_one, far_two, far_three, const(pair.T),
            const(coarse_all.T),
        ),
        1 << 20,
    )

    if fast:
        grad_qkv, grad_out_weight, grad_up, grad_down, *plain = call(
            last_kernel,
            "last",
            [
                (shape(item.shape, F32), vmem())
                for item in (qkv_weight, out_weight, up_weight, down_weight)
            ]
            + [(shape((1, v.shape[0]), F32), vmem()) for v in vectors],
            [vmem()] * 6,
            (*lasts_a, kept_b, other_b),
            1 << 16,
        )
        plain = [item.reshape(-1) for item in plain]
        grad_qv, grad_up_bias = plain[6:8]
    else:

        def reduced(item):
            return lax.psum_scatter(item.astype(F32), AXES, scatter_dimension=0, tiled=True)

        def rows_of(item):
            return reduced(item.transpose(0, 2, 1, 3).reshape(GROUPS * 16, -1))

        all_a = jnp.stack([kept_a, sent_a], axis=1).reshape(GROUPS, *half_a.shape[1:])
        all_b = jnp.stack([kept_b, sent_b], axis=1).reshape(GROUPS, *half_b.shape[1:])
        grad_qkv = rows_of(all_a[:, :-1])
        small = all_a[:, -1]
        chunk = width // GROUPS
        plain = [reduced(small[:, i, :chunk].reshape(-1)) for i in range(6)]
        grad_qv = reduced(jnp.sum(small[:, 6:8, : 2 * chunk], axis=1).reshape(-1))
        grad_up_bias = reduced(jnp.sum(small[:, 8:12, : 4 * chunk], axis=1).reshape(-1))
        split = width // 128
        grad_out_weight = rows_of(all_b[:, :split])
        grad_up = rows_of(all_b[:, split : split * (blocks + 1)])
        downs = all_b[:, split * (blocks + 1) :].reshape(GROUPS, -1, split, 16, 128)
        grad_down = reduced(downs.transpose(0, 1, 3, 2, 4).reshape(hidden, width))

    return (
        result.reshape(layer_input.shape),
        d_input.reshape(layer_input.shape),
        grad_qkv,
        grad_qv,
        grad_out_weight,
        plain[2],
        plain[0],
        plain[1],
        plain[3],
        plain[4],
        grad_up,
        grad_up_bias,
        grad_down,
        plain[5],
    )


def solution(mesh):
    tokens = P(None, "dp", "seq", None)
    matrix = P(AXES, None)
    vector = P(AXES)
    in_specs = (
        tokens, matrix, vector, matrix, vector, vector, vector, vector, vector, matrix, vector,
        matrix, vector, tokens,
    )
    out_specs = (
        tokens, tokens, matrix, vector, matrix, vector, vector, vector, vector, vector, matrix,
        vector, matrix, vector,
    )
    return jax.shard_map(body, mesh=mesh, in_specs=in_specs, out_specs=out_specs, check_vma=False)
```

```python
from functools import partial

import jax
import jax.numpy as jnp
import numpy as np
from jax import lax
from jax.experimental import pallas as pl
from jax.experimental.pallas import tpu as pltpu
from jax.sharding import PartitionSpec as P

HEADS = 8
AXES = ("dp", "seq")
F32 = jnp.float32
BF16 = jnp.bfloat16
GROUPS = 32
SMALL = 16
EPS = 1e-05
MIB = 1024 * 1024


def dot(left, right):
    return jnp.dot(left, right, preferred_element_type=F32)


def dot_right(left, right):
    return lax.dot_general(left, right, (((1,), (1,)), ((), ())), preferred_element_type=F32)


def dot_left(left, right):
    return lax.dot_general(left, right, (((0,), (0,)), ((), ())), preferred_element_type=F32)


def unit_of(values):
    centred = values - jnp.mean(values, axis=-1, keepdims=True)
    scale = lax.rsqrt(jnp.mean(centred * centred, axis=-1, keepdims=True) + EPS)
    return centred * scale, scale


def norm_back(grad, unit, scale, gain):
    scaled = grad * gain
    inner = (
        scaled
        - jnp.mean(scaled, axis=-1, keepdims=True)
        - unit * jnp.mean(scaled * unit, axis=-1, keepdims=True)
    )
    return inner * scale


def column_sum(values):
    return jnp.sum(values, axis=0, keepdims=True)


def expand_small(small, width, chunk):
    eye = lax.broadcasted_iota(jnp.int32, (128, width), 0) == (
        lax.broadcasted_iota(jnp.int32, (128, width), 1) % chunk
    )
    spread = dot(small, eye.astype(F32).astype(BF16))
    runs = GROUPS * chunk // width
    per_run = GROUPS // runs
    group = lax.broadcasted_iota(jnp.int32, (GROUPS * SMALL, width), 0) // SMALL
    column = lax.broadcasted_iota(jnp.int32, (GROUPS * SMALL, width), 1) // chunk
    kept = jnp.where(group % per_run == column, spread, 0.0).reshape(GROUPS, SMALL, width)
    return [jnp.sum(kept[run * per_run : (run + 1) * per_run], axis=0) for run in range(runs)]


def shrink_vectors(vectors, parts):
    width = vectors.shape[1]
    tiled = jnp.broadcast_to(vectors[None], (GROUPS, SMALL, width)).reshape(-1, width)
    row = lax.broadcasted_iota(jnp.int32, (GROUPS * SMALL, width), 0)
    lane = lax.broadcasted_iota(jnp.int32, (GROUPS * SMALL, width), 1)
    group = row // SMALL
    row = row % SMALL
    total = None
    for chunk, first, end in parts:
        runs = GROUPS * chunk // width
        per_run = GROUPS // runs
        keep = (group % per_run == lane // chunk) & (row >= first) & (row < end)
        if runs > 1:
            keep = keep & (row - first == group // per_run)
        eye = lax.broadcasted_iota(jnp.int32, (width, 128), 0) % chunk == lax.broadcasted_iota(
            jnp.int32, (width, 128), 1
        )
        part = dot(jnp.where(keep, tiled, 0.0).astype(BF16), eye.astype(F32).astype(BF16))
        total = part if total is None else total + part
    return total


MIX_TABLE = 128
MIX_BACK_TABLE = 256


def same_core(table_ref):
    return table_ref[0, GROUPS] == 0


def take_groups(parts, table_ref, target_ref, table=0):
    even = same_core(table_ref)
    half = parts[0].shape[0]

    def slot_of(at, low_ref, high_ref):
        slot = table_ref[0, table + at]
        index = lax.rem(slot, half)
        return jnp.where(slot >= half, high_ref[index], low_ref[index])

    for pair in range(GROUPS // 2):
        mine = slot_of(pair, *parts[0:2])
        other = slot_of(GROUPS // 2 + pair, *parts[2:4])
        target_ref[2 * pair] = jnp.where(even, mine, other)
        target_ref[2 * pair + 1] = jnp.where(even, other, mine)


def give_groups(values, first_ref, second_ref, table_ref, tile, first_pair=0, table=0):
    even = same_core(table_ref)
    for i in range(values.shape[0] // 2):
        pair = first_pair + i
        one, two = values[2 * i], values[2 * i + 1]
        first_ref[table_ref[0, table + pair], tile] = jnp.where(even, one, two)
        second_ref[table_ref[0, table + GROUPS // 2 + pair], tile] = jnp.where(even, two, one)


def give_lanes(values, first_ref, second_ref, table_ref, at, first_pair=0, table=0):
    for tile in range(values.shape[1] // 128):
        part = values[:, tile * 128 : tile * 128 + 128].astype(BF16).reshape(-1, 16, 128)
        give_groups(part, first_ref, second_ref, table_ref, at + tile, first_pair, table)


def pair_average(rows):
    out = np.zeros((rows // 2, rows), np.float32)
    for i in range(rows // 2):
        out[i, 2 * i] = out[i, 2 * i + 1] = 0.5
    return out


def average(rows, factor):
    out = np.zeros((rows // factor, rows), np.float32)
    for i in range(rows // factor):
        out[i, i * factor : (i + 1) * factor] = 1.0 / factor
    return out


def level_sizes(piece, far_levels, local_top):
    return tuple(piece >> level for level in range(local_top)) + (16,) * far_levels


def far_constants(seqs):
    out = np.zeros((seqs * 16, seqs * (8 + 16 + 8 + 8)), np.float32)
    starts = (0, seqs * 8, seqs * 24, seqs * 32)
    for seq in range(seqs):
        for slot in range(4):
            for i in range(4):
                row = seq * 16 + slot * 4 + i
                if slot == 1:
                    at = starts[1] + seq * 16 + 4 * i
                    out[row, at : at + 4] = 0.25
                else:
                    at = starts[slot] + seq * 8 + 2 * i
                    out[row, at : at + 2] = 0.5
    return out


def lane_a(rows):
    return lax.broadcasted_iota(jnp.int32, (rows, 128), 1) < 64


def stacked(block, sizes):
    in_a = lane_a(block.shape[0])
    zero = jnp.zeros_like(block)
    head_a = jnp.where(in_a, block, zero)
    head_b = jnp.where(in_a, zero, block)
    parts = []
    at = 0
    for size in sizes:
        parts.append(head_a[at : at + size])
        parts.append(head_b[at : at + size])
        at += size
    return parts


def blocked(parts):
    levels = len(parts) // 2
    rows = []
    for level in range(2, levels):
        block = jnp.concatenate(parts[2 * level : 2 * level + 2], axis=0)
        zero = jnp.zeros_like(block)
        rows.append(
            jnp.concatenate(
                [block if other == level else zero for other in range(2, levels)], axis=1
            )
        )
    return jnp.concatenate(rows, axis=0)


def queries_of(plain_ref, averaged_ref, pair, levels):
    piece = plain_ref.shape[0]
    lanes = slice(pair * 128, pair * 128 + 128)
    rest = jnp.concatenate(
        [averaged_ref[(level - 1) * piece : level * piece, lanes] for level in range(2, levels)],
        axis=1,
    )
    return plain_ref[:, lanes], averaged_ref[0:piece, lanes], rest


def far_rows_of(refs):
    return jnp.concatenate([ref[...].astype(F32) for ref in refs], axis=0)


def pick_far(source_ref, seq, far_rows, seqs):
    parts = []
    at = 0
    for n in far_rows:
        parts.append(source_ref[pl.ds(pl.multiple_of(at + seq * n, n), n), :])
        at += seqs * n
    return jnp.concatenate(parts, axis=0)


def even_average(rows, factor):
    row = lax.broadcasted_iota(jnp.int32, (rows // factor, rows), 0)
    column = lax.broadcasted_iota(jnp.int32, (rows // factor, rows), 1)
    return jnp.where(column // factor == row, 1.0 / factor, 0.0).astype(BF16)


def made_kernel(
    averaged_ref, wide_ref, coarse_ref, coarse_t_ref, mask_ref, ones_ref, *, sizes, local_top
):
    piece = wide_ref.shape[0]
    shape = (piece, piece)
    row = lax.broadcasted_iota(jnp.int32, shape, 0)
    column = lax.broadcasted_iota(jnp.int32, shape, 1)
    for level in range(1, len(sizes)):
        part = jnp.where(row >> level == column >> level, 0.5**level, 0.0).astype(BF16)
        averaged_ref[(level - 1) * piece : level * piece, :] = part
        wide_ref[:, (level - 1) * piece : level * piece] = part
    coarse = [even_average(piece, 2**level) for level in range(1, local_top)]
    coarse_ref[...] = jnp.concatenate(coarse, axis=0)
    at = 0
    for level in range(1, local_top):
        shape = (piece, sizes[level])
        row = lax.broadcasted_iota(jnp.int32, shape, 0)
        column = lax.broadcasted_iota(jnp.int32, shape, 1)
        part = jnp.where(row >> level == column, 0.5**level, 0.0).astype(BF16)
        coarse_t_ref[:, at : at + sizes[level]] = part
        at += sizes[level]
    row = lax.broadcasted_iota(jnp.int32, mask_ref.shape, 0)
    column = lax.broadcasted_iota(jnp.int32, mask_ref.shape, 1)
    keep = column >= 0
    at = 0
    for level in range(local_top):
        key = (column - at) % sizes[level]
        block = (row >> level) // 16
        if level == 0:
            good = block // 2 == key // 32
        else:
            good = block + 1 - 2 * (block % 2) == key // 16
        inside = (column >= at) & (column < at + 2 * sizes[level])
        keep = keep & (good | jnp.logical_not(inside))
        at += 2 * sizes[level]
    mask_ref[...] = jnp.where(keep, 1.0, 0.0)
    at = 0
    for level, size in enumerate(sizes):
        left = lax.broadcasted_iota(jnp.int32, (size, 128), 1) < 64
        ones_ref[at : at + size, :] = jnp.where(left, 2.0**level, 0.0).astype(BF16)
        ones_ref[at + size : at + 2 * size, :] = jnp.where(left, 0.0, 2.0**level).astype(BF16)
        at += 2 * size


def norm_kernel(x_ref, base_ref, next_ref):
    rows = x_ref.shape[0]
    unit, _ = unit_of(x_ref[...].astype(F32))
    base = dot(even_average(rows, rows // base_ref.shape[0]), unit.astype(BF16)).astype(BF16)
    base_ref[...] = base
    next_ref[...] = dot(even_average(base.shape[0], 2), base).astype(BF16)


def pack_kernel(out_ref, up_ref, down_ref, pack_ref):
    width = out_ref.shape[1]
    pack_ref[:, 0:width] = out_ref[...]
    at = width + up_ref.shape[1]
    pack_ref[:, width:at] = up_ref[...]
    for row in range(0, down_ref.shape[0], 16):
        pack_ref[:, at : at + width] = down_ref[row : row + 16, :]
        at += width


def far_kernel(own_ref, one_ref, two_ref, three_ref, gather_ref, pair_ref, five_ref, six_ref):
    rows = far_rows_of((own_ref, one_ref, two_ref, three_ref)).astype(BF16)
    five = dot(gather_ref[...], rows).astype(BF16)
    five_ref[...] = five
    six_ref[...] = dot(pair_ref[...], five).astype(BF16)


def far_back_kernel(
    five_ref, six_a_ref, six_b_ref, one_ref, two_ref, three_ref, spread_ref, pair_ref,
    own_out, one_out, two_out, three_out,
):
    six = (six_a_ref[...].astype(F32) + six_b_ref[...].astype(F32)).astype(BF16)
    five = (five_ref[...].astype(F32) + dot(pair_ref[...], six)).astype(BF16)
    rows = dot(spread_ref[...], five)
    own = own_out.shape[0]
    one = own + one_ref.shape[0]
    two = one + two_ref.shape[0]
    own_out[...] = rows[:own]
    one_out[...] = (rows[own:one] + one_ref[...].astype(F32)).astype(BF16)
    two_out[...] = (rows[one:two] + two_ref[...].astype(F32)).astype(BF16)
    three_out[...] = (rows[two:] + three_ref[...].astype(F32)).astype(BF16)


def mix_kernel(*refs):
    x_ref = refs[0]
    parts = refs[1:5]
    groups_ref = refs[5]
    far_refs = refs[6:-7]
    vec_ref, q_ref, k_ref, v_ref, kf_ref, vf_ref, weight_ref = refs[-7:]
    width = x_ref.shape[1]
    take_groups(parts, groups_ref, weight_ref, MIX_TABLE)
    unit, _ = unit_of(x_ref[...].astype(F32))
    far = far_rows_of(far_refs)
    small = weight_ref[:, :, 3 * width :].reshape(GROUPS * SMALL, 128)
    plain = expand_small(small, width, width // GROUPS)[0]
    biases = expand_small(small, width, 2 * width // GROUPS)
    ups = expand_small(small, width, 4 * width // GROUPS)
    vec_ref[...] = jnp.concatenate(
        [plain[0:6], biases[0][6:7], biases[1][6:7]]
        + [up[7:8] for up in ups]
        + [jnp.zeros((4, width), F32)],
        axis=0,
    )
    gain, shift = plain[0:1], plain[1:2]
    query_bias, value_bias = biases[0][6:7], biases[1][6:7]
    normed = (unit * gain + shift).astype(BF16)
    far = (far * gain + shift).astype(BF16)
    weight = weight_ref[:, :, 0:width].reshape(width, width)
    queries = (dot(normed, weight) + query_bias).astype(BF16).astype(F32)
    q_ref[...] = (queries * 0.125).astype(BF16)
    weight = weight_ref[:, :, width : 2 * width].reshape(width, width)
    k_ref[...] = dot(normed, weight).astype(BF16)
    kf_ref[...] = dot(far, weight)
    weight = weight_ref[:, :, 2 * width : 3 * width].reshape(width, width)
    v_ref[...] = (dot(normed, weight) + value_bias).astype(BF16)
    vf_ref[...] = dot(far, weight) + value_bias


def attention_kernel(
    q_ref, k_ref, v_ref, kf_ref, vf_ref, averaged_ref, coarse_ref, mask_ref, ones_ref,
    kall_ref, vall_ref, p_ref, att_ref, rden_ref,
    qe_ref,
    *, far_rows, sizes, local_top,
):
    piece, width = q_ref.shape
    levels = len(sizes)
    seq = pl.program_id(0)
    count = kf_ref.shape[0] // sum(far_rows)
    queries = q_ref[...]
    qe_ref[...] = dot(averaged_ref[...], queries).astype(BF16)
    keys = k_ref[...]
    values = v_ref[...]
    coarse_keys = dot(coarse_ref[...], keys).astype(BF16)
    coarse_values = dot(coarse_ref[...], values)
    scaled = [values]
    at = 0
    for level in range(1, local_top):
        scaled.append((coarse_values[at : at + sizes[level]] * 2.0**level).astype(BF16))
        at += sizes[level]
    far_values = pick_far(vf_ref, seq, far_rows, count)
    for level in range(local_top, levels):
        at = 16 * (level - local_top)
        scaled.append((far_values[at : at + 16] * 2.0**level).astype(BF16))
    kall_ref[0] = jnp.concatenate(
        [keys, coarse_keys, pick_far(kf_ref, seq, far_rows, count).astype(BF16)], axis=0
    )
    vall_ref[0] = jnp.concatenate(scaled, axis=0)
    for pair in range(width // 128):
        lanes = slice(pair * 128, pair * 128 + 128)
        plain, one, rest = queries_of(q_ref, qe_ref, pair, levels)
        key_parts = stacked(kall_ref[0, :, lanes], sizes)
        scores = jnp.concatenate(
            [
                dot_right(plain, jnp.concatenate(key_parts[0:2], axis=0)),
                dot_right(one, jnp.concatenate(key_parts[2:4], axis=0)),
                dot_right(rest, blocked(key_parts)),
            ],
            axis=1,
        )
        weights = jnp.where(mask_ref[...] > 0.0, jnp.exp(scores), 0.0).astype(BF16)
        p_ref[0, pair] = weights
        both = jnp.concatenate(
            [jnp.concatenate(stacked(vall_ref[0, :, lanes], sizes), axis=0), ones_ref[...]], axis=1
        )
        sums = dot(weights, both)
        rden = 1.0 / sums[:, 128:]
        rden_ref[:, lanes] = rden
        att_ref[:, lanes] = (sums[:, :128] * rden).astype(BF16)


def feed_kernel(
    vec_ref, table_ref, x_ref, cot_ref, att_ref, part_one, part_two, part_three, part_four,
    out_ref, dmid_ref, datt_ref, sum_ref, first_out, second_out,
    weight_ref,
):
    width = x_ref.shape[1]
    blocks = (weight_ref.shape[2] // width - 1) // 2
    take_groups((part_one, part_two, part_three, part_four), table_ref, weight_ref)
    gain = vec_ref[3:4, :]
    out_weight = weight_ref[:, :, 0:width].reshape(width, width)
    middle = x_ref[...].astype(F32) + dot(att_ref[...], out_weight) + vec_ref[2:3, :]
    unit, inverse = unit_of(middle)
    normed = (unit * gain + vec_ref[4:5, :]).astype(BF16)
    g_out = cot_ref[...]
    result = middle + vec_ref[5:6, :]
    d_two = jnp.zeros(x_ref.shape, F32)
    tiles = width // 128
    per_group = blocks * width // GROUPS // 16
    groups = GROUPS // blocks
    sums = []
    for block in range(blocks):
        up = weight_ref[:, :, width * (block + 1) : width * (block + 2)].reshape(width, width)
        down = jnp.concatenate(
            [
                weight_ref[groups * block + group, :, width * at : width * (at + 1)]
                for group in range(groups)
                for at in range(blocks + 1, blocks + 1 + per_group)
            ],
            axis=0,
        )
        pre = dot(normed, up) + vec_ref[8 + block : 9 + block, :]
        cdf = 0.5 + 0.5 * lax.erf(pre * 0.7071067811865476)
        hidden = (pre * cdf).astype(BF16)
        slope = cdf + pre * (0.3989422804014327 * jnp.exp(-0.5 * pre * pre))
        result = result + dot(hidden, down)
        grad = dot_left(hidden, g_out).reshape(groups, per_group, 16, width)
        for part in range(per_group):
            give_lanes(
                grad[:, part].reshape(-1, width), first_out, second_out, table_ref,
                tiles * (blocks + 1 + part), groups // 2 * block,
            )
        g_pre = (dot_right(g_out, down) * slope).astype(BF16)
        sums.append(column_sum(g_pre.astype(F32)))
        grad = dot_left(normed, g_pre)
        give_lanes(grad, first_out, second_out, table_ref, tiles * (block + 1))
        d_two = d_two + dot_right(g_pre, up)
    out_ref[...] = result.astype(BF16)
    cot = g_out.astype(F32)
    d_middle = cot + norm_back(d_two, unit, inverse, gain)
    dmid_ref[...] = d_middle
    branch = d_middle.astype(BF16)
    datt_ref[...] = dot_right(branch, out_weight)
    give_lanes(dot_left(att_ref[...], branch), first_out, second_out, table_ref, 0)
    sum_ref[...] = jnp.concatenate(
        [
            jnp.zeros((2, width), F32),
            column_sum(branch.astype(F32)),
            column_sum(d_two * unit),
            column_sum(d_two),
            column_sum(cot),
            jnp.zeros((2, width), F32),
        ]
        + sums
        + [jnp.zeros((8 - blocks, width), F32)],
        axis=0,
    )


def attention_back_kernel(
    q_ref, kall_ref, vall_ref, p_ref, att_ref, rden_ref, datt_ref, averaged_ref, wide_ref,
    coarse_t_ref, ones_ref,
    dq_ref, dk_ref, dv_ref, dkf_ref, dvf_ref,
    qe_ref, dkall_ref, dvall_ref, t_ref, dqacc_ref,
    *, sizes, local_top,
):
    piece, width = q_ref.shape
    levels = len(sizes)
    starts = np.concatenate([[0], np.cumsum(sizes)]).tolist()
    local = starts[local_top]

    qe_ref[...] = dot(averaged_ref[...], q_ref[...]).astype(BF16)
    near = 2 * sizes[0]
    mid = near + 2 * sizes[1]
    for pair in range(width // 128):
        lanes = slice(pair * 128, pair * 128 + 128)
        plain, one, rest = queries_of(q_ref, qe_ref, pair, levels)
        key_parts = stacked(kall_ref[0, :, lanes], sizes)
        both = jnp.concatenate(
            [jnp.concatenate(stacked(vall_ref[0, :, lanes], sizes), axis=0), ones_ref[...]], axis=1
        )
        d_num = datt_ref[:, lanes] * rden_ref[:, lanes]
        d_den = -d_num * att_ref[:, lanes].astype(F32)
        d_num = d_num.astype(BF16)
        weights = p_ref[0, pair]
        d_weights = dot_right(jnp.concatenate([d_num, d_den.astype(BF16)], axis=1), both)
        d_scores = (weights.astype(F32) * d_weights).astype(BF16)
        d_key_near = dot_left(d_scores[:, :near], plain)
        d_key_mid = dot_left(d_scores[:, near:mid], one)
        d_key_rest = dot_left(d_scores[:, mid:], rest)
        d_value = dot_left(weights, d_num)
        dqacc_ref[:, lanes] = dot(d_scores[:, :near], jnp.concatenate(key_parts[0:2], axis=0))
        t_ref[0:piece, lanes] = dot(
            d_scores[:, near:mid], jnp.concatenate(key_parts[2:4], axis=0)
        ).astype(BF16)
        d_rest = dot(d_scores[:, mid:], blocked(key_parts)).astype(BF16)
        at = 0
        for level in range(levels):
            size = sizes[level]
            low, high = starts[level], starts[level + 1]
            in_a = lane_a(size)
            if level == 0:
                source = d_key_near
            elif level == 1:
                source = d_key_mid
            else:
                block = slice((level - 2) * 128, (level - 1) * 128)
                source = d_key_rest[at - mid : at - mid + 2 * size, block]
                t_ref[(level - 1) * piece : level * piece, lanes] = d_rest[:, block]
            dkall_ref[low:high, lanes] = jnp.where(in_a, source[:size], source[size:])
            values = d_value[at : at + 2 * size]
            dvall_ref[low:high, lanes] = jnp.where(in_a, values[:size], values[size:]) * 2.0**level
            at += 2 * size
    dq_ref[...] = ((dqacc_ref[...] + dot(wide_ref[...], t_ref[...])) * 0.125).astype(BF16)
    for target, source in ((dk_ref, dkall_ref), (dv_ref, dvall_ref)):
        spread = dot(coarse_t_ref[...], source[piece:local, :].astype(BF16))
        target[...] = (source[0:piece, :] + spread).astype(BF16)
    dkf_ref[0] = dkall_ref[local:, :]
    dvf_ref[0] = dvall_ref[local:, :]


def mix_back_kernel(*refs, far_rows):
    fars = len(far_rows)
    x_ref, vec_ref, sum_ref = refs[:3]
    parts = refs[3:7]
    groups_ref = refs[7]
    grad_refs = [refs[8 + 2 * i : 10 + 2 * i] for i in range(5)]
    far_refs = refs[18 : 18 + fars]
    scaled_ref, first_ref, second_ref = refs[18 + fars : 21 + fars]
    dfar_refs = refs[21 + fars : 21 + 2 * fars]
    weight_ref = refs[-1]
    width = x_ref.shape[1]
    grads = [jnp.concatenate([ref[...] for ref in pair], axis=0) for pair in grad_refs[:3]]

    def by_ref(pair):
        rows = []
        at = 0
        for n in far_rows:
            for ref in pair:
                rows += [ref[seq, at : at + n, :] for seq in range(ref.shape[0])]
            at += n
        return jnp.concatenate(rows, axis=0)

    take_groups(parts, groups_ref, weight_ref, MIX_TABLE)
    gain = vec_ref[0:1, :]
    shift = vec_ref[1:2, :]
    unit, _ = unit_of(x_ref[...].astype(F32))
    normed = (unit * gain + shift).astype(BF16)
    far = far_rows_of(far_refs)
    far_normed = (far * gain + shift).astype(BF16)
    both = jnp.concatenate([normed, far_normed], axis=0)
    far_values = by_ref(grad_refs[4])
    far_grads = (None, by_ref(grad_refs[3]).astype(BF16), far_values.astype(BF16))
    d_one = jnp.zeros(x_ref.shape, F32)
    d_far = jnp.zeros(far.shape, F32)
    for part in range(3):
        lanes = slice(part * width, part * width + width)
        weight = weight_ref[:, :, lanes].reshape(width, width)
        d_one = d_one + dot_right(grads[part], weight)
        if part == 0:
            grad = dot_left(normed, grads[part])
        else:
            d_far = d_far + dot_right(far_grads[part], weight)
            grad = dot_left(both, jnp.concatenate([grads[part], far_grads[part]], axis=0))
        at = part * width // 128
        give_lanes(grad, first_ref, second_ref, groups_ref, at, table=MIX_BACK_TABLE)
    scaled_ref[...] = d_one * gain
    at = 0
    for ref in dfar_refs:
        ref[...] = (d_far[at : at + ref.shape[0]] * gain).astype(BF16)
        at += ref.shape[0]
    vectors = jnp.concatenate(
        [
            column_sum(d_one * unit) + column_sum(d_far * far),
            column_sum(d_one) + column_sum(d_far),
            sum_ref[2:6, :],
            column_sum(grads[0].astype(F32)),
            column_sum(grads[2].astype(F32)) + column_sum(far_values),
            sum_ref[8:16, :],
        ],
        axis=0,
    )
    chunk = width // GROUPS
    small = shrink_vectors(vectors, ((chunk, 0, 6), (2 * chunk, 6, 8), (4 * chunk, 8, 12)))
    at = 3 * width // 128
    give_lanes(small, first_ref, second_ref, groups_ref, at, table=MIX_BACK_TABLE)


def input_kernel(
    x_ref, dmid_ref, scaled_ref, own_ref, one_ref, two_ref, three_ref, pair_ref, spread_ref,
    din_ref,
):
    unit, inverse = unit_of(x_ref[...].astype(F32))
    lower = own_ref[...] + two_ref[...].astype(F32) + three_ref[...].astype(F32)
    base = one_ref[...].astype(F32) + dot(pair_ref[...], lower.astype(BF16))
    scaled = scaled_ref[...] + dot(spread_ref[...], base.astype(BF16))
    inner = (
        scaled
        - jnp.mean(scaled, axis=-1, keepdims=True)
        - unit * jnp.mean(scaled * unit, axis=-1, keepdims=True)
    )
    din_ref[...] = dmid_ref[...] + inner * inverse


def last_kernel(
    mix_one, mix_two, mix_three, mix_four, feed_ref, other_feed_ref,
    matrix_ref, out_ref, up_ref, down_ref, *vector_refs,
):
    total = feed_ref[0].astype(F32) + other_feed_ref[0].astype(F32)
    at = 0
    for ref in (out_ref, up_ref):
        for lane in range(0, ref.shape[1], 128):
            ref[:, lane : lane + 128] = total[at]
            at += 1
    for row in range(0, down_ref.shape[0], 16):
        for lane in range(0, down_ref.shape[1], 128):
            down_ref[row : row + 16, lane : lane + 128] = total[at]
            at += 1
    total = mix_one[0].astype(F32) + mix_two[0].astype(F32)
    total += mix_three[0].astype(F32) + mix_four[0].astype(F32)
    for lane in range(0, matrix_ref.shape[1], 128):
        matrix_ref[:, lane : lane + 128] = total[lane // 128]
    small = total[matrix_ref.shape[1] // 128]
    for i in range(6):
        vector_refs[i][...] = small[i : i + 1, : vector_refs[i].shape[1]]
    vector_refs[6][...] = column_sum(small[6:8])[:, : vector_refs[6].shape[1]]
    vector_refs[7][...] = column_sum(small[8:12])[:, : vector_refs[7].shape[1]]


def vmem():
    return pl.BlockSpec(memory_space=pltpu.VMEM)


def anywhere():
    return pl.BlockSpec(memory_space=pl.ANY)


def scalars():
    return pl.BlockSpec(memory_space=pltpu.SMEM)


def fixed(*dims):
    return pl.BlockSpec(dims, lambda i: (0,) * len(dims))


def moving(*dims):
    return pl.BlockSpec(dims, lambda i: (i,) + (0,) * (len(dims) - 1))


def shape(dims, dtype):
    return jax.ShapeDtypeStruct(dims, dtype)


def const(values):
    return jnp.asarray(values, BF16)


def bit_orders():
    return ((8, 4, 16, 2), (2, 8, 4, 16))


def mix_orders():
    return ((8, 4, 16, 2), (8, 4, 16, 2))


def mix_back_orders():
    return ((8, 4, 16, 2), (8, 4, 2, 16))


def slot_offset(slot, order):
    return sum(bit for k, bit in enumerate(order) if slot >> k & 1)


def group_table(orders):
    table = np.zeros((32, 128), np.int32)
    for device in range(32):
        core = device & 1
        table[device, GROUPS] = core
        for slot in range(16):
            table[device, (device ^ slot_offset(slot, orders[core])) // 2] = slot
            group = device ^ 1 ^ slot_offset(slot, orders[1 - core])
            table[device, GROUPS // 2 + group // 2] = slot
    return table


def exchange(value, bits):
    if isinstance(bits, int):
        bits = (bits, bits)
    count = lax.axis_size(AXES)
    return lax.ppermute(value, AXES, [(i, i ^ bits[i & 1]) for i in range(count)])


def after(value, *others):
    return lax.optimization_barrier((value,) + others)[0]


def added(*parts):
    total = parts[0].astype(F32)
    for part in parts[1:]:
        total = total + part.astype(F32)
    return total.astype(BF16)


def send(buffer, k, orders=None):
    orders = orders or bit_orders()
    return exchange(buffer, (orders[0][k], orders[1][k]))


def halves(kept, other):
    half = kept.shape[0] // 2
    return added(kept[:half], other[:half]), added(kept[half:], other[half:])


def joined(buffer, other):
    return jnp.concatenate([buffer, other], axis=0)


def call(kernel, name, outs, ins, args, work, scratch=(), grid=None, room=6):
    return pl.pallas_call(
        kernel,
        out_shape=tuple(item[0] for item in outs),
        in_specs=list(ins),
        out_specs=tuple(item[1] for item in outs),
        scratch_shapes=list(scratch),
        compiler_params=pltpu.CompilerParams(vmem_limit_bytes=room * MIB),
        cost_estimate=pl.CostEstimate(flops=work, bytes_accessed=work >> 9, transcendentals=0),
        name=name,
        **({} if grid is None else {"grid": grid}),
    )(*args)


def coarsen(values):
    return (values[:, 0::2] + values[:, 1::2]) * 0.5


def whole_far(base, seqs, far_levels, position):
    rows = base.reshape(seqs, 16, base.shape[1])
    full = lax.all_gather(rows, "seq", axis=1, tiled=True).astype(F32)
    parts = []
    for extra in range(far_levels):
        partner = (position // 2**extra) ^ 1
        parts.append(lax.dynamic_slice_in_dim(full, partner * 16, 16, axis=1))
        if extra + 1 < far_levels:
            full = coarsen(full)
    return jnp.concatenate(parts, axis=1).astype(BF16).reshape(seqs * 16 * far_levels, -1)


def whole_far_back(grad, seqs, far_levels, position):
    stack = grad.reshape(seqs, far_levels, 16, -1).astype(F32)
    ids = jnp.arange(far_levels).reshape(1, far_levels, 1, 1)
    count = lax.axis_size("seq")
    for bit in range(far_levels):
        pairs = [(i, i ^ 1 << bit) for i in range(count)]
        other = lax.ppermute(stack.astype(BF16), "seq", pairs).astype(F32)
        stack = jnp.where(ids > bit, stack + other, jnp.where(ids == bit, other, stack))
    own = jnp.zeros((seqs, 16, stack.shape[-1]), F32)
    for extra in range(far_levels):
        rows = 16 >> extra
        offset = position % 2**extra * rows
        part = lax.dynamic_slice_in_dim(stack[:, extra], offset, rows, axis=1)
        own = own + jnp.repeat(part, 2**extra, axis=1) * 0.5**extra
    return own.reshape(seqs * 16, -1).astype(BF16)


def body(
    layer_input, qkv_weight, qv_bias, out_weight, out_bias, first_gain, first_shift, second_gain,
    second_shift, up_weight, up_bias, down_weight, down_bias, cotangent,
):
    batches, per_batch, piece, width = layer_input.shape
    seqs = batches * per_batch
    tokens = seqs * piece
    hidden = up_weight.shape[1]
    blocks = hidden // width
    devices = lax.axis_size(AXES)
    pieces = lax.axis_size("seq")
    position = lax.axis_index("seq")
    far_levels = pieces.bit_length() - 1
    local_top = (piece // 16).bit_length() - 1
    fast = devices == GROUPS and pieces == 16
    x = layer_input.reshape(tokens, width)
    cot = cotangent.reshape(tokens, width)
    sizes = level_sizes(piece, far_levels, local_top)
    keys = sum(sizes)
    flat = (tokens, width)
    base_rows = seqs * 16
    coarse_all = np.kron(np.eye(seqs, dtype=np.float32), average(piece, piece // 16))
    pair = np.kron(np.eye(seqs, dtype=np.float32), pair_average(16))
    gather_far = far_constants(seqs)
    vectors = (
        first_gain, first_shift, out_bias, second_gain, second_shift, down_bias, qv_bias, up_bias,
    )

    if fast:
        me = lax.axis_index(AXES)
        orders = (bit_orders(), mix_orders(), mix_back_orders())
        table = np.concatenate([group_table(item) for item in orders], axis=1)
        groups = lax.dynamic_slice_in_dim(jnp.asarray(table), me, 1, axis=0)
    if fast:
        (pack_b,) = call(
            pack_kernel,
            "pack",
            [(shape((16, width + 2 * hidden), BF16), vmem())],
            [vmem()] * 3,
            (out_weight, up_weight, down_weight),
            1 << 16,
            room=60,
        )
    base, below = call(
        norm_kernel,
        "norm",
        [(shape((base_rows, width), BF16), vmem()), (shape((base_rows // 2, width), BF16), vmem())],
        [vmem()],
        (after(x, groups, pack_b) if fast else x,),
        1 << 20,
    )
    coarse_rows = sum(sizes[1:local_top])
    top = len(sizes) - 1
    made = (
        ((top * piece, piece), BF16),
        ((piece, top * piece), BF16),
        ((coarse_rows, piece), BF16),
        ((piece, coarse_rows), BF16),
        ((piece, 2 * keys), F32),
        ((2 * keys, 128), BF16),
    )
    averaged, averaged_wide, coarse, coarse_t, mask, ones = call(
        partial(made_kernel, sizes=sizes, local_top=local_top),
        "made",
        [(shape(*item), vmem()) for item in made],
        [],
        (),
        1 << 20,
    )

    if fast:
        a = jnp.pad(qkv_weight, ((0, 0), (0, 128)))
        for row, vector in enumerate(vectors):
            item = vector.reshape(1, -1)
            lanes = (3 * width, 128 - item.shape[1])
            a = a + jnp.pad(item, ((row, SMALL - 1 - row), lanes))
        a = a[None]
        b = pack_b[None]
        other_a = send(a, 0, mix_orders())
        other_b = send(b, 0)
        a = joined(a, other_a)
        other_a = send(after(a, base), 1, mix_orders())
        a = joined(a, other_a)
        other_a = send(a, 2, mix_orders())
        b = joined(after(b, a), other_b)
        other_b = send(b, 1)
        near, half = after(base, a), after(below, a)
        one, two, three = exchange(near, 1), exchange(half, 2), exchange(half, 3)
        a = joined(a, other_a)
        other_a = send(a, 3, mix_orders())
        five, six = call(
            far_kernel,
            "far",
            [
                (shape((base_rows, width), BF16), vmem()),
                (shape((base_rows // 2, width), BF16), vmem()),
            ],
            [vmem()] * 6,
            (after(below, a, mask), one, two, three, const(gather_far), const(pair)),
            1 << 20,
        )
        far = (one, two, three, exchange(five, 4), exchange(six, 8), exchange(six, 12))
        far_rows = (16, 8, 8, 16, 8, 8)
        b = joined(after(b, a), other_b)
        other_b = send(b, 2)
        lower = exchange(a, 1)
        other_a = after(other_a, five, six)
        parts_a = (a, other_a, lower, exchange(other_a, 1))
        b = joined(after(b, other_a, *far), other_b)
        other_b = send(b, 3)
        lower = exchange(after(b, other_a), 1)
    else:
        groups = [slot % (GROUPS // 2) for slot in range(GROUPS)] + [0] * (128 - GROUPS)
        groups = jnp.asarray([groups * 3], jnp.int32)

        def whole(value):
            return lax.all_gather(value, AXES, axis=0, tiled=True).reshape(
                (GROUPS, -1) + value.shape[1:]
            )

        small = [jnp.pad(v, ((0, 0), (0, 128 - v.shape[1]))) for v in map(whole, vectors)]
        small += [jnp.zeros((GROUPS, 128), BF16)] * (SMALL - len(small))
        gathered_a = jnp.concatenate([whole(qkv_weight), jnp.stack(small, axis=1)], axis=2)
        downs = whole(down_weight).reshape(GROUPS, -1, 16, width).transpose(0, 2, 1, 3)
        parts = [whole(out_weight), whole(up_weight), downs.reshape(GROUPS, 16, -1)]
        gathered_b = jnp.concatenate(parts, axis=2)

        def quarters(item):
            return item[0:16:2], item[16::2], item[1:16:2], item[17::2]

        parts_a, parts_b = quarters(gathered_a), quarters(gathered_b)
        far = (whole_far(base, seqs, far_levels, position),)
        far_rows = (16 * far_levels,)

    lanes_a = 3 * width + 128
    tiles_a = lanes_a // 128
    tiles_b = (width + 2 * hidden) // 128
    top = len(sizes) - 1
    pairs = width // 128
    total_far = seqs * 16 * far_levels
    half_a = shape((GROUPS // 2, tiles_a, 16, 128), BF16)
    half_b = shape((GROUPS // 2, tiles_b, 16, 128), BF16)
    far_flat = shape((total_far, width), F32)
    low, high = shape(flat, BF16), shape(flat, F32)
    sixteen = shape((16, width), F32)
    level = dict(far_rows=far_rows, sizes=sizes, local_top=local_top)

    vec, queries, key, value, far_key, far_value = call(
        mix_kernel,
        "mix",
        [(sixteen, vmem())] + [(low, vmem())] * 3 + [(far_flat, vmem())] * 2,
        [vmem()] * 5 + [scalars()] + [vmem()] * len(far),
        (x, *parts_a, groups, *far),
        1 << 24,
        [pltpu.VMEM((GROUPS, 16, lanes_a), BF16)],
        room=14,
    )
    rows_spec = moving(piece, width)
    keys_spec = moving(1, keys, width)
    p_spec = moving(1, pairs, piece, 2 * keys)
    keys_shape = shape((seqs, keys, width), BF16)
    kall, vall, weights, attended, rden = call(
        partial(attention_kernel, **level),
        "attention",
        [
            (keys_shape, keys_spec),
            (keys_shape, keys_spec),
            (shape((seqs, pairs, piece, 2 * keys), BF16), p_spec),
            (low, rows_spec),
            (high, rows_spec),
        ],
        [rows_spec] * 3
        + [fixed(total_far, width)] * 2
        + [
            fixed(top * piece, piece),
            fixed(coarse_rows, piece),
            fixed(piece, 2 * keys),
            fixed(2 * keys, 128),
        ],
        (
            queries, key, value, far_key, far_value, averaged, coarse, mask, ones,
        ),
        1 << 24,
        [pltpu.VMEM((top * piece, width), BF16)],
        (seqs,),
        room=12,
    )
    if fast:
        other_b = after(other_b, attended)
        parts_b = (b, other_b, lower, exchange(other_b, 1))

    result, d_middle, d_attended, sums, kept_b, sent_b = call(
        feed_kernel,
        "feed",
        [(low, vmem()), (high, vmem()), (high, vmem()), (sixteen, vmem())] + [(half_b, vmem())] * 2,
        [vmem(), scalars()] + [vmem()] * 7,
        (vec, groups, x, cot, attended, *parts_b),
        8 << 30,
        [
            pltpu.VMEM((GROUPS, 16, width + 2 * hidden), BF16),
        ],
        room=30,
    )
    def back_call(seq, count, d_attended):
        def later(*dims):
            return pl.BlockSpec(dims, lambda i: (i + seq,) + (0,) * (len(dims) - 1))

        rows, wide_keys = later(piece, width), later(1, keys, width)
        half = (shape((count * piece, width), BF16), rows_spec)
        far_half = shape((count, keys - local, width), F32), moving(1, keys - local, width)
        return call(
            partial(attention_back_kernel, sizes=sizes, local_top=local_top),
            "attention_back",
            [half] * 3 + [far_half] * 2,
            [rows, wide_keys, wide_keys, later(1, pairs, piece, 2 * keys), rows, rows, rows]
            + [
                fixed(top * piece, piece),
                fixed(piece, top * piece),
                fixed(piece, coarse_rows),
                fixed(2 * keys, 128),
            ],
            (
                queries, kall, vall, weights, attended, rden, d_attended, averaged, averaged_wide,
                coarse_t, ones,
            ),
            6 << 30,
            [
                pltpu.VMEM((top * piece, width), BF16),
                pltpu.VMEM((keys, width), F32),
                pltpu.VMEM((keys, width), F32),
                pltpu.VMEM((top * piece, width), BF16),
                pltpu.VMEM((piece, width), F32),
            ],
            (count,),
            room=16,
        )

    local = sum(sizes[:local_top])
    if fast:
        late = exchange(sent_b[12:], 1)
        rest = exchange(after(sent_b, late)[:12], 1)
        upper_b = added(kept_b[12:], late)
        late_b = send(upper_b, 3)
        d_attended = after(d_attended, upper_b)
    most = max(1, seqs // 2)
    back_one = back_call(0, most, d_attended)
    if fast:
        rest, *back_one = lax.optimization_barrier((rest, *back_one))
        upper_b = added(kept_b[8:12], rest[8:])
        early_b = send(upper_b, 3)
        d_attended = after(d_attended, upper_b)
    back_two = back_call(most, seqs - most, d_attended)
    outs = call(
        partial(mix_back_kernel, far_rows=far_rows),
        "mix_back",
        [(high, vmem())]
        + [(half_a, vmem())] * 2
        + [(shape(item.shape, BF16), vmem()) for item in far],
        [vmem()] * 7 + [scalars()] + [vmem()] * (10 + len(far)),
        (
            x, vec, sums, *parts_a, groups,
            *[item for pair in zip(back_one, back_two) for item in pair], *far,
        ),
        2 << 30,
        [pltpu.VMEM((GROUPS, 16, lanes_a), BF16)],
        room=24,
    )
    scaled, kept_a, sent_a = outs[:3]
    d_far = outs[3:]

    if fast:
        upper_b = added(after(kept_b[4:8], scaled, early_b), rest[4:8], late_b)
        middle_b = send(upper_b, 2)
        other_a = exchange(after(sent_a, upper_b), 1)
        kept_a, upper_a = halves(kept_a, other_a)
        other_a = send(upper_a, 3, mix_back_orders())
        back = [after(item, upper_a) for item in d_far[3:]]
        back = [exchange(item, bits) for item, bits in zip(back, (4, 8, 12))]
        kept_b = added(after(kept_b, upper_a, *back)[:4], rest[:4], early_b, middle_b)
        kept_b, upper_b = kept_b[:2], kept_b[2:]
        other_b = send(upper_b, 1)
        kept_a, upper_a = halves(after(kept_a, upper_b), other_a)
        other_a = send(upper_a, 2, mix_back_orders())
        back = [after(item, upper_b) for item in back]
        own, out_one, out_two, out_three = call(
            far_back_kernel,
            "far_back",
            [
                (shape((base_rows // 2, width), F32), vmem()),
                (shape((base_rows, width), BF16), vmem()),
                (shape((base_rows // 2, width), BF16), vmem()),
                (shape((base_rows // 2, width), BF16), vmem()),
            ],
            [vmem()] * 8,
            (*back, d_far[0], d_far[1], d_far[2], const(gather_far.T), const(pair.T)),
            1 << 20,
        )
        far_one = exchange(out_one, 1)
        far_two = exchange(out_two, 2)
        far_three = exchange(out_three, 3)
        own_a, far_a = halves(after(kept_a, own, other_b), other_a)
        one_a, two_a = own_a[0:1], own_a[1:2]
        lasts_a = (
            one_a,
            exchange(two_a, 8),
            exchange(far_a[0:1], 4),
            exchange(far_a[1:2], 12),
        )
        kept_b, upper_b = halves(after(kept_b, own_a), other_b)
        other_b = send(upper_b, 0)
    else:
        far_one = whole_far_back(d_far[0], seqs, far_levels, position)
        own = jnp.zeros((base_rows // 2, width), F32)
        far_two = far_three = jnp.zeros((base_rows // 2, width), BF16)

    (d_input,) = call(
        input_kernel,
        "input_grad",
        [(high, vmem())],
        [vmem()] * 9,
        (
            x, d_middle, scaled, own, far_one, far_two, far_three, const(pair.T),
            const(coarse_all.T),
        ),
        1 << 20,
    )

    if fast:
        grad_qkv, grad_out_weight, grad_up, grad_down, *plain = call(
            last_kernel,
            "last",
            [
                (shape(item.shape, F32), vmem())
                for item in (qkv_weight, out_weight, up_weight, down_weight)
            ]
            + [(shape((1, v.shape[0]), F32), vmem()) for v in vectors],
            [vmem()] * 6,
            (*lasts_a, kept_b, other_b),
            1 << 16,
        )
        plain = [item.reshape(-1) for item in plain]
        grad_qv, grad_up_bias = plain[6:8]
    else:

        def reduced(item):
            return lax.psum_scatter(item.astype(F32), AXES, scatter_dimension=0, tiled=True)

        def rows_of(item):
            return reduced(item.transpose(0, 2, 1, 3).reshape(GROUPS * 16, -1))

        all_a = jnp.stack([kept_a, sent_a], axis=1).reshape(GROUPS, *half_a.shape[1:])
        all_b = jnp.stack([kept_b, sent_b], axis=1).reshape(GROUPS, *half_b.shape[1:])
        grad_qkv = rows_of(all_a[:, :-1])
        small = all_a[:, -1]
        chunk = width // GROUPS
        plain = [reduced(small[:, i, :chunk].reshape(-1)) for i in range(6)]
        grad_qv = reduced(jnp.sum(small[:, 6:8, : 2 * chunk], axis=1).reshape(-1))
        grad_up_bias = reduced(jnp.sum(small[:, 8:12, : 4 * chunk], axis=1).reshape(-1))
        split = width // 128
        grad_out_weight = rows_of(all_b[:, :split])
        grad_up = rows_of(all_b[:, split : split * (blocks + 1)])
        downs = all_b[:, split * (blocks + 1) :].reshape(GROUPS, -1, split, 16, 128)
        grad_down = reduced(downs.transpose(0, 1, 3, 2, 4).reshape(hidden, width))

    return (
        result.reshape(layer_input.shape),
        d_input.reshape(layer_input.shape),
        grad_qkv,
        grad_qv,
        grad_out_weight,
        plain[2],
        plain[0],
        plain[1],
        plain[3],
        plain[4],
        grad_up,
        grad_up_bias,
        grad_down,
        plain[5],
    )


def solution(mesh):
    tokens = P(None, "dp", "seq", None)
    matrix = P(AXES, None)
    vector = P(AXES)
    in_specs = (
        tokens, matrix, vector, matrix, vector, vector, vector, vector, vector, matrix, vector,
        matrix, vector, tokens,
    )
    out_specs = (
        tokens, tokens, matrix, vector, matrix, vector, vector, vector, vector, vector, matrix,
        vector, matrix, vector,
    )
    return jax.shard_map(body, mesh=mesh, in_specs=in_specs, out_specs=out_specs, check_vma=False)
```
